32 devices in a mesh: tm: 8 (over y, x, core), rows: 4 (over z).
Axes of the slice: x: 2, y: 2, z: 4, core: 2. Of those that a mesh axis runs over, the one named last changes fastest.
Arguments:
- starts: float32 [8, 2, 32, 8192], P('tm', None, 'rows'), may hold values from -6 to 6
- conductivity: float32 [32, 8192], P('rows'), may hold values from 0.03 to 0.12
Outputs:
- new_ends: float32 [8, 2, 32, 8192], P('tm', None, 'rows')
- coarse_next: float32 [8, 2, 4, 1024], P('tm')
The draws below stay inside these ranges and needn't reach their ends.
All inputs are finite; a program needn't handle non-finite values.
Results may differ from the reference program's by a relative error of at most 0.0001.
Values sent between devices are 32-bit elements; how exact they have to be, the bound alone decides.
A program may use at most 64 MiB of HBM per device.

```python
import math
import jax
import jax.numpy as jnp
from jax import lax

NY = 8192
FINE = 8
COARSE = 2
COARSEN = 8
SLICES = 8
NX = 32


def shard_levels(own_key, extent, cuts, least, largest):
    def one(dim, shards_of):
        draws = jax.random.uniform(jax.random.fold_in(jax.random.fold_in(own_key, 6), dim), (shards_of,), jnp.float32, least / len(cuts), largest / len(cuts))
        return jnp.repeat(jnp.exp(draws), extent[dim] // shards_of).reshape((-1,) + (1,) * (len(extent) - dim - 1))

    factor_of = one(*cuts[0])
    for cut in cuts[1:]:
        factor_of = factor_of * one(*cut)
    return factor_of


def scatter_about(key, dims, deviation, limit, pieces=(), kind=jnp.bfloat16):
    values = jax.random.normal(key, dims, jnp.float32) * deviation
    if len(pieces) > 0:
        values = shard_levels(key, dims, pieces, -0.22, 0.18) * values
    return jnp.clip(values, min=-limit, max=limit).astype(kind)


def setup_inputs(seed: int = 0) -> dict:
    arg_keys = jax.random.split(jax.random.key(seed), 3)
    return {
        "starts": scatter_about(arg_keys[0], (SLICES, 2, NX, NY), 1.0, 6.0, ((0, 8), (2, 4)), jnp.float32),
        "conductivity": jnp.clip(jnp.exp(math.log(0.12) - 1.3862944 * jax.random.uniform(arg_keys[1], (NX, NY), jnp.float32) ** shard_levels(arg_keys[1], (NX, NY), ((0, 4),), -0.2, 0.2)), 0.03, 0.12),
    }


EXCHANGE = 0.05
TRACER_DIFF = 0.5


def advance(extended, kappa_ext, step_len, spacing_sq):
    centre = extended[:, 1:-1]
    kappa_mid = kappa_ext[1:-1]
    upper = 0.5 * (kappa_mid + kappa_ext[2:])
    lower = 0.5 * (kappa_mid + kappa_ext[:-2])
    right_face = 0.5 * (kappa_mid + jnp.roll(kappa_mid, -1, 1))
    left_face = 0.5 * (kappa_mid + jnp.roll(kappa_mid, 1, 1))
    spread = (upper * (extended[:, 2:] - centre) + lower * (extended[:, :-2] - centre)
              + right_face * (jnp.roll(centre, -1, 2) - centre)
              + left_face * (jnp.roll(centre, 1, 2) - centre)) / spacing_sq
    transfer = EXCHANGE * (centre[1] - centre[0])
    heat = centre[0] + step_len * (spread[0] + transfer)
    tracer = centre[1] + step_len * (TRACER_DIFF * spread[1] - transfer)
    return jnp.stack([heat, tracer])


def pad_fields(values):
    return jnp.pad(values, ((0, 0), (1, 1), (0, 0)))


def pad_kappa(values):
    return jnp.pad(values, ((1, 1), (0, 0)))


def restrict(values):
    lead = values.shape[:-2]
    nrow = values.shape[-2]
    ncol = values.shape[-1]
    blocks = values.reshape(lead + (nrow // COARSEN, COARSEN, ncol // COARSEN, COARSEN))
    return jnp.mean(blocks, axis=(-3, -1))


def prolong(values):
    return jnp.repeat(jnp.repeat(values, COARSEN, -2), COARSEN, -1)


def coarse_prop(coarse, kappa_coarse):
    kappa_ext = pad_kappa(kappa_coarse)
    for substep in range(COARSE):
        coarse = advance(pad_fields(coarse), kappa_ext, FINE / COARSE, float(COARSEN * COARSEN))
    return coarse


def fine_prop(fields, conductivity):
    kappa_ext = pad_kappa(conductivity)
    for substep in range(FINE):
        fields = advance(pad_fields(fields), kappa_ext, 1.0, 1.0)
    return fields


def reference(starts, conductivity):
    kappa_coarse = restrict(conductivity)

    def per_slice(start):
        fine_end = fine_prop(start, conductivity)
        old = coarse_prop(restrict(start), kappa_coarse)
        return fine_end - prolong(old)

    defects = lax.map(per_slice, starts)
    coarse_defects = restrict(defects)

    def link(coarse, defect):
        advanced = coarse_prop(coarse, kappa_coarse)
        following = advanced + defect
        return following, (advanced, following)

    last, outputs = lax.scan(link, restrict(starts[0]), coarse_defects)
    advanced_all, following_all = outputs
    return prolong(advanced_all) + defects, following_all
```

```python
import functools
import math

import jax
import jax.numpy as jnp
from jax import lax
from jax.experimental import pallas as pl
from jax.experimental.pallas import tpu as pltpu
from jax.sharding import PartitionSpec as P

FINE = 8
COARSE = 2
COARSEN = 8
EXCHANGE = 0.05
TRACER_DIFF = 0.5

SUB = 8
LANES = 128
MESH = pl.DeviceIdType.MESH
SHARE = 4


def roll_left(v):
    width = v.shape[1]
    r = pltpu.roll(v, width - 1, 1)
    last = r[:, width - LANES:]
    lane = lax.broadcasted_iota(jnp.int32, last.shape, 1)
    last = jnp.where(lane == LANES - 1, pltpu.roll(last, SUB - 1, 0), last)
    if width == LANES:
        return last
    return jnp.concatenate([r[:, : width - LANES], last], axis=1)


def roll_right(v):
    width = v.shape[1]
    r = pltpu.roll(v, 1, 1)
    first = r[:, :LANES]
    lane = lax.broadcasted_iota(jnp.int32, first.shape, 1)
    first = jnp.where(lane == 0, pltpu.roll(first, 1, 0), first)
    if width == LANES:
        return first
    return jnp.concatenate([first, r[:, LANES:]], axis=1)


def exact_dot(x, w):
    rows = x.shape[0]
    hi = x.astype(jnp.bfloat16)
    rest = x - hi.astype(jnp.float32)
    mid = rest.astype(jnp.bfloat16)
    low = (rest - mid.astype(jnp.float32)).astype(jnp.bfloat16)
    y = jnp.dot(jnp.concatenate([hi.astype(jnp.float32), mid.astype(jnp.float32), low.astype(jnp.float32)], axis=0).astype(jnp.bfloat16), w,
                preferred_element_type=jnp.float32)
    return y[:rows] + y[rows:2 * rows] + y[2 * rows:]


def neighbours(v, above, below, k_up, k_down, k_left, k_right):
    return (k_right * roll_left(v) + k_left * roll_right(v)) + (k_down * below + k_up * above)


def kernel(nt, nr, group, s_hbm, k_hbm, out_ref, nxt_ref,
           s_ref, k_ref, in_sem, vb, own, kown, kh, kr, kl, kd, ku, ch, ct, pool, kcs, rss, rfs, kc, rsn, rf, jall,
           vsend, vrecv, ksend, krecv, kfwd, kcsend, kcrecv, rssend, rsrecv, rfsend, rfrecv, jsend, jrecv, tok_down, tok_up):
    t = lax.axis_index("tm")
    r = lax.axis_index("rows")
    width = own.shape[-1]
    tiles = width // LANES
    member = lax.rem(t, group)
    base = t - member
    has_up = r > 0
    has_down = r < nr - 1
    has_prev = t > 0
    has_next = t < nt - 1

    k_in = pltpu.make_async_copy(k_hbm, k_ref, in_sem.at[0])
    s_in = pltpu.make_async_copy(s_hbm, s_ref, in_sem.at[1])
    k_in.start()
    s_in.start()

    barrier = pltpu.get_barrier_semaphore()

    def greet(tm, row):
        pl.semaphore_signal(barrier, inc=1, device_id=(tm, row), device_id_type=MESH)

    pl.when(has_up)(lambda: greet(t, r - 1))
    pl.when(has_down)(lambda: greet(t, r + 1))
    for o in range(1, nt):
        greet(lax.rem(t + o, nt), r)

    cell = lax.broadcasted_iota(jnp.int32, pool.shape, 0)
    block = lax.broadcasted_iota(jnp.int32, pool.shape, 1)
    inside = (cell >= block * COARSEN) & (cell < (block + 1) * COARSEN)
    pool[...] = jnp.where(inside, 1.0 / (COARSEN * COARSEN), 0.0).astype(jnp.bfloat16)
    k_in.wait()
    s_in.wait()

    def split_row(ref, row):
        return jnp.concatenate(
            [ref[pl.ds(m * SUB + row, SUB, stride=tiles * SUB), :] for m in range(tiles)], axis=1)

    sums = [None, None, None]
    for row in range(SUB):
        for f in range(2):
            x = split_row(s_ref.at[f], row)
            own[row, f] = x
            vb[0, SUB + row, f] = x
            sums[f] = x if sums[f] is None else sums[f] + x
        x = split_row(k_ref, row)
        kown[row] = x
        sums[2] = x if sums[2] is None else sums[2] + x

    coarse = exact_dot(jnp.concatenate(sums, axis=0), pool[...])
    rss[0] = coarse[:SUB]
    rss[1] = coarse[SUB:2 * SUB]
    kcs[...] = coarse[2 * SUB:]
    kc[r] = coarse[2 * SUB:]

    @pl.when(jnp.logical_not(has_up))
    def _():
        vb[0, 0:SUB] = jnp.zeros((SUB,) + vb.shape[2:], jnp.float32)
        kh[0] = jnp.zeros(kh.shape[1:], jnp.float32)

    @pl.when(jnp.logical_not(has_down))
    def _():
        vb[0, 2 * SUB:] = jnp.zeros((SUB,) + vb.shape[2:], jnp.float32)
        kh[1] = jnp.zeros(kh.shape[1:], jnp.float32)

    pl.semaphore_wait(barrier, (nt - 1) + has_up.astype(jnp.int32) + has_down.astype(jnp.int32))

    def tell(tok, row):
        pl.semaphore_signal(tok, inc=1, device_id=(t, row), device_id_type=MESH)

    pl.when(jnp.logical_not(has_up) & has_down)(lambda: tell(tok_down, r + 1))
    pl.when(jnp.logical_not(has_down) & has_up)(lambda: tell(tok_up, r - 1))

    def v_copy(side, d):
        if side == 0:
            return pltpu.make_async_remote_copy(
                own.at[SUB - d], vb.at[0, SUB - d], vsend.at[side, d - 1], vrecv.at[side, d - 1],
                device_id=(t, r + 1), device_id_type=MESH)
        return pltpu.make_async_remote_copy(
            own.at[d - 1], vb.at[0, 2 * SUB - 1 + d], vsend.at[side, d - 1], vrecv.at[side, d - 1],
            device_id=(t, r - 1), device_id_type=MESH)

    def k_copy(side, d):
        return pltpu.make_async_remote_copy(
            kown.at[SUB - d if side == 0 else d - 1], kh.at[side, d - 1], ksend.at[side, d - 1], krecv.at[side, d - 1],
            device_id=(t, r + 1 if side == 0 else r - 1), device_id_type=MESH)

    def k_forward(side, d, o):
        return pltpu.make_async_remote_copy(
            kh.at[side, d - 1], kh.at[side, d - 1], kfwd.at[side, d - 1, o], krecv.at[side, d - 1],
            device_id=(base + lax.rem(member + o, group), r), device_id_type=MESH)

    def when_mine(d, cond, act):
        pl.when(cond & (member == (d - 1) % group))(act)

    sends = (has_down, has_up)
    gets = (has_up, has_down)
    for d in range(1, FINE + 1):
        for side in range(2):
            when_mine(d, sends[side], lambda: k_copy(side, d).start())
    for side in range(2):
        @pl.when(sends[side])
        def _():
            v_copy(side, 1).start()
    for d in range(2, FINE + 1):
        for side in range(2):
            @pl.when(sends[side])
            def _():
                v_copy(side, d).start()

    def kc_copy(o):
        return pltpu.make_async_remote_copy(
            kcs, kc.at[r], kcsend.at[o], kcrecv.at[o],
            device_id=(t, lax.rem(r + o, nr)), device_id_type=MESH)

    def rs_first():
        return pltpu.make_async_remote_copy(
            rss, rsn.at[r], rssend.at[0], rsrecv.at[0],
            device_id=(t - 1, r), device_id_type=MESH)

    def rs_copy(o):
        return pltpu.make_async_remote_copy(
            rsn.at[r], rsn.at[r], rssend.at[o], rsrecv.at[o],
            device_id=(t, lax.rem(r + o, nr)), device_id_type=MESH)

    pl.when(has_prev)(lambda: rs_first().start())

    @pl.when(has_up)
    def _():
        pl.semaphore_wait(tok_down, 1)
        pl.when(has_down)(lambda: tell(tok_down, r + 1))

    def columns_of(i, k):
        kr[i] = 0.5 * (k + roll_left(k))
        kl[i] = 0.5 * (k + roll_right(k))

    def centre_of(i):
        total = (kr[i] + kl[i]) + (ku[i] + kd[i])
        ch[i] = (1.0 - EXCHANGE) - total
        ct[i] = (1.0 - EXCHANGE) - TRACER_DIFF * total

    for row in range(SUB):
        k = kown[row]
        columns_of(SUB + row, k)
        if row < SUB - 1:
            face = 0.5 * (k + kown[row + 1])
            kd[SUB + row] = face
            ku[SUB + row + 1] = face
        if 0 < row < SUB - 1:
            centre_of(SUB + row)

    @pl.when(has_down)
    def _():
        pl.semaphore_wait(tok_up, 1)
        pl.when(has_up)(lambda: tell(tok_up, r - 1))

    for o in range(1, nr):
        kc_copy(o).start()

    def row_pair(level, diagonal):
        p = lax.rem(level + 1, 2)
        new = []
        for i in (SUB + level - diagonal, 2 * SUB - 1 - level + diagonal):
            faces = ku[i], kd[i], kl[i], kr[i]
            heat, tracer = vb[p, i, 0], vb[p, i, 1]
            around_h = neighbours(heat, vb[p, i - 1, 0], vb[p, i + 1, 0], *faces)
            around_t = neighbours(tracer, vb[p, i - 1, 1], vb[p, i + 1, 1], *faces)
            new.append((i, (ch[i] * heat + EXCHANGE * tracer) + around_h,
                        (ct[i] * tracer + EXCHANGE * heat) + TRACER_DIFF * around_t))
        for i, heat, tracer in new:
            vb[1 - p, i, 0] = heat
            vb[1 - p, i, 1] = tracer

    def run_diagonal(diagonal):
        def step(level, carry):
            row_pair(level, diagonal)
            return carry
        lax.fori_loop(1, min(FINE, SUB // 2 - 1 + diagonal) + 1, step, 0)

    for diagonal in range(2 - SUB // 2, 1):
        run_diagonal(diagonal)

    for d in range(1, FINE + 1):
        for side in range(2):
            def pass_on():
                k_copy(side, d).wait_recv()
                for o in range(1, group):
                    k_forward(side, d, o).start()
            when_mine(d, gets[side], pass_on)

    outside = (jnp.where(has_up, 1.0, 0.0), jnp.where(has_down, 1.0, 0.0))
    for d in range(1, FINE + 1):
        for side in range(2):
            @pl.when(gets[side])
            def _():
                v_copy(side, d).wait_recv()

            pl.when(gets[side] & (member != (d - 1) % group))(lambda: k_copy(side, d).wait_recv())
            k = kh[side, d - 1]
            if d > 1:
                inner = kh[side, d - 2]
            else:
                inner = kown[0 if side == 0 else SUB - 1]
            face = 0.5 * (k + inner)
            edge = face * outside[side] if d == 1 else face
            i = SUB - d if side == 0 else 2 * SUB - 1 + d
            columns_of(i, k)
            if side == 0:
                ku[i + 1] = face
                kd[i] = edge
                centre_of(i + 1)
            else:
                kd[i - 1] = face
                ku[i] = edge
                centre_of(i - 1)
        run_diagonal(d)
        if d == FINE // 2:
            @pl.when(has_next)
            def _():
                rs_first().wait_recv()
                for o in range(1, nr):
                    rs_copy(o).start()

    ends = []
    for f in range(2):
        total = vb[0, SUB, f]
        for row in range(1, SUB):
            total = total + vb[0, SUB + row, f]
        ends.append(total)
    coarse_end = exact_dot(jnp.concatenate(ends, axis=0), pool[...])
    for f in range(2):
        rfs[f] = coarse_end[f * SUB:(f + 1) * SUB]
        rf[r, f] = coarse_end[f * SUB:(f + 1) * SUB]

    def rf_copy(o):
        return pltpu.make_async_remote_copy(
            rfs, rf.at[r], rfsend.at[o], rfrecv.at[o],
            device_id=(t, lax.rem(r + o, nr)), device_id_type=MESH)

    for o in range(1, nr):
        rf_copy(o).start()
    for o in range(1, nr):
        kc_copy(o).wait_recv()

    ratio = (FINE / COARSE) / float(COARSEN * COARSEN)
    kcv = [kc[i] for i in range(nr)]
    c_right = [ratio * 0.5 * (k + roll_left(k)) for k in kcv]
    c_left = [ratio * 0.5 * (k + roll_right(k)) for k in kcv]
    c_face = [ratio * 0.5 * kcv[0]]
    c_face += [ratio * 0.5 * (kcv[i] + kcv[i + 1]) for i in range(nr - 1)]
    c_face += [ratio * 0.5 * kcv[nr - 1]]

    rate = EXCHANGE * (FINE / COARSE)
    totals = [(c_right[i] + c_left[i]) + (c_face[i] + c_face[i + 1]) for i in range(nr)]
    c_centre = [[(1.0 - rate) - x for x in totals], [(1.0 - rate) - TRACER_DIFF * x for x in totals]]

    def coarse_prop(state):
        for substep in range(COARSE):
            new = []
            for f in range(2):
                rows = state[f * nr:(f + 1) * nr]
                other = state[(1 - f) * nr:(2 - f) * nr]
                for i in range(nr):
                    v = rows[i]
                    around = c_right[i] * roll_left(v) + c_left[i] * roll_right(v)
                    rowwise = None
                    if i > 0:
                        rowwise = c_face[i] * rows[i - 1]
                    if i < nr - 1:
                        below = c_face[i + 1] * rows[i + 1]
                        rowwise = below if rowwise is None else rowwise + below
                    if rowwise is not None:
                        around = around + rowwise
                    if f == 1:
                        around = TRACER_DIFF * around
                    new.append((c_centre[f][i] * v + rate * other[i]) + around)
            state = tuple(new)
        return state

    for o in range(1, nr):
        rf_copy(o).wait_recv()

    def j_copy(o):
        return pltpu.make_async_remote_copy(
            jall.at[t], jall.at[t], jsend.at[o], jrecv.at[t],
            device_id=(t + o, r), device_id_type=MESH)

    @pl.when(has_next)
    def _():
        for o in range(1, nr):
            rs_copy(o).wait_recv()
        jall[t] = rf[...] - rsn[...]

    for o in range(1, nt):
        pl.when(t + o < nt)(lambda: j_copy(o).start())

    def link(n, state):
        pltpu.make_async_remote_copy(
            jall.at[n], jall.at[n], jsend.at[0], jrecv.at[n],
            device_id=(n, r), device_id_type=MESH).wait_recv()
        state = coarse_prop(state)
        return tuple(state[f * nr + i] + jall[n, i, f] for f in range(2) for i in range(nr))

    state = tuple(jnp.zeros((SUB, width // COARSEN), jnp.float32) for _ in range(2 * nr))
    state = lax.fori_loop(0, t, link, state)
    state = coarse_prop(state)

    mine = [state[f * nr] for f in range(2)]
    for f in range(2):
        for i in range(nr):
            value = state[f * nr + i]
            nxt_ref[f, pl.ds(i, SUB, stride=nr), :] = value + rf[i, f]
            if i > 0:
                mine[f] = jnp.where(r == i, value, mine[f])

    spread_back = lax.dot_general(
        *split_terms(jnp.concatenate(mine, axis=0), pool), (((1,), (1,)), ((), ())),
        preferred_element_type=jnp.float32) * float(COARSEN * COARSEN)
    rows = 2 * SUB
    fix = spread_back[:rows] + spread_back[rows:2 * rows] + spread_back[2 * rows:]
    for f in range(2):
        for row in range(SUB):
            end = vb[0, SUB + row, f] + fix[f * SUB:(f + 1) * SUB]
            for m in range(tiles):
                out_ref[f, pl.ds(m * SUB + row, SUB, stride=tiles * SUB), :] = end[:, m * LANES:(m + 1) * LANES]

    for d in range(1, FINE + 1):
        for side in range(2):
            pl.when(sends[side])(lambda: v_copy(side, d).wait_send())
            when_mine(d, sends[side], lambda: k_copy(side, d).wait_send())

            def passed_on():
                for o in range(1, group):
                    k_forward(side, d, o).wait_send()
            when_mine(d, gets[side], passed_on)
    for o in range(1, nr):
        kc_copy(o).wait_send()
        rf_copy(o).wait_send()

    pl.when(has_prev)(lambda: rs_first().wait_send())

    @pl.when(has_next)
    def _():
        for o in range(1, nr):
            rs_copy(o).wait_send()

    for o in range(1, nt):
        pl.when(t + o < nt)(lambda: j_copy(o).wait_send())


def split_terms(x, pool):
    hi = x.astype(jnp.bfloat16).astype(jnp.float32)
    mid = (x - hi).astype(jnp.bfloat16).astype(jnp.float32)
    low = x - hi - mid
    return jnp.concatenate([hi, mid, low], axis=0).astype(jnp.bfloat16), pool[...]


def deliver(ends, following, ends_out, following_out, sem):
    first = pltpu.make_async_copy(ends, ends_out, sem.at[0])
    second = pltpu.make_async_copy(following, following_out, sem.at[1])
    first.start()
    second.start()
    first.wait()
    second.wait()


def body(nt, nr, starts, conductivity):
    rows, columns = conductivity.shape
    assert rows == SUB == COARSEN == FINE
    width = columns // SUB
    blocks = columns // LANES
    ncoarse = width // COARSEN
    group = math.gcd(SHARE, nt)
    slab = starts[0].reshape(2, rows, blocks, LANES).transpose(0, 2, 1, 3).reshape(2, blocks * rows, LANES)
    kappa = conductivity.reshape(rows, blocks, LANES).transpose(1, 0, 2).reshape(blocks * rows, LANES)
    slab = pltpu.with_memory_space_constraint(slab, pltpu.HBM)
    kappa = pltpu.with_memory_space_constraint(kappa, pltpu.HBM)
    f32 = jnp.float32
    dma = pltpu.SemaphoreType.DMA
    ends, following = pl.pallas_call(
        functools.partial(kernel, nt, nr, group),
        out_shape=(
            jax.ShapeDtypeStruct((2, blocks * rows, LANES), f32),
            jax.ShapeDtypeStruct((2, SUB * nr, ncoarse), f32),
        ),
        in_specs=[pl.BlockSpec(memory_space=pltpu.HBM)] * 2,
        out_specs=[pl.BlockSpec(memory_space=pltpu.VMEM)] * 2,
        scratch_shapes=[
            pltpu.VMEM((2, blocks * rows, LANES), f32),
            pltpu.VMEM((blocks * rows, LANES), f32),
            dma((2,)),
            pltpu.VMEM((2, 3 * SUB, 2, SUB, width), f32),
            pltpu.VMEM((SUB, 2, SUB, width), f32),
            pltpu.VMEM((SUB, SUB, width), f32),
            pltpu.VMEM((2, FINE, SUB, width), f32),
            pltpu.VMEM((3 * SUB, SUB, width), f32),
            pltpu.VMEM((3 * SUB, SUB, width), f32),
            pltpu.VMEM((3 * SUB, SUB, width), f32),
            pltpu.VMEM((3 * SUB, SUB, width), f32),
            pltpu.VMEM((3 * SUB, SUB, width), f32),
            pltpu.VMEM((3 * SUB, SUB, width), f32),
            pltpu.VMEM((width, ncoarse), jnp.bfloat16),
            pltpu.VMEM((SUB, ncoarse), f32),
            pltpu.VMEM((2, SUB, ncoarse), f32),
            pltpu.VMEM((2, SUB, ncoarse), f32),
            pltpu.VMEM((nr, SUB, ncoarse), f32),
            pltpu.VMEM((nr, 2, SUB, ncoarse), f32),
            pltpu.VMEM((nr, 2, SUB, ncoarse), f32),
            pltpu.VMEM((nt, nr, 2, SUB, ncoarse), f32),
            dma((2, FINE)), dma((2, FINE)),
            dma((2, FINE)), dma((2, FINE)), dma((2, FINE, group)),
            dma((nr,)), dma((nr,)),
            dma((nr,)), dma((nr,)),
            dma((nr,)), dma((nr,)),
            dma((nt,)), dma((nt,)),
            pltpu.SemaphoreType.REGULAR, pltpu.SemaphoreType.REGULAR,
        ],
        compiler_params=pltpu.CompilerParams(
            collective_id=0, has_side_effects=True, vmem_limit_bytes=48 * 1024 * 1024),
        name="parareal",
    )(slab, kappa)
    ends, following = pl.pallas_call(
        deliver,
        out_shape=(
            jax.ShapeDtypeStruct(ends.shape, f32),
            jax.ShapeDtypeStruct(following.shape, f32),
        ),
        in_specs=[pl.BlockSpec(memory_space=pltpu.VMEM)] * 2,
        out_specs=[pl.BlockSpec(memory_space=pltpu.HBM)] * 2,
        scratch_shapes=[dma((2,))],
        compiler_params=pltpu.CompilerParams(vmem_limit_bytes=1024 * 1024),
        name="deliver",
    )(ends, following)
    new_ends = ends.reshape(2, blocks, rows, LANES).transpose(0, 2, 1, 3).reshape(2, rows, columns)
    coarse_next = following.reshape(2, SUB, nr, ncoarse).transpose(0, 2, 1, 3).reshape(2, nr, SUB * ncoarse)
    return new_ends[None], coarse_next[None]


def solution(mesh):
    nt, nr = mesh.shape["tm"], mesh.shape["rows"]
    in_specs = (P("tm", None, "rows", None), P("rows", None))
    out_specs = (P("tm", None, "rows", None), P("tm", None, None, None))
    return jax.shard_map(functools.partial(body, nt, nr), mesh=mesh, in_specs=in_specs, out_specs=out_specs, check_vma=False)
```

```python
import functools
import math

import jax
import jax.numpy as jnp
from jax import lax
from jax.experimental import pallas as pl
from jax.experimental.pallas import tpu as pltpu
from jax.sharding import PartitionSpec as P

FINE = 8
COARSE = 2
COARSEN = 8
EXCHANGE = 0.05
TRACER_DIFF = 0.5

SUB = 8
LANES = 128
MESH = pl.DeviceIdType.MESH
SHARE = 2
EARLY = 2
AREA = 1.0 / (COARSEN * COARSEN)


def lane_index():
    return lax.broadcasted_iota(jnp.int32, (SUB, LANES), 1)


def following(v):
    lane = lane_index()
    wrapped = pltpu.roll(pltpu.roll(v, LANES - 1, 1), SUB - 1, 0)
    edge = jnp.where(lane < LANES - 1, pltpu.roll(v, LANES - SUB - 1, 1), wrapped)
    return jnp.where(lane < LANES - SUB, pltpu.roll(v, LANES - SUB, 1), edge)


def preceding(v):
    lane = lane_index()
    wrapped = pltpu.roll(pltpu.roll(v, 1, 1), 1, 0)
    edge = jnp.where(lane >= 1, pltpu.roll(v, SUB + 1, 1), wrapped)
    return jnp.where(lane >= SUB, pltpu.roll(v, SUB, 1), edge)


def to_right(v):
    return jnp.concatenate([v[1:], following(v[0])[None]], axis=0)


def to_left(v):
    return jnp.concatenate([preceding(v[COARSEN - 1])[None], v[:COARSEN - 1]], axis=0)


def exchange_lanes(rows):
    lane = lane_index()
    rows = list(rows)
    for step in (1, 2, 4):
        high = (lane & step) != 0
        for i in range(SUB):
            if not i & step:
                a, b = rows[i], rows[i | step]
                rows[i] = jnp.where(high, pltpu.roll(b, step, 1), a)
                rows[i | step] = jnp.where(high, b, pltpu.roll(a, LANES - step, 1))
    return rows


def exact_dot(x, w):
    rows = x.shape[0]
    hi = x.astype(jnp.bfloat16)
    rest = x - hi.astype(jnp.float32)
    mid = rest.astype(jnp.bfloat16)
    low = (rest - mid.astype(jnp.float32)).astype(jnp.bfloat16)
    y = jnp.dot(jnp.concatenate([hi.astype(jnp.float32), mid.astype(jnp.float32), low.astype(jnp.float32)], axis=0).astype(jnp.bfloat16), w,
                preferred_element_type=jnp.float32)
    return y[:rows] + y[rows:2 * rows] + y[2 * rows:]


def kernel(nt, nr, group, s_hbm, k_hbm, out_ref, nxt_ref,
           s_ref, k_ref, in_sem, wb, ub, own, kown, kh, kr, kl, kd, ku, ch, ct, part, order, ers, erg, cts, ctg, jall,
           vsend, vrecv, ksend, krecv, kfwd, ersend, errecv, ctsend, ctrecv, jsend, jrecv, tok_down, tok_up):
    t = lax.axis_index("tm")
    r = lax.axis_index("rows")
    member = lax.rem(t, group)
    base = t - member
    has_up = r > 0
    has_down = r < nr - 1
    sends = (has_down, has_up)
    gets = (has_up, has_down)
    f32 = jnp.float32

    k_in = pltpu.make_async_copy(k_hbm, k_ref, in_sem.at[0])
    s_in = pltpu.make_async_copy(s_hbm, s_ref, in_sem.at[1])
    k_in.start()
    s_in.start()

    barrier = pltpu.get_barrier_semaphore()

    def greet(tm, row):
        pl.semaphore_signal(barrier, inc=1, device_id=(tm, row), device_id_type=MESH)

    pl.when(has_up)(lambda: greet(t, r - 1))
    pl.when(has_down)(lambda: greet(t, r + 1))
    for o in range(1, nt):
        greet(lax.rem(t + o, nt), r)

    source = lax.broadcasted_iota(jnp.int32, order.shape, 0)
    target = lax.broadcasted_iota(jnp.int32, order.shape, 1)
    goes = (source & (SUB - 1)) * (LANES // SUB) + (source >> 3)
    order[...] = jnp.where(goes == target, 1.0, 0.0).astype(jnp.bfloat16)
    for d in range(1, FINE):
        zero = jnp.zeros(wb.shape[2:], f32)
        wb[(d - 1) % 2, SUB - d] = zero
        wb[(d - 1) % 2, 2 * SUB - 1 + d] = zero

    @pl.when(jnp.logical_not(has_up))
    def _():
        ub[0, 0:SUB] = jnp.zeros((SUB,) + ub.shape[2:], f32)
        kh[0] = jnp.zeros(kh.shape[1:], f32)

    @pl.when(jnp.logical_not(has_down))
    def _():
        ub[0, 2 * SUB:] = jnp.zeros((SUB,) + ub.shape[2:], f32)
        kh[1] = jnp.zeros(kh.shape[1:], f32)

    def read_row(ref, row):
        return jnp.stack(exchange_lanes(
            [ref[pl.ds(m * SUB + row, SUB, stride=SUB * SUB), :] for m in range(SUB)]), axis=0)

    outer_first = [row for d in range(SUB // 2) for row in (SUB - 1 - d, d)]

    k_in.wait()
    total = None
    for row in outer_first:
        x = read_row(k_ref, row)
        kown[row] = x
        total = x if total is None else total + x
    ers[0] = jnp.sum(total, axis=0) * AREA

    pl.semaphore_wait(barrier, (nt - 1) + has_up.astype(jnp.int32) + has_down.astype(jnp.int32))

    def tell(tok, row):
        pl.semaphore_signal(tok, inc=1, device_id=(t, row), device_id_type=MESH)

    pl.when(jnp.logical_not(has_up) & has_down)(lambda: tell(tok_down, r + 1))
    pl.when(jnp.logical_not(has_down) & has_up)(lambda: tell(tok_up, r - 1))

    def v_copy(side, d):
        if side == 0:
            return pltpu.make_async_remote_copy(
                own.at[SUB - d], ub.at[0, SUB - d], vsend.at[side, d - 1], vrecv.at[side, d - 1],
                device_id=(t, r + 1), device_id_type=MESH)
        return pltpu.make_async_remote_copy(
            own.at[d - 1], ub.at[0, 2 * SUB - 1 + d], vsend.at[side, d - 1], vrecv.at[side, d - 1],
            device_id=(t, r - 1), device_id_type=MESH)

    def k_copy(side, d):
        return pltpu.make_async_remote_copy(
            kown.at[SUB - d if side == 0 else d - 1], kh.at[side, d - 1], ksend.at[side, d - 1], krecv.at[side, d - 1],
            device_id=(t, r + 1 if side == 0 else r - 1), device_id_type=MESH)

    def k_forward(side, d, o):
        return pltpu.make_async_remote_copy(
            kh.at[side, d - 1], kh.at[side, d - 1], kfwd.at[side, d - 1, o], krecv.at[side, d - 1],
            device_id=(base + lax.rem(member + o, group), r), device_id_type=MESH)

    def mine(d):
        return member == (d - 1) % group

    def er_copy(o):
        return pltpu.make_async_remote_copy(
            ers, erg.at[r], ersend.at[o], errecv.at[o],
            device_id=(t, lax.rem(r + o, nr)), device_id_type=MESH)

    def ct_copy(o):
        return pltpu.make_async_remote_copy(
            cts, ctg.at[r], ctsend.at[o], ctrecv.at[o],
            device_id=(t, lax.rem(r + o, nr)), device_id_type=MESH)

    def j_copy(o):
        return pltpu.make_async_remote_copy(
            jall.at[t], jall.at[t], jsend.at[o], jrecv.at[t],
            device_id=(t + o, r), device_id_type=MESH)

    for d in range(1, FINE + 1):
        for side in range(2):
            pl.when(sends[side] & mine(d))(lambda: k_copy(side, d).start())

    s_in.wait()
    sums = [None, None]
    for row in outer_first:
        for f in range(2):
            x = read_row(s_ref.at[f], row)
            own[row, f] = x
            wb[0, SUB + row, f] = x
            ub[0, SUB + row, f] = x
            sums[f] = x if sums[f] is None else sums[f] + x
    for f in range(2):
        ers[1 + f] = jnp.sum(sums[f], axis=0) * AREA
    erg[r] = ers[...]

    def send_rows(first, last):
        for d in range(first, last + 1):
            for side in range(2):
                pl.when(sends[side])(lambda: v_copy(side, d).start())

    send_rows(1, EARLY)

    def columns_of(i, k):
        right = 0.5 * (k + to_right(k))
        kr[i] = right
        kl[i] = preceding(right[COARSEN - 1])

    def left_of(i):
        return jnp.concatenate([kl[i][None], kr[i, 0:COARSEN - 1]], axis=0)

    def centre_of(i):
        total = (kr[i] + left_of(i)) + (ku[i] + kd[i])
        ch[i] = (1.0 - EXCHANGE) - total
        ct[i] = (1.0 - EXCHANGE) - TRACER_DIFF * total

    for row in range(SUB):
        k = kown[row]
        columns_of(SUB + row, k)
        if row < SUB - 1:
            face = 0.5 * (k + kown[row + 1])
            kd[SUB + row] = face
            ku[SUB + row + 1] = face
        if 0 < row < SUB - 1:
            centre_of(SUB + row)

    def advance(buf, p, i, above=True, below=True):
        heat, tracer = buf[p, i, 0], buf[p, i, 1]
        right, left = kr[i], left_of(i)
        terms = [right * to_right(heat) + left * to_left(heat), right * to_right(tracer) + left * to_left(tracer)]
        if below:
            face = kd[i]
            terms = [terms[f] + face * buf[p, i + 1, f] for f in range(2)]
        if above:
            face = ku[i]
            terms = [terms[f] + face * buf[p, i - 1, f] for f in range(2)]
        return ((ch[i] * heat + EXCHANGE * tracer) + terms[0],
                (ct[i] * tracer + EXCHANGE * heat) + TRACER_DIFF * terms[1])

    for level in range(1, SUB // 2):
        p = (level - 1) % 2
        for row in range(level, SUB - level):
            heat, tracer = advance(wb, p, SUB + row)
            for f, x in enumerate((heat, tracer)):
                wb[1 - p, SUB + row, f] = x
                ub[1 - p, SUB + row, f] = x

    @pl.when(has_up)
    def _():
        pl.semaphore_wait(tok_down, 1)
        pl.when(has_down)(lambda: tell(tok_down, r + 1))

    @pl.when(has_down)
    def _():
        pl.semaphore_wait(tok_up, 1)
        pl.when(has_up)(lambda: tell(tok_up, r - 1))

    for o in range(1, nr):
        er_copy(o).start()

    def pass_on(d):
        for side in range(2):
            @pl.when(gets[side] & mine(d))
            def _():
                k_copy(side, d).wait_recv()
                for o in range(1, group):
                    k_forward(side, d, o).start()

    outside = (jnp.where(has_up, 1.0, 0.0), jnp.where(has_down, 1.0, 0.0))

    def faces_at(d):
        for side in range(2):
            pl.when(gets[side] & jnp.logical_not(mine(d)))(lambda: k_copy(side, d).wait_recv())
            k = kh[side, d - 1]
            inner = kh[side, d - 2] if d > 1 else kown[0 if side == 0 else SUB - 1]
            face = 0.5 * (k + inner)
            edge = face * outside[side] if d == 1 else face
            i = SUB - d if side == 0 else 2 * SUB - 1 + d
            columns_of(i, k)
            if side == 0:
                ku[i + 1] = face
                kd[i] = edge
                centre_of(i + 1)
            else:
                kd[i - 1] = face
                ku[i] = edge
                centre_of(i - 1)

    pass_on(1)
    for level in range(1, FINE):
        pass_on(level + 1)
        faces_at(level)
        p = (level - 1) % 2
        first, last = SUB + 1 - level, 2 * SUB - 2 + level
        for i in range(first, last + 1):
            if SUB + level <= i < 2 * SUB - level:
                continue
            heat, tracer = advance(wb, p, i)
            wb[1 - p, i, 0] = heat
            wb[1 - p, i, 1] = tracer
        for i, inner, face in ((first - 1, first, kd), (last + 1, last, ku)):
            for f in range(2):
                wb[1 - p, i, f] = (1.0, TRACER_DIFF)[f] * face[i] * wb[p, inner, f]

    p = (FINE - 1) % 2
    fluxes = [[jnp.sum(ku[SUB] * (wb[p, SUB - 1, f] - wb[p, SUB, f]), axis=0) for f in range(2)],
              [jnp.sum(kd[2 * SUB - 1] * (wb[p, 2 * SUB, f] - wb[p, 2 * SUB - 1, f]), axis=0) for f in range(2)]]
    for b in range(3):
        whole, gain = [], []
        for f in range(2):
            total, side_flux = None, None
            for i in range(max(1, SUB * b), min(3 * SUB - 1, SUB * (b + 1))):
                x = wb[p, i, f]
                flux = kr[i, COARSEN - 1] * (following(x[0]) - x[COARSEN - 1])
                total = x if total is None else total + x
                side_flux = flux if side_flux is None else side_flux + flux
            change = side_flux - preceding(side_flux)
            if b == 0:
                change = change - fluxes[0][f]
            elif b == 1:
                change = change + (fluxes[0][f] + fluxes[1][f])
            else:
                change = change - fluxes[1][f]
            whole.append(jnp.sum(total, axis=0))
            gain.append((1.0, TRACER_DIFF)[f] * change)
        moved = EXCHANGE * (whole[1] - whole[0])
        cts[b, 0] = AREA * ((whole[0] + moved) + gain[0])
        cts[b, 1] = AREA * ((whole[1] - moved) + gain[1])
    for o in range(1, nr):
        ct_copy(o).start()
    ctg[r] = cts[...]
    send_rows(EARLY + 1, FINE)

    faces_at(FINE)

    def row_pair(level, diagonal):
        p = lax.rem(level + 1, 2)
        new = [(i,) + advance(ub, p, i) for i in (SUB + level - diagonal, 2 * SUB - 1 - level + diagonal)]
        for i, heat, tracer in new:
            ub[1 - p, i, 0] = heat
            ub[1 - p, i, 1] = tracer

    def run_diagonal(diagonal):
        for side in range(2):
            pl.when(gets[side])(lambda: v_copy(side, diagonal).wait_recv())

        def step(level, carry):
            row_pair(level, diagonal)
            return carry
        lax.fori_loop(1, min(FINE, SUB // 2 - 1 + diagonal) + 1, step, 0)

    ratio = (FINE / COARSE) / float(COARSEN * COARSEN)
    rate = EXCHANGE * (FINE / COARSE)

    run_diagonal(1)
    run_diagonal(2)

    for o in range(1, nr):
        er_copy(o).wait_recv()
    kcv = [erg[i, 0] for i in range(nr)]
    c_right = [ratio * 0.5 * (k + following(k)) for k in kcv]
    c_left = [ratio * 0.5 * (k + preceding(k)) for k in kcv]
    c_face = [ratio * 0.5 * kcv[0]]
    c_face += [ratio * 0.5 * (kcv[i] + kcv[i + 1]) for i in range(nr - 1)]
    c_face += [ratio * 0.5 * kcv[nr - 1]]
    totals = [(c_right[i] + c_left[i]) + (c_face[i] + c_face[i + 1]) for i in range(nr)]
    c_centre = [[(1.0 - rate) - x for x in totals], [(1.0 - rate) - TRACER_DIFF * x for x in totals]]

    def coarse_prop(state):
        for substep in range(COARSE):
            new = []
            for f in range(2):
                rows = state[f * nr:(f + 1) * nr]
                other = state[(1 - f) * nr:(2 - f) * nr]
                for i in range(nr):
                    v = rows[i]
                    around = c_right[i] * following(v) + c_left[i] * preceding(v)
                    if i > 0:
                        around = around + c_face[i] * rows[i - 1]
                    if i < nr - 1:
                        around = around + c_face[i + 1] * rows[i + 1]
                    if f == 1:
                        around = TRACER_DIFF * around
                    new.append((c_centre[f][i] * v + rate * other[i]) + around)
            state = tuple(new)
        return state

    later = jnp.where(t > 0, 1.0, 0.0)
    old = coarse_prop(tuple(later * erg[i, 1 + f] for f in range(2) for i in range(nr)))

    for o in range(1, nr):
        ct_copy(o).wait_recv()
    change = []
    for f in range(2):
        for i in range(nr):
            x = ctg[i, 1, f]
            if i > 0:
                x = x + ctg[i - 1, 2, f]
            if i < nr - 1:
                x = x + ctg[i + 1, 0, f]
            x = x - old[f * nr + i]
            jall[t, i, f] = x
            change.append(x)
    for o in range(1, nt):
        pl.when(t + o < nt)(lambda: j_copy(o).start())

    for d in range(3, FINE):
        run_diagonal(d)

    def place(level, side):
        return level if side == 0 else 3 * SUB - 1 - level

    for level in range(1, FINE + 1):
        for side in range(2):
            heat, tracer = advance(ub, (level - 1) % 2, place(level, side), above=side == 1, below=side == 0)
            part[level - 1, side, 0] = heat
            part[level - 1, side, 1] = tracer

    def link(n, state):
        pltpu.make_async_remote_copy(
            jall.at[n], jall.at[n], jsend.at[0], jrecv.at[n],
            device_id=(n, r), device_id_type=MESH).wait_recv()
        state = coarse_prop(state)
        return tuple(state[f * nr + i] + jall[n, i, f] for f in range(2) for i in range(nr))

    state = tuple(jnp.zeros((SUB, LANES), f32) for _ in range(2 * nr))
    state = lax.fori_loop(0, t, link, state)
    state = coarse_prop(state)

    fix = [None, None]
    for f in range(2):
        for i in range(nr):
            value = state[f * nr + i] - old[f * nr + i]
            fix[f] = value if i == 0 else jnp.where(r == i, value, fix[f])
    natural = exact_dot(jnp.concatenate([state[n] + change[n] for n in range(2 * nr)], axis=0), order[...])
    for f in range(2):
        for i in range(nr):
            n = f * nr + i
            nxt_ref[f, pl.ds(i, SUB, stride=nr), :] = natural[n * SUB:(n + 1) * SUB]

    def write_row(row, f, end):
        end = exchange_lanes([end[m] + fix[f] for m in range(COARSEN)])
        for m in range(SUB):
            out_ref[f, pl.ds(m * SUB + row, SUB, stride=SUB * SUB), :] = end[m]

    for row in range(1, SUB - 1):
        for f in range(2):
            write_row(row, f, ub[0, SUB + row, f])

    last = []
    for side in range(2):
        pl.when(gets[side])(lambda: v_copy(side, FINE).wait_recv())
    for side in range(2):
        i = place(0, side)
        last.append([ub[0, i, 0], ub[0, i, 1]])
    for level in range(1, FINE + 1):
        for side in range(2):
            face = (ku, kd)[side][place(level, side)]
            heat, tracer = last[side]
            last[side] = [part[level - 1, side, 0] + face * heat,
                          part[level - 1, side, 1] + (TRACER_DIFF * face) * tracer]
    for side in range(2):
        for f in range(2):
            write_row((0, SUB - 1)[side], f, last[side][f])

    for d in range(1, FINE + 1):
        for side in range(2):
            pl.when(sends[side])(lambda: v_copy(side, d).wait_send())
            pl.when(sends[side] & mine(d))(lambda: k_copy(side, d).wait_send())

            @pl.when(gets[side] & mine(d))
            def _():
                for o in range(1, group):
                    k_forward(side, d, o).wait_send()
    for o in range(1, nr):
        er_copy(o).wait_send()
        ct_copy(o).wait_send()
    for o in range(1, nt):
        pl.when(t + o < nt)(lambda: j_copy(o).wait_send())


def deliver(ends, following, ends_out, following_out, sem):
    first = pltpu.make_async_copy(ends, ends_out, sem.at[0])
    second = pltpu.make_async_copy(following, following_out, sem.at[1])
    first.start()
    second.start()
    first.wait()
    second.wait()


def body(nt, nr, starts, conductivity):
    rows, columns = conductivity.shape
    assert rows == SUB == COARSEN == FINE
    assert columns == COARSEN * SUB * LANES
    blocks = columns // LANES
    group = math.gcd(SHARE, nt)
    slab = starts[0].reshape(2, rows, blocks, LANES).transpose(0, 2, 1, 3).reshape(2, blocks * rows, LANES)
    kappa = conductivity.reshape(rows, blocks, LANES).transpose(1, 0, 2).reshape(blocks * rows, LANES)
    slab = pltpu.with_memory_space_constraint(slab, pltpu.HBM)
    kappa = pltpu.with_memory_space_constraint(kappa, pltpu.HBM)
    f32 = jnp.float32
    dma = pltpu.SemaphoreType.DMA
    cell = (SUB, LANES)
    line = (COARSEN,) + cell
    ends, following = pl.pallas_call(
        functools.partial(kernel, nt, nr, group),
        out_shape=(
            jax.ShapeDtypeStruct((2, blocks * rows, LANES), f32),
            jax.ShapeDtypeStruct((2, SUB * nr, LANES), f32),
        ),
        in_specs=[pl.BlockSpec(memory_space=pltpu.HBM)] * 2,
        out_specs=[pl.BlockSpec(memory_space=pltpu.VMEM)] * 2,
        scratch_shapes=[
            pltpu.VMEM((2, blocks * rows, LANES), f32),
            pltpu.VMEM((blocks * rows, LANES), f32),
            dma((2,)),
            pltpu.VMEM((2, 3 * SUB, 2) + line, f32),
            pltpu.VMEM((2, 3 * SUB, 2) + line, f32),
            pltpu.VMEM((SUB, 2) + line, f32),
            pltpu.VMEM((SUB,) + line, f32),
            pltpu.VMEM((2, FINE) + line, f32),
            pltpu.VMEM((3 * SUB,) + line, f32),
            pltpu.VMEM((3 * SUB,) + cell, f32),
            pltpu.VMEM((3 * SUB,) + line, f32),
            pltpu.VMEM((3 * SUB,) + line, f32),
            pltpu.VMEM((3 * SUB,) + line, f32),
            pltpu.VMEM((3 * SUB,) + line, f32),
            pltpu.VMEM((FINE, 2, 2) + line, f32),
            pltpu.VMEM((LANES, LANES), jnp.bfloat16),
            pltpu.VMEM((3,) + cell, f32),
            pltpu.VMEM((nr, 3) + cell, f32),
            pltpu.VMEM((3, 2) + cell, f32),
            pltpu.VMEM((nr, 3, 2) + cell, f32),
            pltpu.VMEM((nt, nr, 2) + cell, f32),
            dma((2, FINE)), dma((2, FINE)),
            dma((2, FINE)), dma((2, FINE)), dma((2, FINE, group)),
            dma((nr,)), dma((nr,)),
            dma((nr,)), dma((nr,)),
            dma((nt,)), dma((nt,)),
            pltpu.SemaphoreType.REGULAR, pltpu.SemaphoreType.REGULAR,
        ],
        compiler_params=pltpu.CompilerParams(
            collective_id=0, has_side_effects=True, vmem_limit_bytes=48 * 1024 * 1024),
        name="parareal",
    )(slab, kappa)
    ends, following = pl.pallas_call(
        deliver,
        out_shape=(
            jax.ShapeDtypeStruct(ends.shape, f32),
            jax.ShapeDtypeStruct(following.shape, f32),
        ),
        in_specs=[pl.BlockSpec(memory_space=pltpu.VMEM)] * 2,
        out_specs=[pl.BlockSpec(memory_space=pltpu.HBM)] * 2,
        scratch_shapes=[dma((2,))],
        compiler_params=pltpu.CompilerParams(vmem_limit_bytes=1024 * 1024),
        name="deliver",
    )(ends, following)
    new_ends = ends.reshape(2, blocks, rows, LANES).transpose(0, 2, 1, 3).reshape(2, rows, columns)
    coarse_next = following.reshape(2, SUB, nr, LANES).transpose(0, 2, 1, 3).reshape(2, nr, SUB * LANES)
    return new_ends[None], coarse_next[None]


def solution(mesh):
    nt, nr = mesh.shape["tm"], mesh.shape["rows"]
    in_specs = (P("tm", None, "rows", None), P("rows", None))
    out_specs = (P("tm", None, "rows", None), P("tm", None, None, None))
    return jax.shard_map(functools.partial(body, nt, nr), mesh=mesh, in_specs=in_specs, out_specs=out_specs, check_vma=False)
```

```python
import functools
import math

import jax
import jax.numpy as jnp
from jax import lax
from jax.experimental import pallas as pl
from jax.experimental.pallas import tpu as pltpu
from jax.sharding import PartitionSpec as P

FINE = 8
COARSE = 2
COARSEN = 8
EXCHANGE = 0.05
TRACER_DIFF = 0.5

SUB = 8
LANES = 128
MESH = pl.DeviceIdType.MESH
SHARE = 2
EARLY = 3
SLOTS = 3
AREA = 1.0 / (COARSEN * COARSEN)


def cell_index(axis):
    return lax.broadcasted_iota(jnp.int32, (SUB, LANES), axis)


def following(v):
    lane = cell_index(1)
    near = pltpu.roll(v, LANES - SUB, 1)
    far = jnp.where(lane < LANES - 1, pltpu.roll(v, LANES - SUB - 1, 1), pltpu.roll(v, LANES - 1, 1))
    edge = pltpu.roll(jnp.where(cell_index(0) == 0, far, near), SUB - 1, 0)
    return jnp.where(lane < LANES - SUB, near, edge)


def preceding(v):
    lane = cell_index(1)
    near = pltpu.roll(v, SUB, 1)
    far = jnp.where(lane >= 1, pltpu.roll(v, SUB + 1, 1), pltpu.roll(v, 1, 1))
    edge = pltpu.roll(jnp.where(cell_index(0) == SUB - 1, far, near), 1, 0)
    return jnp.where(lane >= SUB, near, edge)


def lines_to_lanes(v):
    lane, line = cell_index(1), cell_index(0)
    for step in (1, 2, 4):
        high_lane, high_line = (lane & (step * 16)) != 0, (line & step) != 0
        up = pltpu.roll(pltpu.roll(v, SUB - step, 0), step * 16, 1)
        down = pltpu.roll(pltpu.roll(v, step, 0), LANES - step * 16, 1)
        v = jnp.where(high_lane, jnp.where(high_line, v, up), jnp.where(high_line, down, v))
    return v


def to_right(v):
    return jnp.concatenate([v[1:], following(v[0])[None]], axis=0)


def to_left(v):
    return jnp.concatenate([preceding(v[COARSEN - 1])[None], v[:COARSEN - 1]], axis=0)


def exchange_lanes(rows):
    lane = cell_index(1)
    rows = list(rows)
    for step in (1, 2, 4):
        high = (lane & step) != 0
        for i in range(SUB):
            if not i & step:
                a, b = rows[i], rows[i | step]
                rows[i] = jnp.where(high, pltpu.roll(b, step, 1), a)
                rows[i | step] = jnp.where(high, b, pltpu.roll(a, LANES - step, 1))
    return rows


def exact_dot(x, w):
    rows = x.shape[0]
    hi = x.astype(jnp.bfloat16)
    rest = x - hi.astype(jnp.float32)
    mid = rest.astype(jnp.bfloat16)
    low = (rest - mid.astype(jnp.float32)).astype(jnp.bfloat16)
    y = jnp.dot(jnp.concatenate([hi.astype(jnp.float32), mid.astype(jnp.float32), low.astype(jnp.float32)], axis=0).astype(jnp.bfloat16), w,
                preferred_element_type=jnp.float32)
    return y[:rows] + y[rows:2 * rows] + y[2 * rows:]


def kernel(nt, nr, group, s_hbm, k_hbm, out_ref, nxt_ref,
           s_ref, k_ref, in_sem, wb, ub, own, kown, kh, kr, kl, kd, ku, ch, ct, part, order, ers, erg, cts, ctg, jall,
           vsend, vrecv, ksend, krecv, kfwd, ersend, errecv, ctsend, ctrecv, jsend, jrecv, tok_down, tok_up, tok_tm):
    t = lax.axis_index("tm")
    r = lax.axis_index("rows")
    member = lax.rem(t, group)
    base = t - member
    has_up = r > 0
    has_down = r < nr - 1
    sends = (has_down, has_up)
    gets = (has_up, has_down)
    f32 = jnp.float32

    outer_first = [row for d in range(SUB // 2) for row in (SUB - 1 - d, d)]

    k_in = pltpu.make_async_copy(k_hbm, k_ref, in_sem.at[0])
    s_in = pltpu.make_async_copy(s_hbm, s_ref, in_sem.at[1])
    k_in.start()
    s_in.start()

    barrier = pltpu.get_barrier_semaphore()

    def greet(tm, row):
        pl.semaphore_signal(barrier, inc=1, device_id=(tm, row), device_id_type=MESH)

    pl.when(has_up)(lambda: greet(t, r - 1))
    pl.when(has_down)(lambda: greet(t, r + 1))
    for o in range(1, nt):
        pl.when(t + o < nt)(lambda: greet(t + o, r))
    for o in range(1, group):
        pl.when(member >= o)(lambda: greet(t - o, r))

    source = lax.broadcasted_iota(jnp.int32, order.shape, 0)
    target = lax.broadcasted_iota(jnp.int32, order.shape, 1)
    goes = (source & (SUB - 1)) * (LANES // SUB) + (source >> 3)
    order[...] = jnp.where(goes == target, 1.0, 0.0).astype(jnp.bfloat16)
    for d in range(1, FINE):
        zero = jnp.zeros(wb.shape[2:], f32)
        wb[(d - 1) % 2, SUB - d] = zero
        wb[(d - 1) % 2, 2 * SUB - 1 + d] = zero

    @pl.when(jnp.logical_not(has_up))
    def _():
        ub[0, 0:SUB] = jnp.zeros((SUB,) + ub.shape[2:], f32)
        kh[0] = jnp.zeros(kh.shape[1:], f32)

    @pl.when(jnp.logical_not(has_down))
    def _():
        ub[0, 2 * SUB:] = jnp.zeros((SUB,) + ub.shape[2:], f32)
        kh[1] = jnp.zeros(kh.shape[1:], f32)

    def read_row(ref, row):
        return jnp.stack(exchange_lanes(
            [ref[pl.ds(m * SUB * SUB + row, SUB, stride=SUB), :] for m in range(SUB)]), axis=0)

    k_in.wait()
    total = None
    for row in outer_first:
        x = read_row(k_ref, row)
        kown[row] = x
        total = x if total is None else total + x
    ers[0] = jnp.sum(total, axis=0) * AREA

    pl.semaphore_wait(barrier, t + (group - 1 - member) + has_up.astype(jnp.int32) + has_down.astype(jnp.int32))

    def tell(tok, row):
        pl.semaphore_signal(tok, inc=1, device_id=(t, row), device_id_type=MESH)

    pl.when(jnp.logical_not(has_up) & has_down)(lambda: tell(tok_down, r + 1))
    pl.when(jnp.logical_not(has_down) & has_up)(lambda: tell(tok_up, r - 1))

    for o in range(1, nt):
        @pl.when(t >= o)
        def _():
            pl.semaphore_signal(tok_tm, inc=1, device_id=(t - o, r), device_id_type=MESH)

    def relay(slot):
        @pl.when(has_up & (jnp.minimum(r - 1, SLOTS - 1) == slot))
        def _():
            pl.semaphore_wait(tok_down, 1)
            pl.when(has_down)(lambda: tell(tok_down, r + 1))

        @pl.when(has_down & (jnp.minimum(nr - 2 - r, SLOTS - 1) == slot))
        def _():
            pl.semaphore_wait(tok_up, 1)
            pl.when(has_up)(lambda: tell(tok_up, r - 1))

    def v_copy(side, d):
        if side == 0:
            return pltpu.make_async_remote_copy(
                own.at[SUB - d], ub.at[0, SUB - d], vsend.at[side, d - 1], vrecv.at[side, d - 1],
                device_id=(t, r + 1), device_id_type=MESH)
        return pltpu.make_async_remote_copy(
            own.at[d - 1], ub.at[0, 2 * SUB - 1 + d], vsend.at[side, d - 1], vrecv.at[side, d - 1],
            device_id=(t, r - 1), device_id_type=MESH)

    def k_copy(side, d):
        return pltpu.make_async_remote_copy(
            kown.at[SUB - d if side == 0 else d - 1], kh.at[side, d - 1], ksend.at[side, d - 1], krecv.at[side, d - 1],
            device_id=(t, r + 1 if side == 0 else r - 1), device_id_type=MESH)

    def k_forward(side, d, o):
        return pltpu.make_async_remote_copy(
            kh.at[side, d - 1], kh.at[side, d - 1], kfwd.at[side, d - 1, o], krecv.at[side, d - 1],
            device_id=(base + lax.rem(member + o, group), r), device_id_type=MESH)

    def mine(d):
        return member == (d - 1) % group

    def er_copy(o):
        return pltpu.make_async_remote_copy(
            ers, erg.at[r], ersend.at[o], errecv.at[o],
            device_id=(t, lax.rem(r + o, nr)), device_id_type=MESH)

    def ct_copy(o):
        return pltpu.make_async_remote_copy(
            cts, ctg.at[r], ctsend.at[o], ctrecv.at[o],
            device_id=(t, lax.rem(r + o, nr)), device_id_type=MESH)

    def j_copy(o):
        return pltpu.make_async_remote_copy(
            jall.at[t], jall.at[t], jsend.at[o], jrecv.at[t],
            device_id=(t + o, r), device_id_type=MESH)

    for d in range(1, FINE + 1):
        for side in range(2):
            pl.when(sends[side] & mine(d))(lambda: k_copy(side, d).start())

    s_in.wait()
    sums = [None, None]
    for row in outer_first:
        for f in range(2):
            x = read_row(s_ref.at[f], row)
            own[row, f] = x
            wb[0, SUB + row, f] = x
            ub[0, SUB + row, f] = x
            sums[f] = x if sums[f] is None else sums[f] + x
    for f in range(2):
        ers[1 + f] = jnp.sum(sums[f], axis=0) * AREA
    erg[r] = ers[...]

    def send_rows(first, last):
        for d in range(first, last + 1):
            for side in range(2):
                pl.when(sends[side])(lambda: v_copy(side, d).start())

    send_rows(1, EARLY)

    def columns_of(i, k):
        right = 0.5 * (k + to_right(k))
        kr[i] = right
        kl[i] = preceding(right[COARSEN - 1])

    def left_of(i):
        return jnp.concatenate([kl[i][None], kr[i, 0:COARSEN - 1]], axis=0)

    def centre_of(i):
        total = (kr[i] + left_of(i)) + (ku[i] + kd[i])
        ch[i] = (1.0 - EXCHANGE) - total
        ct[i] = (1.0 - EXCHANGE) - TRACER_DIFF * total

    for row in range(SUB):
        k = kown[row]
        columns_of(SUB + row, k)
        if row < SUB - 1:
            face = 0.5 * (k + kown[row + 1])
            kd[SUB + row] = face
            ku[SUB + row + 1] = face
        if 0 < row < SUB - 1:
            centre_of(SUB + row)

    def advance(buf, p, i, above=True, below=True):
        heat, tracer = buf[p, i, 0], buf[p, i, 1]
        right, left = kr[i], left_of(i)
        terms = [right * to_right(heat) + left * to_left(heat), right * to_right(tracer) + left * to_left(tracer)]
        if below:
            face = kd[i]
            terms = [terms[f] + face * buf[p, i + 1, f] for f in range(2)]
        if above:
            face = ku[i]
            terms = [terms[f] + face * buf[p, i - 1, f] for f in range(2)]
        return ((ch[i] * heat + EXCHANGE * tracer) + terms[0],
                (ct[i] * tracer + EXCHANGE * heat) + TRACER_DIFF * terms[1])

    relay(0)
    for level in range(1, SUB // 2):
        p = (level - 1) % 2
        for row in range(level, SUB - level):
            heat, tracer = advance(wb, p, SUB + row)
            for f, x in enumerate((heat, tracer)):
                wb[1 - p, SUB + row, f] = x
                ub[1 - p, SUB + row, f] = x

    def pass_on(d):
        for side in range(2):
            @pl.when(gets[side] & mine(d))
            def _():
                k_copy(side, d).wait_recv()
                for o in range(1, group):
                    k_forward(side, d, o).start()

    outside = (jnp.where(has_up, 1.0, 0.0), jnp.where(has_down, 1.0, 0.0))

    def faces_at(d):
        for side in range(2):
            pl.when(gets[side] & jnp.logical_not(mine(d)))(lambda: k_copy(side, d).wait_recv())
            k = kh[side, d - 1]
            inner = kh[side, d - 2] if d > 1 else kown[0 if side == 0 else SUB - 1]
            face = 0.5 * (k + inner)
            edge = face * outside[side] if d == 1 else face
            i = SUB - d if side == 0 else 2 * SUB - 1 + d
            columns_of(i, k)
            if side == 0:
                ku[i + 1] = face
                kd[i] = edge
                centre_of(i + 1)
            else:
                kd[i - 1] = face
                ku[i] = edge
                centre_of(i - 1)

    pass_on(1)
    for level in range(1, FINE):
        pass_on(level + 1)
        faces_at(level)
        if level in (2, 4):
            relay(level // 2)
        if level == 4:
            for o in range(1, nr):
                er_copy(o).start()
        p = (level - 1) % 2
        first, last = SUB + 1 - level, 2 * SUB - 2 + level
        for i in range(first, last + 1):
            if SUB + level <= i < 2 * SUB - level:
                continue
            heat, tracer = advance(wb, p, i)
            wb[1 - p, i, 0] = heat
            wb[1 - p, i, 1] = tracer
        for i, inner, face in ((first - 1, first, kd), (last + 1, last, ku)):
            for f in range(2):
                wb[1 - p, i, f] = (1.0, TRACER_DIFF)[f] * face[i] * wb[p, inner, f]

    p = (FINE - 1) % 2
    fluxes = [[jnp.sum(ku[SUB] * (wb[p, SUB - 1, f] - wb[p, SUB, f]), axis=0) for f in range(2)],
              [jnp.sum(kd[2 * SUB - 1] * (wb[p, 2 * SUB, f] - wb[p, 2 * SUB - 1, f]), axis=0) for f in range(2)]]
    for b in range(3):
        whole, gain = [], []
        for f in range(2):
            total, side_flux = None, None
            for i in range(max(1, SUB * b), min(3 * SUB - 1, SUB * (b + 1))):
                x = wb[p, i, f]
                flux = kr[i, COARSEN - 1] * (following(x[0]) - x[COARSEN - 1])
                total = x if total is None else total + x
                side_flux = flux if side_flux is None else side_flux + flux
            change = side_flux - preceding(side_flux)
            if b == 0:
                change = change - fluxes[0][f]
            elif b == 1:
                change = change + (fluxes[0][f] + fluxes[1][f])
            else:
                change = change - fluxes[1][f]
            whole.append(jnp.sum(total, axis=0))
            gain.append((1.0, TRACER_DIFF)[f] * change)
        moved = EXCHANGE * (whole[1] - whole[0])
        cts[b, 0] = AREA * ((whole[0] + moved) + gain[0])
        cts[b, 1] = AREA * ((whole[1] - moved) + gain[1])
    for o in range(1, nr):
        ct_copy(o).start()
    ctg[r] = cts[...]
    send_rows(EARLY + 1, FINE)

    faces_at(FINE)

    def row_pair(level, diagonal):
        p = lax.rem(level + 1, 2)
        new = [(i,) + advance(ub, p, i) for i in (SUB + level - diagonal, 2 * SUB - 1 - level + diagonal)]
        for i, heat, tracer in new:
            ub[1 - p, i, 0] = heat
            ub[1 - p, i, 1] = tracer

    def run_diagonal(diagonal):
        for side in range(2):
            pl.when(gets[side])(lambda: v_copy(side, diagonal).wait_recv())

        def step(level, carry):
            row_pair(level, diagonal)
            return carry
        lax.fori_loop(1, min(FINE, SUB // 2 - 1 + diagonal) + 1, step, 0)

    ratio = (FINE / COARSE) / float(COARSEN * COARSEN)
    rate = EXCHANGE * (FINE / COARSE)

    run_diagonal(1)
    run_diagonal(2)

    for o in range(1, nr):
        er_copy(o).wait_recv()
    kcv = [erg[i, 0] for i in range(nr)]
    c_right = [ratio * 0.5 * (k + following(k)) for k in kcv]
    c_left = [ratio * 0.5 * (k + preceding(k)) for k in kcv]
    c_face = [ratio * 0.5 * kcv[0]]
    c_face += [ratio * 0.5 * (kcv[i] + kcv[i + 1]) for i in range(nr - 1)]
    c_face += [ratio * 0.5 * kcv[nr - 1]]
    totals = [(c_right[i] + c_left[i]) + (c_face[i] + c_face[i + 1]) for i in range(nr)]
    c_centre = [[(1.0 - rate) - x for x in totals], [(1.0 - rate) - TRACER_DIFF * x for x in totals]]

    def coarse_prop(state):
        for substep in range(COARSE):
            new = []
            for f in range(2):
                rows = state[f * nr:(f + 1) * nr]
                other = state[(1 - f) * nr:(2 - f) * nr]
                for i in range(nr):
                    v = rows[i]
                    around = c_right[i] * following(v) + c_left[i] * preceding(v)
                    if i > 0:
                        around = around + c_face[i] * rows[i - 1]
                    if i < nr - 1:
                        around = around + c_face[i + 1] * rows[i + 1]
                    if f == 1:
                        around = TRACER_DIFF * around
                    new.append((c_centre[f][i] * v + rate * other[i]) + around)
            state = tuple(new)
        return state

    later = jnp.where(t > 0, 1.0, 0.0)
    old = coarse_prop(tuple(later * erg[i, 1 + f] for f in range(2) for i in range(nr)))

    for o in range(1, nr):
        ct_copy(o).wait_recv()
    change = []
    for f in range(2):
        for i in range(nr):
            x = ctg[i, 1, f]
            if i > 0:
                x = x + ctg[i - 1, 2, f]
            if i < nr - 1:
                x = x + ctg[i + 1, 0, f]
            x = x - old[f * nr + i]
            jall[t, i, f] = x
            change.append(x)
    pl.when(t < nt - 1)(lambda: pl.semaphore_wait(tok_tm, nt - 1 - t))
    for o in range(1, nt):
        pl.when(t + o < nt)(lambda: j_copy(o).start())

    for d in range(3, FINE):
        run_diagonal(d)

    def place(level, side):
        return level if side == 0 else 3 * SUB - 1 - level

    for level in range(1, FINE + 1):
        for side in range(2):
            heat, tracer = advance(ub, (level - 1) % 2, place(level, side), above=side == 1, below=side == 0)
            part[level - 1, side, 0] = heat
            part[level - 1, side, 1] = tracer

    def link(n, state):
        pltpu.make_async_remote_copy(
            jall.at[n], jall.at[n], jsend.at[0], jrecv.at[n],
            device_id=(n, r), device_id_type=MESH).wait_recv()
        state = coarse_prop(state)
        return tuple(state[f * nr + i] + jall[n, i, f] for f in range(2) for i in range(nr))

    state = tuple(jnp.zeros((SUB, LANES), f32) for _ in range(2 * nr))
    state = lax.fori_loop(0, t, link, state)
    state = coarse_prop(state)

    fix = [None, None]
    for f in range(2):
        for i in range(nr):
            value = state[f * nr + i] - old[f * nr + i]
            fix[f] = value if i == 0 else jnp.where(r == i, value, fix[f])
    natural = exact_dot(jnp.concatenate([state[n] + change[n] for n in range(2 * nr)], axis=0), order[...])
    for f in range(2):
        for i in range(nr):
            n = f * nr + i
            nxt_ref[f, pl.ds(i, SUB, stride=nr), :] = lines_to_lanes(natural[n * SUB:(n + 1) * SUB])

    def write_row(row, f, end):
        end = exchange_lanes([end[m] + fix[f] for m in range(COARSEN)])
        for m in range(SUB):
            out_ref[f, row, m * SUB:(m + 1) * SUB, :] = end[m]

    for row in range(1, SUB - 1):
        for f in range(2):
            write_row(row, f, ub[0, SUB + row, f])

    last = []
    for side in range(2):
        pl.when(gets[side])(lambda: v_copy(side, FINE).wait_recv())
    for side in range(2):
        i = place(0, side)
        last.append([ub[0, i, 0], ub[0, i, 1]])
    for level in range(1, FINE + 1):
        for side in range(2):
            face = (ku, kd)[side][place(level, side)]
            heat, tracer = last[side]
            last[side] = [part[level - 1, side, 0] + face * heat,
                          part[level - 1, side, 1] + (TRACER_DIFF * face) * tracer]
    for side in range(2):
        for f in range(2):
            write_row((0, SUB - 1)[side], f, last[side][f])

    for d in range(1, FINE + 1):
        for side in range(2):
            pl.when(sends[side])(lambda: v_copy(side, d).wait_send())
            pl.when(sends[side] & mine(d))(lambda: k_copy(side, d).wait_send())

            @pl.when(gets[side] & mine(d))
            def _():
                for o in range(1, group):
                    k_forward(side, d, o).wait_send()
    for o in range(1, nr):
        er_copy(o).wait_send()
        ct_copy(o).wait_send()
    for o in range(1, nt):
        pl.when(t + o < nt)(lambda: j_copy(o).wait_send())


def deliver(ends, following, ends_out, following_out, sem):
    fields, rows = ends.shape[:2]
    copies = [pltpu.make_async_copy(ends.at[f, row], ends_out.at[f, :, row, :], sem.at[f * rows + row])
              for row in range(rows) for f in range(fields)]
    copies.append(pltpu.make_async_copy(following, following_out, sem.at[fields * rows]))
    for copy in copies:
        copy.start()
    for copy in copies:
        copy.wait()


def body(nt, nr, starts, conductivity):
    rows, columns = conductivity.shape
    assert rows == SUB == COARSEN == FINE
    assert columns == COARSEN * SUB * LANES
    blocks = columns // LANES
    group = math.gcd(SHARE, nt)
    slab = starts[0].reshape(2, rows, blocks, LANES).transpose(0, 2, 1, 3).reshape(2, blocks * rows, LANES)
    kappa = conductivity.reshape(rows, blocks, LANES).transpose(1, 0, 2).reshape(blocks * rows, LANES)
    slab = pltpu.with_memory_space_constraint(slab, pltpu.HBM)
    kappa = pltpu.with_memory_space_constraint(kappa, pltpu.HBM)
    f32 = jnp.float32
    dma = pltpu.SemaphoreType.DMA
    cell = (SUB, LANES)
    line = (COARSEN,) + cell
    ends, following = pl.pallas_call(
        functools.partial(kernel, nt, nr, group),
        out_shape=(
            jax.ShapeDtypeStruct((2, rows, blocks, LANES), f32),
            jax.ShapeDtypeStruct((2, SUB * nr, LANES), f32),
        ),
        in_specs=[pl.BlockSpec(memory_space=pltpu.HBM)] * 2,
        out_specs=[pl.BlockSpec(memory_space=pltpu.VMEM)] * 2,
        scratch_shapes=[
            pltpu.VMEM((2, blocks * rows, LANES), f32),
            pltpu.VMEM((blocks * rows, LANES), f32),
            dma((2,)),
            pltpu.VMEM((2, 3 * SUB, 2) + line, f32),
            pltpu.VMEM((2, 3 * SUB, 2) + line, f32),
            pltpu.VMEM((SUB, 2) + line, f32),
            pltpu.VMEM((SUB,) + line, f32),
            pltpu.VMEM((2, FINE) + line, f32),
            pltpu.VMEM((3 * SUB,) + line, f32),
            pltpu.VMEM((3 * SUB,) + cell, f32),
            pltpu.VMEM((3 * SUB,) + line, f32),
            pltpu.VMEM((3 * SUB,) + line, f32),
            pltpu.VMEM((3 * SUB,) + line, f32),
            pltpu.VMEM((3 * SUB,) + line, f32),
            pltpu.VMEM((FINE, 2, 2) + line, f32),
            pltpu.VMEM((LANES, LANES), jnp.bfloat16),
            pltpu.VMEM((3,) + cell, f32),
            pltpu.VMEM((nr, 3) + cell, f32),
            pltpu.VMEM((3, 2) + cell, f32),
            pltpu.VMEM((nr, 3, 2) + cell, f32),
            pltpu.VMEM((nt, nr, 2) + cell, f32),
            dma((2, FINE)), dma((2, FINE)),
            dma((2, FINE)), dma((2, FINE)), dma((2, FINE, group)),
            dma((nr,)), dma((nr,)),
            dma((nr,)), dma((nr,)),
            dma((nt,)), dma((nt,)),
            pltpu.SemaphoreType.REGULAR, pltpu.SemaphoreType.REGULAR, pltpu.SemaphoreType.REGULAR,
        ],
        compiler_params=pltpu.CompilerParams(
            collective_id=0, has_side_effects=True, vmem_limit_bytes=48 * 1024 * 1024),
        name="parareal",
    )(slab, kappa)
    ends, following = pl.pallas_call(
        deliver,
        out_shape=(
            jax.ShapeDtypeStruct((2, blocks, rows, LANES), f32),
            jax.ShapeDtypeStruct(following.shape, f32),
        ),
        in_specs=[pl.BlockSpec(memory_space=pltpu.VMEM)] * 2,
        out_specs=[pl.BlockSpec(memory_space=pltpu.HBM)] * 2,
        scratch_shapes=[dma((2 * rows + 1,))],
        compiler_params=pltpu.CompilerParams(vmem_limit_bytes=1024 * 1024),
        name="deliver",
    )(ends, following)
    new_ends = ends.transpose(0, 2, 1, 3).reshape(2, rows, columns)
    coarse_next = following.reshape(2, SUB, nr, LANES).transpose(0, 2, 1, 3).reshape(2, nr, SUB * LANES)
    return new_ends[None], coarse_next[None]


def solution(mesh):
    nt, nr = mesh.shape["tm"], mesh.shape["rows"]
    in_specs = (P("tm", None, "rows", None), P("rows", None))
    out_specs = (P("tm", None, "rows", None), P("tm", None, None, None))
    return jax.shard_map(functools.partial(body, nt, nr), mesh=mesh, in_specs=in_specs, out_specs=out_specs, check_vma=False)
```

```python
import functools
import math

import jax
import jax.numpy as jnp
from jax import lax
from jax.experimental import pallas as pl
from jax.experimental.pallas import tpu as pltpu
from jax.sharding import PartitionSpec as P

FINE = 8
COARSE = 2
COARSEN = 8
EXCHANGE = 0.05
TRACER_DIFF = 0.5

SUB = 8
LANES = 128
MESH = pl.DeviceIdType.MESH
SHARE = 2
EARLY = 4
SLOTS = 3
AREA = 1.0 / (COARSEN * COARSEN)


def cell_index(axis):
    return lax.broadcasted_iota(jnp.int32, (SUB, LANES), axis)


def following(v):
    lane = cell_index(1)
    near = pltpu.roll(v, LANES - SUB, 1)
    far = jnp.where(lane < LANES - 1, pltpu.roll(v, LANES - SUB - 1, 1), pltpu.roll(v, LANES - 1, 1))
    edge = pltpu.roll(jnp.where(cell_index(0) == 0, far, near), SUB - 1, 0)
    return jnp.where(lane < LANES - SUB, near, edge)


def preceding(v):
    lane = cell_index(1)
    near = pltpu.roll(v, SUB, 1)
    far = jnp.where(lane >= 1, pltpu.roll(v, SUB + 1, 1), pltpu.roll(v, 1, 1))
    edge = pltpu.roll(jnp.where(cell_index(0) == SUB - 1, far, near), 1, 0)
    return jnp.where(lane >= SUB, near, edge)


def lines_to_lanes(v):
    lane, line = cell_index(1), cell_index(0)
    for step in (1, 2, 4):
        high_lane, high_line = (lane & (step * 16)) != 0, (line & step) != 0
        up = pltpu.roll(pltpu.roll(v, SUB - step, 0), step * 16, 1)
        down = pltpu.roll(pltpu.roll(v, step, 0), LANES - step * 16, 1)
        v = jnp.where(high_lane, jnp.where(high_line, v, up), jnp.where(high_line, down, v))
    return v


def to_right(v):
    return jnp.concatenate([v[1:], following(v[0])[None]], axis=0)


def to_left(v):
    return jnp.concatenate([preceding(v[COARSEN - 1])[None], v[:COARSEN - 1]], axis=0)


def exchange_lanes(rows):
    lane = cell_index(1)
    rows = list(rows)
    for step in (1, 2, 4):
        high = (lane & step) != 0
        for i in range(SUB):
            if not i & step:
                a, b = rows[i], rows[i | step]
                rows[i] = jnp.where(high, pltpu.roll(b, step, 1), a)
                rows[i | step] = jnp.where(high, b, pltpu.roll(a, LANES - step, 1))
    return rows


def exact_dot(x, w):
    rows = x.shape[0]
    hi = x.astype(jnp.bfloat16)
    rest = x - hi.astype(jnp.float32)
    mid = rest.astype(jnp.bfloat16)
    low = (rest - mid.astype(jnp.float32)).astype(jnp.bfloat16)
    y = jnp.dot(jnp.concatenate([hi.astype(jnp.float32), mid.astype(jnp.float32), low.astype(jnp.float32)], axis=0).astype(jnp.bfloat16), w,
                preferred_element_type=jnp.float32)
    return y[:rows] + y[rows:2 * rows] + y[2 * rows:]


def kernel(nt, nr, group, s_hbm, k_hbm, out_ref, nxt_ref,
           s_ref, k_ref, in_sem, wb, ub, own, kown, kh, kr, kl, kd, ku, ch, ct, part, order, ers, erg, cts, ctg, jall,
           vsend, vrecv, ksend, krecv, kfwd, ersend, errecv, ctsend, ctrecv, jsend, jrecv, tok_down, tok_up, tok_tm):
    t = lax.axis_index("tm")
    r = lax.axis_index("rows")
    member = lax.rem(t, group)
    base = t - member
    has_up = r > 0
    has_down = r < nr - 1
    sends = (has_down, has_up)
    gets = (has_up, has_down)
    f32 = jnp.float32

    outer_first = [row for d in range(SUB // 2) for row in (SUB - 1 - d, d)]

    k_in = pltpu.make_async_copy(k_hbm, k_ref, in_sem.at[0])
    s_in = pltpu.make_async_copy(s_hbm, s_ref, in_sem.at[1])
    k_in.start()
    s_in.start()

    barrier = pltpu.get_barrier_semaphore()

    def greet(tm, row):
        pl.semaphore_signal(barrier, inc=1, device_id=(tm, row), device_id_type=MESH)

    pl.when(has_up)(lambda: greet(t, r - 1))
    pl.when(has_down)(lambda: greet(t, r + 1))
    for o in range(1, nt):
        pl.when(t + o < nt)(lambda: greet(t + o, r))
    for o in range(1, group):
        pl.when(member >= o)(lambda: greet(t - o, r))

    source = lax.broadcasted_iota(jnp.int32, order.shape, 0)
    target = lax.broadcasted_iota(jnp.int32, order.shape, 1)
    goes = (source & (SUB - 1)) * (LANES // SUB) + (source >> 3)
    order[...] = jnp.where(goes == target, 1.0, 0.0).astype(jnp.bfloat16)
    for d in range(1, FINE):
        zero = jnp.zeros(wb.shape[2:], f32)
        wb[(d - 1) % 2, SUB - d] = zero
        wb[(d - 1) % 2, 2 * SUB - 1 + d] = zero

    @pl.when(jnp.logical_not(has_up))
    def _():
        ub[0, 0:SUB] = jnp.zeros((SUB,) + ub.shape[2:], f32)
        kh[0] = jnp.zeros(kh.shape[1:], f32)

    @pl.when(jnp.logical_not(has_down))
    def _():
        ub[0, 2 * SUB:] = jnp.zeros((SUB,) + ub.shape[2:], f32)
        kh[1] = jnp.zeros(kh.shape[1:], f32)

    def read_row(ref, row):
        return jnp.stack(exchange_lanes(
            [ref[pl.ds(m * SUB * SUB + row, SUB, stride=SUB), :] for m in range(SUB)]), axis=0)

    k_in.wait()
    total = None
    for row in outer_first:
        x = read_row(k_ref, row)
        kown[row] = x
        total = x if total is None else total + x
    ers[0] = jnp.sum(total, axis=0) * AREA

    pl.semaphore_wait(barrier, t + (group - 1 - member) + has_up.astype(jnp.int32) + has_down.astype(jnp.int32))

    def tell(tok, row):
        pl.semaphore_signal(tok, inc=1, device_id=(t, row), device_id_type=MESH)

    pl.when(jnp.logical_not(has_up) & has_down)(lambda: tell(tok_down, r + 1))
    pl.when(jnp.logical_not(has_down) & has_up)(lambda: tell(tok_up, r - 1))

    for o in range(1, nt):
        @pl.when(t >= o)
        def _():
            pl.semaphore_signal(tok_tm, inc=1, device_id=(t - o, r), device_id_type=MESH)

    def relay(slot):
        @pl.when(has_up & (jnp.minimum(r - 1, SLOTS - 1) == slot))
        def _():
            pl.semaphore_wait(tok_down, 1)
            pl.when(has_down)(lambda: tell(tok_down, r + 1))

        @pl.when(has_down & (jnp.minimum(nr - 2 - r, SLOTS - 1) == slot))
        def _():
            pl.semaphore_wait(tok_up, 1)
            pl.when(has_up)(lambda: tell(tok_up, r - 1))

    def v_copy(side, d):
        if side == 0:
            return pltpu.make_async_remote_copy(
                own.at[SUB - d], ub.at[0, SUB - d], vsend.at[side], vrecv.at[side, d - 1],
                device_id=(t, r + 1), device_id_type=MESH)
        return pltpu.make_async_remote_copy(
            own.at[d - 1], ub.at[0, 2 * SUB - 1 + d], vsend.at[side], vrecv.at[side, d - 1],
            device_id=(t, r - 1), device_id_type=MESH)

    def k_copy(side, d):
        return pltpu.make_async_remote_copy(
            kown.at[SUB - d if side == 0 else d - 1], kh.at[side, d - 1], ksend.at[side], krecv.at[side, d - 1],
            device_id=(t, r + 1 if side == 0 else r - 1), device_id_type=MESH)

    def k_forward(side, d, o):
        return pltpu.make_async_remote_copy(
            kh.at[side, d - 1], kh.at[side, d - 1], kfwd.at[side], krecv.at[side, d - 1],
            device_id=(base + lax.rem(member + o, group), r), device_id_type=MESH)

    def mine(d):
        return member == (d - 1) % group

    def er_copy(o):
        return pltpu.make_async_remote_copy(
            ers, erg.at[r], ersend, errecv.at[o],
            device_id=(t, lax.rem(r + o, nr)), device_id_type=MESH)

    def ct_copy(o):
        return pltpu.make_async_remote_copy(
            cts, ctg.at[r], ctsend, ctrecv.at[o],
            device_id=(t, lax.rem(r + o, nr)), device_id_type=MESH)

    def j_copy(o):
        return pltpu.make_async_remote_copy(
            jall.at[t], jall.at[t], jsend.at[o], jrecv.at[t],
            device_id=(t + o, r), device_id_type=MESH)

    for d in range(1, FINE + 1):
        for side in range(2):
            pl.when(sends[side] & mine(d))(lambda: k_copy(side, d).start())

    s_in.wait()
    sums = [None, None]
    for row in outer_first:
        for f in range(2):
            x = read_row(s_ref.at[f], row)
            own[row, f] = x
            wb[0, SUB + row, f] = x
            ub[0, SUB + row, f] = x
            sums[f] = x if sums[f] is None else sums[f] + x
    for f in range(2):
        ers[1 + f] = jnp.sum(sums[f], axis=0) * AREA
    erg[r] = ers[...]

    def send_rows(first, last):
        for d in range(first, last + 1):
            for side in range(2):
                pl.when(sends[side])(lambda: v_copy(side, d).start())

    def columns_of(i, k):
        right = 0.5 * (k + to_right(k))
        kr[i] = right
        kl[i] = preceding(right[COARSEN - 1])

    def left_of(i):
        return jnp.concatenate([kl[i][None], kr[i, 0:COARSEN - 1]], axis=0)

    def centre_of(i):
        total = (kr[i] + left_of(i)) + (ku[i] + kd[i])
        ch[i] = (1.0 - EXCHANGE) - total
        ct[i] = (1.0 - EXCHANGE) - TRACER_DIFF * total

    for row in range(SUB):
        k = kown[row]
        columns_of(SUB + row, k)
        if row < SUB - 1:
            face = 0.5 * (k + kown[row + 1])
            kd[SUB + row] = face
            ku[SUB + row + 1] = face
        if 0 < row < SUB - 1:
            centre_of(SUB + row)

    def advance(buf, p, i, above=True, below=True):
        heat, tracer = buf[p, i, 0], buf[p, i, 1]
        right, left = kr[i], left_of(i)
        terms = [right * to_right(heat) + left * to_left(heat), right * to_right(tracer) + left * to_left(tracer)]
        if below:
            face = kd[i]
            terms = [terms[f] + face * buf[p, i + 1, f] for f in range(2)]
        if above:
            face = ku[i]
            terms = [terms[f] + face * buf[p, i - 1, f] for f in range(2)]
        return ((ch[i] * heat + EXCHANGE * tracer) + terms[0],
                (ct[i] * tracer + EXCHANGE * heat) + TRACER_DIFF * terms[1])

    relay(0)
    for level in range(1, SUB // 2):
        p = (level - 1) % 2
        for row in range(level, SUB - level):
            heat, tracer = advance(wb, p, SUB + row)
            for f, x in enumerate((heat, tracer)):
                wb[1 - p, SUB + row, f] = x
                ub[1 - p, SUB + row, f] = x

    def pass_on(d):
        for side in range(2):
            @pl.when(gets[side] & mine(d))
            def _():
                k_copy(side, d).wait_recv()
                for o in range(1, group):
                    k_forward(side, d, o).start()

    outside = (jnp.where(has_up, 1.0, 0.0), jnp.where(has_down, 1.0, 0.0))

    def faces_at(d):
        for side in range(2):
            pl.when(gets[side] & jnp.logical_not(mine(d)))(lambda: k_copy(side, d).wait_recv())
            k = kh[side, d - 1]
            inner = kh[side, d - 2] if d > 1 else kown[0 if side == 0 else SUB - 1]
            face = 0.5 * (k + inner)
            edge = face * outside[side] if d == 1 else face
            i = SUB - d if side == 0 else 2 * SUB - 1 + d
            columns_of(i, k)
            if side == 0:
                ku[i + 1] = face
                kd[i] = edge
                centre_of(i + 1)
            else:
                kd[i - 1] = face
                ku[i] = edge
                centre_of(i - 1)

    pass_on(1)
    for level in range(1, FINE):
        pass_on(level + 1)
        faces_at(level)
        if level == 1:
            send_rows(1, EARLY)
        if level in (2, 4):
            relay(level // 2)
        if level == 4:
            for o in range(1, nr):
                er_copy(o).start()
        p = (level - 1) % 2
        first, last = SUB + 1 - level, 2 * SUB - 2 + level
        for i in range(first, last + 1):
            if SUB + level <= i < 2 * SUB - level:
                continue
            heat, tracer = advance(wb, p, i)
            wb[1 - p, i, 0] = heat
            wb[1 - p, i, 1] = tracer
        for i, inner, face in ((first - 1, first, kd), (last + 1, last, ku)):
            for f in range(2):
                wb[1 - p, i, f] = (1.0, TRACER_DIFF)[f] * face[i] * wb[p, inner, f]

    p = (FINE - 1) % 2
    fluxes = [[jnp.sum(ku[SUB] * (wb[p, SUB - 1, f] - wb[p, SUB, f]), axis=0) for f in range(2)],
              [jnp.sum(kd[2 * SUB - 1] * (wb[p, 2 * SUB, f] - wb[p, 2 * SUB - 1, f]), axis=0) for f in range(2)]]
    for b in range(3):
        whole, gain = [], []
        for f in range(2):
            total, side_flux = None, None
            for i in range(max(1, SUB * b), min(3 * SUB - 1, SUB * (b + 1))):
                x = wb[p, i, f]
                flux = kr[i, COARSEN - 1] * (following(x[0]) - x[COARSEN - 1])
                total = x if total is None else total + x
                side_flux = flux if side_flux is None else side_flux + flux
            change = side_flux - preceding(side_flux)
            if b == 0:
                change = change - fluxes[0][f]
            elif b == 1:
                change = change + (fluxes[0][f] + fluxes[1][f])
            else:
                change = change - fluxes[1][f]
            whole.append(jnp.sum(total, axis=0))
            gain.append((1.0, TRACER_DIFF)[f] * change)
        moved = EXCHANGE * (whole[1] - whole[0])
        cts[b, 0] = AREA * ((whole[0] + moved) + gain[0])
        cts[b, 1] = AREA * ((whole[1] - moved) + gain[1])
    for o in range(1, nr):
        ct_copy(o).start()
    ctg[r] = cts[...]
    faces_at(FINE)

    def row_pair(level, diagonal):
        p = lax.rem(level + 1, 2)
        new = [(i,) + advance(ub, p, i) for i in (SUB + level - diagonal, 2 * SUB - 1 - level + diagonal)]
        for i, heat, tracer in new:
            ub[1 - p, i, 0] = heat
            ub[1 - p, i, 1] = tracer

    def run_diagonal(diagonal):
        for side in range(2):
            pl.when(gets[side])(lambda: v_copy(side, diagonal).wait_recv())
        if diagonal != 3:
            send_rows(diagonal + EARLY, min(diagonal + EARLY, FINE))

        def step(level, carry):
            row_pair(level, diagonal)
            return carry
        lax.fori_loop(1, min(FINE, SUB // 2 - 1 + diagonal) + 1, step, 0)

    ratio = (FINE / COARSE) / float(COARSEN * COARSEN)
    rate = EXCHANGE * (FINE / COARSE)

    run_diagonal(1)
    run_diagonal(2)
    send_rows(EARLY + 3, EARLY + 3)

    for o in range(1, nr):
        er_copy(o).wait_recv()
    kcv = [erg[i, 0] for i in range(nr)]
    c_right = [ratio * 0.5 * (k + following(k)) for k in kcv]
    c_left = [ratio * 0.5 * (k + preceding(k)) for k in kcv]
    c_face = [ratio * 0.5 * kcv[0]]
    c_face += [ratio * 0.5 * (kcv[i] + kcv[i + 1]) for i in range(nr - 1)]
    c_face += [ratio * 0.5 * kcv[nr - 1]]
    totals = [(c_right[i] + c_left[i]) + (c_face[i] + c_face[i + 1]) for i in range(nr)]
    c_centre = [[(1.0 - rate) - x for x in totals], [(1.0 - rate) - TRACER_DIFF * x for x in totals]]

    def coarse_prop(state):
        for substep in range(COARSE):
            new = []
            for f in range(2):
                rows = state[f * nr:(f + 1) * nr]
                other = state[(1 - f) * nr:(2 - f) * nr]
                for i in range(nr):
                    v = rows[i]
                    around = c_right[i] * following(v) + c_left[i] * preceding(v)
                    if i > 0:
                        around = around + c_face[i] * rows[i - 1]
                    if i < nr - 1:
                        around = around + c_face[i + 1] * rows[i + 1]
                    if f == 1:
                        around = TRACER_DIFF * around
                    new.append((c_centre[f][i] * v + rate * other[i]) + around)
            state = tuple(new)
        return state

    later = jnp.where(t > 0, 1.0, 0.0)
    old = coarse_prop(tuple(later * erg[i, 1 + f] for f in range(2) for i in range(nr)))

    for o in range(1, nr):
        ct_copy(o).wait_recv()
    change = []
    for f in range(2):
        for i in range(nr):
            x = ctg[i, 1, f]
            if i > 0:
                x = x + ctg[i - 1, 2, f]
            if i < nr - 1:
                x = x + ctg[i + 1, 0, f]
            x = x - old[f * nr + i]
            jall[t, i, f] = x
            change.append(x)
    pl.when(t < nt - 1)(lambda: pl.semaphore_wait(tok_tm, nt - 1 - t))
    for o in range(1, nt):
        pl.when(t + o < nt)(lambda: j_copy(o).start())

    for d in range(3, FINE):
        run_diagonal(d)

    def place(level, side):
        return level if side == 0 else 3 * SUB - 1 - level

    for level in range(1, FINE + 1):
        for side in range(2):
            heat, tracer = advance(ub, (level - 1) % 2, place(level, side), above=side == 1, below=side == 0)
            part[level - 1, side, 0] = heat
            part[level - 1, side, 1] = tracer

    share = FINE // group
    for side in range(2):
        @pl.when(sends[side])
        def _():
            pltpu.make_async_remote_copy(
                kown.at[pl.ds(0, share)], kh.at[side, pl.ds(0, share)], ksend.at[side], krecv.at[side, 0],
                device_id=(t, r + 1 if side == 0 else r - 1), device_id_type=MESH).wait_send()

        if group > 1:
            @pl.when(gets[side])
            def _():
                passed = kh.at[side, pl.ds(0, share * (group - 1))]
                pltpu.make_async_remote_copy(
                    passed, passed, kfwd.at[side], krecv.at[side, 0],
                    device_id=(base + lax.rem(member + 1, group), r), device_id_type=MESH).wait_send()
    if nr > 1:
        for ref, send, recv in ((erg, ersend, errecv), (ctg, ctsend, ctrecv)):
            spread = ref.at[pl.ds(0, nr - 1)]
            pltpu.make_async_remote_copy(
                spread, spread, send, recv.at[0],
                device_id=(t, lax.rem(r + 1, nr)), device_id_type=MESH).wait_send()
    for o in range(1, nt):
        pl.when(t + o < nt)(lambda: j_copy(o).wait_send())

    def link(n, state):
        pltpu.make_async_remote_copy(
            jall.at[n], jall.at[n], jsend.at[0], jrecv.at[n],
            device_id=(n, r), device_id_type=MESH).wait_recv()
        state = coarse_prop(state)
        return tuple(state[f * nr + i] + jall[n, i, f] for f in range(2) for i in range(nr))

    state = tuple(jnp.zeros((SUB, LANES), f32) for _ in range(2 * nr))
    state = lax.fori_loop(0, t, link, state)
    state = coarse_prop(state)

    fix = [None, None]
    for f in range(2):
        for i in range(nr):
            value = state[f * nr + i] - old[f * nr + i]
            fix[f] = value if i == 0 else jnp.where(r == i, value, fix[f])
    natural = exact_dot(jnp.concatenate([state[n] + change[n] for n in range(2 * nr)], axis=0), order[...])
    for f in range(2):
        for i in range(nr):
            n = f * nr + i
            nxt_ref[f, pl.ds(i, SUB, stride=nr), :] = lines_to_lanes(natural[n * SUB:(n + 1) * SUB])

    def write_row(row, f, end):
        end = exchange_lanes([end[m] + fix[f] for m in range(COARSEN)])
        for m in range(SUB):
            out_ref[f, row, m * SUB:(m + 1) * SUB, :] = end[m]

    for row in range(1, SUB - 1):
        for f in range(2):
            write_row(row, f, ub[0, SUB + row, f])

    last = []
    for side in range(2):
        pl.when(gets[side])(lambda: v_copy(side, FINE).wait_recv())
    for side in range(2):
        i = place(0, side)
        last.append([ub[0, i, 0], ub[0, i, 1]])
    for level in range(1, FINE + 1):
        for side in range(2):
            face = (ku, kd)[side][place(level, side)]
            heat, tracer = last[side]
            last[side] = [part[level - 1, side, 0] + face * heat,
                          part[level - 1, side, 1] + (TRACER_DIFF * face) * tracer]
    for side in range(2):
        for f in range(2):
            write_row((0, SUB - 1)[side], f, last[side][f])

    for side in range(2):
        @pl.when(sends[side])
        def _():
            pltpu.make_async_remote_copy(
                own, ub.at[0, pl.ds(0, SUB)], vsend.at[side], vrecv.at[side, 0],
                device_id=(t, r + 1 if side == 0 else r - 1), device_id_type=MESH).wait_send()


def deliver(ends, following, ends_out, following_out, sem):
    fields, rows = ends.shape[:2]
    copies = [pltpu.make_async_copy(ends.at[f, row], ends_out.at[f, :, row, :], sem.at[f * rows + row])
              for row in range(rows) for f in range(fields)]
    copies.append(pltpu.make_async_copy(following, following_out, sem.at[fields * rows]))
    for copy in copies:
        copy.start()
    for copy in copies:
        copy.wait()


def body(nt, nr, starts, conductivity):
    rows, columns = conductivity.shape
    assert rows == SUB == COARSEN == FINE
    assert columns == COARSEN * SUB * LANES
    blocks = columns // LANES
    group = math.gcd(SHARE, nt)
    slab = starts[0].reshape(2, rows, blocks, LANES).transpose(0, 2, 1, 3).reshape(2, blocks * rows, LANES)
    kappa = conductivity.reshape(rows, blocks, LANES).transpose(1, 0, 2).reshape(blocks * rows, LANES)
    slab = pltpu.with_memory_space_constraint(slab, pltpu.HBM)
    kappa = pltpu.with_memory_space_constraint(kappa, pltpu.HBM)
    f32 = jnp.float32
    dma = pltpu.SemaphoreType.DMA
    cell = (SUB, LANES)
    line = (COARSEN,) + cell
    ends, following = pl.pallas_call(
        functools.partial(kernel, nt, nr, group),
        out_shape=(
            jax.ShapeDtypeStruct((2, rows, blocks, LANES), f32),
            jax.ShapeDtypeStruct((2, SUB * nr, LANES), f32),
        ),
        in_specs=[pl.BlockSpec(memory_space=pltpu.HBM)] * 2,
        out_specs=[pl.BlockSpec(memory_space=pltpu.VMEM)] * 2,
        scratch_shapes=[
            pltpu.VMEM((2, blocks * rows, LANES), f32),
            pltpu.VMEM((blocks * rows, LANES), f32),
            dma((2,)),
            pltpu.VMEM((2, 3 * SUB, 2) + line, f32),
            pltpu.VMEM((2, 3 * SUB, 2) + line, f32),
            pltpu.VMEM((SUB, 2) + line, f32),
            pltpu.VMEM((SUB,) + line, f32),
            pltpu.VMEM((2, FINE) + line, f32),
            pltpu.VMEM((3 * SUB,) + line, f32),
            pltpu.VMEM((3 * SUB,) + cell, f32),
            pltpu.VMEM((3 * SUB,) + line, f32),
            pltpu.VMEM((3 * SUB,) + line, f32),
            pltpu.VMEM((3 * SUB,) + line, f32),
            pltpu.VMEM((3 * SUB,) + line, f32),
            pltpu.VMEM((FINE, 2, 2) + line, f32),
            pltpu.VMEM((LANES, LANES), jnp.bfloat16),
            pltpu.VMEM((3,) + cell, f32),
            pltpu.VMEM((nr, 3) + cell, f32),
            pltpu.VMEM((3, 2) + cell, f32),
            pltpu.VMEM((nr, 3, 2) + cell, f32),
            pltpu.VMEM((nt, nr, 2) + cell, f32),
            dma((2,)), dma((2, FINE)),
            dma((2,)), dma((2, FINE)), dma((2,)),
            dma, dma((nr,)),
            dma, dma((nr,)),
            dma((nt,)), dma((nt,)),
            pltpu.SemaphoreType.REGULAR, pltpu.SemaphoreType.REGULAR, pltpu.SemaphoreType.REGULAR,
        ],
        compiler_params=pltpu.CompilerParams(
            collective_id=0, has_side_effects=True, vmem_limit_bytes=48 * 1024 * 1024),
        name="parareal",
    )(slab, kappa)
    ends, following = pl.pallas_call(
        deliver,
        out_shape=(
            jax.ShapeDtypeStruct((2, blocks, rows, LANES), f32),
            jax.ShapeDtypeStruct(following.shape, f32),
        ),
        in_specs=[pl.BlockSpec(memory_space=pltpu.VMEM)] * 2,
        out_specs=[pl.BlockSpec(memory_space=pltpu.HBM)] * 2,
        scratch_shapes=[dma((2 * rows + 1,))],
        compiler_params=pltpu.CompilerParams(vmem_limit_bytes=1024 * 1024),
        name="deliver",
    )(ends, following)
    new_ends = ends.transpose(0, 2, 1, 3).reshape(2, rows, columns)
    coarse_next = following.reshape(2, SUB, nr, LANES).transpose(0, 2, 1, 3).reshape(2, nr, SUB * LANES)
    return new_ends[None], coarse_next[None]


def solution(mesh):
    nt, nr = mesh.shape["tm"], mesh.shape["rows"]
    in_specs = (P("tm", None, "rows", None), P("rows", None))
    out_specs = (P("tm", None, "rows", None), P("tm", None, None, None))
    return jax.shard_map(functools.partial(body, nt, nr), mesh=mesh, in_specs=in_specs, out_specs=out_specs, check_vma=False)
```

```python
import functools
import math

import jax
import jax.numpy as jnp
from jax import lax
from jax.experimental import pallas as pl
from jax.experimental.pallas import tpu as pltpu
from jax.sharding import PartitionSpec as P

FINE = 8
COARSE = 2
COARSEN = 8
EXCHANGE = 0.05
TRACER_DIFF = 0.5

SUB = 8
LANES = 128
MESH = pl.DeviceIdType.MESH
SHARE = 2
SLOTS = 3
STARTS = (1, 3, 5)
AREA = 1.0 / (COARSEN * COARSEN)


def cell_index(axis):
    return lax.broadcasted_iota(jnp.int32, (SUB, LANES), axis)


def following(v):
    lane = cell_index(1)
    near = pltpu.roll(v, LANES - SUB, 1)
    far = jnp.where(lane < LANES - 1, pltpu.roll(v, LANES - SUB - 1, 1), pltpu.roll(v, LANES - 1, 1))
    edge = pltpu.roll(jnp.where(cell_index(0) == 0, far, near), SUB - 1, 0)
    return jnp.where(lane < LANES - SUB, near, edge)


def preceding(v):
    lane = cell_index(1)
    near = pltpu.roll(v, SUB, 1)
    far = jnp.where(lane >= 1, pltpu.roll(v, SUB + 1, 1), pltpu.roll(v, 1, 1))
    edge = pltpu.roll(jnp.where(cell_index(0) == SUB - 1, far, near), 1, 0)
    return jnp.where(lane >= SUB, near, edge)


def lines_to_lanes(v):
    lane, line = cell_index(1), cell_index(0)
    for step in (1, 2, 4):
        high_lane, high_line = (lane & (step * 16)) != 0, (line & step) != 0
        up = pltpu.roll(pltpu.roll(v, SUB - step, 0), step * 16, 1)
        down = pltpu.roll(pltpu.roll(v, step, 0), LANES - step * 16, 1)
        v = jnp.where(high_lane, jnp.where(high_line, v, up), jnp.where(high_line, down, v))
    return v


def to_right(v):
    return jnp.concatenate([v[1:], following(v[0])[None]], axis=0)


def to_left(v):
    return jnp.concatenate([preceding(v[COARSEN - 1])[None], v[:COARSEN - 1]], axis=0)


def exchange_lanes(rows):
    lane = cell_index(1)
    rows = list(rows)
    for step in (1, 2, 4):
        high = (lane & step) != 0
        for i in range(SUB):
            if not i & step:
                a, b = rows[i], rows[i | step]
                rows[i] = jnp.where(high, pltpu.roll(b, step, 1), a)
                rows[i | step] = jnp.where(high, b, pltpu.roll(a, LANES - step, 1))
    return rows


def exact_dot(x, w):
    rows = x.shape[0]
    hi = x.astype(jnp.bfloat16)
    rest = x - hi.astype(jnp.float32)
    mid = rest.astype(jnp.bfloat16)
    low = (rest - mid.astype(jnp.float32)).astype(jnp.bfloat16)
    y = jnp.dot(jnp.concatenate([hi.astype(jnp.float32), mid.astype(jnp.float32), low.astype(jnp.float32)], axis=0).astype(jnp.bfloat16), w,
                preferred_element_type=jnp.float32)
    return y[:rows] + y[rows:2 * rows] + y[2 * rows:]


def kernel(nt, nr, group, s_hbm, k_hbm, out_ref, nxt_ref,
           s_ref, k_ref, in_sem, wb, ub, own, kown, kh, kr, kl, kd, ku, ch, ct, part, order, ers, erg, cts, ctg, jall,
           vsend, vrecv, ksend, krecv, kfwd, ersend, errecv, ctsend, ctrecv, jsend, jrecv, tok_down, tok_up, tok_tm):
    t = lax.axis_index("tm")
    r = lax.axis_index("rows")
    member = lax.rem(t, group)
    base = t - member
    has_up = r > 0
    has_down = r < nr - 1
    sends = (has_down, has_up)
    gets = (has_up, has_down)
    f32 = jnp.float32

    outer_first = [row for d in range(SUB // 2) for row in (SUB - 1 - d, d)]

    k_in = pltpu.make_async_copy(k_hbm, k_ref, in_sem.at[0])
    s_in = pltpu.make_async_copy(s_hbm, s_ref, in_sem.at[1])
    k_in.start()
    s_in.start()

    barrier = pltpu.get_barrier_semaphore()

    def greet(tm, row):
        pl.semaphore_signal(barrier, inc=1, device_id=(tm, row), device_id_type=MESH)

    pl.when(has_up)(lambda: greet(t, r - 1))
    pl.when(has_down)(lambda: greet(t, r + 1))
    for o in range(1, nt):
        pl.when(t + o < nt)(lambda: greet(t + o, r))
    for o in range(1, group):
        pl.when(member >= o)(lambda: greet(t - o, r))

    source = lax.broadcasted_iota(jnp.int32, order.shape, 0)
    target = lax.broadcasted_iota(jnp.int32, order.shape, 1)
    goes = (source & (SUB - 1)) * (LANES // SUB) + (source >> 3)
    order[...] = jnp.where(goes == target, 1.0, 0.0).astype(jnp.bfloat16)
    for d in range(1, FINE):
        zero = jnp.zeros(wb.shape[2:], f32)
        wb[(d - 1) % 2, SUB - d] = zero
        wb[(d - 1) % 2, 2 * SUB - 1 + d] = zero

    @pl.when(jnp.logical_not(has_up))
    def _():
        ub[0, 0:SUB] = jnp.zeros((SUB,) + ub.shape[2:], f32)
        kh[0] = jnp.zeros(kh.shape[1:], f32)

    @pl.when(jnp.logical_not(has_down))
    def _():
        ub[0, 2 * SUB:] = jnp.zeros((SUB,) + ub.shape[2:], f32)
        kh[1] = jnp.zeros(kh.shape[1:], f32)

    def read_row(ref, row):
        return jnp.stack(exchange_lanes(
            [ref[pl.ds(m * SUB * SUB + row, SUB, stride=SUB), :] for m in range(SUB)]), axis=0)

    k_in.wait()
    total = None
    for row in outer_first:
        x = read_row(k_ref, row)
        kown[row] = x
        total = x if total is None else total + x
    ers[0] = jnp.sum(total, axis=0) * AREA

    pl.semaphore_wait(barrier, t + (group - 1 - member) + has_up.astype(jnp.int32) + has_down.astype(jnp.int32))

    def tell(tok, row):
        pl.semaphore_signal(tok, inc=1, device_id=(t, row), device_id_type=MESH)

    pl.when(jnp.logical_not(has_up) & has_down)(lambda: tell(tok_down, r + 1))
    pl.when(jnp.logical_not(has_down) & has_up)(lambda: tell(tok_up, r - 1))

    for o in range(1, nt):
        @pl.when(t >= o)
        def _():
            pl.semaphore_signal(tok_tm, inc=1, device_id=(t - o, r), device_id_type=MESH)

    def relay(slot):
        @pl.when(has_up & (jnp.minimum(r - 1, SLOTS - 1) == slot))
        def _():
            pl.semaphore_wait(tok_down, 1)
            pl.when(has_down)(lambda: tell(tok_down, r + 1))

        @pl.when(has_down & (jnp.minimum(nr - 2 - r, SLOTS - 1) == slot))
        def _():
            pl.semaphore_wait(tok_up, 1)
            pl.when(has_up)(lambda: tell(tok_up, r - 1))

    def v_copy(side, d):
        if side == 0:
            return pltpu.make_async_remote_copy(
                own.at[SUB - d], ub.at[0, SUB - d], vsend.at[side], vrecv.at[side, d - 1],
                device_id=(t, r + 1), device_id_type=MESH)
        return pltpu.make_async_remote_copy(
            own.at[d - 1], ub.at[0, 2 * SUB - 1 + d], vsend.at[side], vrecv.at[side, d - 1],
            device_id=(t, r - 1), device_id_type=MESH)

    def k_copy(side, d):
        return pltpu.make_async_remote_copy(
            kown.at[SUB - d if side == 0 else d - 1], kh.at[side, d - 1], ksend.at[side], krecv.at[side, d - 1],
            device_id=(t, r + 1 if side == 0 else r - 1), device_id_type=MESH)

    def k_forward(side, d, o):
        return pltpu.make_async_remote_copy(
            kh.at[side, d - 1], kh.at[side, d - 1], kfwd.at[side], krecv.at[side, d - 1],
            device_id=(base + lax.rem(member + o, group), r), device_id_type=MESH)

    def mine(d):
        return member == (d - 1) % group

    def er_copy(o):
        return pltpu.make_async_remote_copy(
            ers, erg.at[r], ersend, errecv.at[o],
            device_id=(t, lax.rem(r + o, nr)), device_id_type=MESH)

    def ct_copy(o):
        return pltpu.make_async_remote_copy(
            cts, ctg.at[r], ctsend, ctrecv.at[o],
            device_id=(t, lax.rem(r + o, nr)), device_id_type=MESH)

    def j_copy(o):
        return pltpu.make_async_remote_copy(
            jall.at[t], jall.at[t], jsend.at[o], jrecv.at[t],
            device_id=(t + o, r), device_id_type=MESH)

    for d in range(1, FINE + 1):
        for side in range(2):
            pl.when(sends[side] & mine(d))(lambda: k_copy(side, d).start())

    s_in.wait()
    sums = [None, None]
    for row in outer_first:
        for f in range(2):
            x = read_row(s_ref.at[f], row)
            own[row, f] = x
            wb[0, SUB + row, f] = x
            ub[0, SUB + row, f] = x
            sums[f] = x if sums[f] is None else sums[f] + x
    for f in range(2):
        ers[1 + f] = jnp.sum(sums[f], axis=0) * AREA
    erg[r] = ers[...]

    def send_row(d):
        for side in range(2):
            pl.when(sends[side])(lambda: v_copy(side, d).start())

    def columns_of(i, k):
        right = 0.5 * (k + to_right(k))
        kr[i] = right
        kl[i] = preceding(right[COARSEN - 1])

    def left_of(i):
        return jnp.concatenate([kl[i][None], kr[i, 0:COARSEN - 1]], axis=0)

    def centre_of(i):
        total = (kr[i] + left_of(i)) + (ku[i] + kd[i])
        ch[i] = (1.0 - EXCHANGE) - total
        ct[i] = (1.0 - EXCHANGE) - TRACER_DIFF * total

    for row in range(SUB):
        k = kown[row]
        columns_of(SUB + row, k)
        if row < SUB - 1:
            face = 0.5 * (k + kown[row + 1])
            kd[SUB + row] = face
            ku[SUB + row + 1] = face
        if 0 < row < SUB - 1:
            centre_of(SUB + row)

    def advance(buf, p, i, above=True, below=True):
        heat, tracer = buf[p, i, 0], buf[p, i, 1]
        right, left = kr[i], left_of(i)
        terms = [right * to_right(heat) + left * to_left(heat), right * to_right(tracer) + left * to_left(tracer)]
        if below:
            face = kd[i]
            terms = [terms[f] + face * buf[p, i + 1, f] for f in range(2)]
        if above:
            face = ku[i]
            terms = [terms[f] + face * buf[p, i - 1, f] for f in range(2)]
        return ((ch[i] * heat + EXCHANGE * tracer) + terms[0],
                (ct[i] * tracer + EXCHANGE * heat) + TRACER_DIFF * terms[1])

    relay(0)
    for level in range(1, SUB // 2):
        p = (level - 1) % 2
        for row in range(level, SUB - level):
            heat, tracer = advance(wb, p, SUB + row)
            for f, x in enumerate((heat, tracer)):
                wb[1 - p, SUB + row, f] = x
                ub[1 - p, SUB + row, f] = x

    def pass_on(d):
        for side in range(2):
            @pl.when(gets[side] & mine(d))
            def _():
                k_copy(side, d).wait_recv()
                for o in range(1, group):
                    k_forward(side, d, o).start()

    outside = (jnp.where(has_up, 1.0, 0.0), jnp.where(has_down, 1.0, 0.0))

    def faces_at(d):
        for side in range(2):
            pl.when(gets[side] & jnp.logical_not(mine(d)))(lambda: k_copy(side, d).wait_recv())
            k = kh[side, d - 1]
            inner = kh[side, d - 2] if d > 1 else kown[0 if side == 0 else SUB - 1]
            face = 0.5 * (k + inner)
            edge = face * outside[side] if d == 1 else face
            i = SUB - d if side == 0 else 2 * SUB - 1 + d
            columns_of(i, k)
            if side == 0:
                ku[i + 1] = face
                kd[i] = edge
                centre_of(i + 1)
            else:
                kd[i - 1] = face
                ku[i] = edge
                centre_of(i - 1)

    for d in range(1, 5):
        pass_on(d)
    for level in range(1, FINE):
        for d in range(2 * level + 3, min(2 * level + 4, FINE) + 1):
            pass_on(d)
        faces_at(level)
        if level in STARTS:
            send_row(STARTS.index(level) + 1)
        if level in (2, 4):
            relay(level // 2)
        if level == 4:
            for o in range(1, nr):
                er_copy(o).start()
        p = (level - 1) % 2
        first, last = SUB + 1 - level, 2 * SUB - 2 + level
        for i in range(first, last + 1):
            if SUB + level <= i < 2 * SUB - level:
                continue
            heat, tracer = advance(wb, p, i)
            wb[1 - p, i, 0] = heat
            wb[1 - p, i, 1] = tracer
        for i, inner, face in ((first - 1, first, kd), (last + 1, last, ku)):
            for f in range(2):
                wb[1 - p, i, f] = (1.0, TRACER_DIFF)[f] * face[i] * wb[p, inner, f]

    p = (FINE - 1) % 2
    fluxes = [[jnp.sum(ku[SUB] * (wb[p, SUB - 1, f] - wb[p, SUB, f]), axis=0) for f in range(2)],
              [jnp.sum(kd[2 * SUB - 1] * (wb[p, 2 * SUB, f] - wb[p, 2 * SUB - 1, f]), axis=0) for f in range(2)]]
    for b in range(3):
        whole, gain = [], []
        for f in range(2):
            total, side_flux = None, None
            for i in range(max(1, SUB * b), min(3 * SUB - 1, SUB * (b + 1))):
                x = wb[p, i, f]
                flux = kr[i, COARSEN - 1] * (following(x[0]) - x[COARSEN - 1])
                total = x if total is None else total + x
                side_flux = flux if side_flux is None else side_flux + flux
            change = side_flux - preceding(side_flux)
            if b == 0:
                change = change - fluxes[0][f]
            elif b == 1:
                change = change + (fluxes[0][f] + fluxes[1][f])
            else:
                change = change - fluxes[1][f]
            whole.append(jnp.sum(total, axis=0))
            gain.append((1.0, TRACER_DIFF)[f] * change)
        moved = EXCHANGE * (whole[1] - whole[0])
        cts[b, 0] = AREA * ((whole[0] + moved) + gain[0])
        cts[b, 1] = AREA * ((whole[1] - moved) + gain[1])
    for o in range(1, nr):
        ct_copy(o).start()
    ctg[r] = cts[...]
    faces_at(FINE)

    def row_pair(level, diagonal):
        p = lax.rem(level + 1, 2)
        new = [(i,) + advance(ub, p, i) for i in (SUB + level - diagonal, 2 * SUB - 1 - level + diagonal)]
        for i, heat, tracer in new:
            ub[1 - p, i, 0] = heat
            ub[1 - p, i, 1] = tracer

    def run_diagonal(diagonal):
        for side in range(2):
            pl.when(gets[side])(lambda: v_copy(side, diagonal).wait_recv())
        def step(level, carry):
            row_pair(level, diagonal)
            return carry
        lax.fori_loop(1, min(FINE, SUB // 2 - 1 + diagonal) + 1, step, 0)

    ratio = (FINE / COARSE) / float(COARSEN * COARSEN)
    rate = EXCHANGE * (FINE / COARSE)

    run_diagonal(1)
    run_diagonal(2)
    send_row(4)

    for o in range(1, nr):
        er_copy(o).wait_recv()
    kcv = [erg[i, 0] for i in range(nr)]
    c_right = [ratio * 0.5 * (k + following(k)) for k in kcv]
    c_left = [ratio * 0.5 * (k + preceding(k)) for k in kcv]
    c_face = [ratio * 0.5 * kcv[0]]
    c_face += [ratio * 0.5 * (kcv[i] + kcv[i + 1]) for i in range(nr - 1)]
    c_face += [ratio * 0.5 * kcv[nr - 1]]
    totals = [(c_right[i] + c_left[i]) + (c_face[i] + c_face[i + 1]) for i in range(nr)]
    c_centre = [[(1.0 - rate) - x for x in totals], [(1.0 - rate) - TRACER_DIFF * x for x in totals]]

    def coarse_prop(state):
        for substep in range(COARSE):
            new = []
            for f in range(2):
                rows = state[f * nr:(f + 1) * nr]
                other = state[(1 - f) * nr:(2 - f) * nr]
                for i in range(nr):
                    v = rows[i]
                    around = c_right[i] * following(v) + c_left[i] * preceding(v)
                    if i > 0:
                        around = around + c_face[i] * rows[i - 1]
                    if i < nr - 1:
                        around = around + c_face[i + 1] * rows[i + 1]
                    if f == 1:
                        around = TRACER_DIFF * around
                    new.append((c_centre[f][i] * v + rate * other[i]) + around)
            state = tuple(new)
        return state

    send_row(5)
    later = jnp.where(t > 0, 1.0, 0.0)
    old = coarse_prop(tuple(later * erg[i, 1 + f] for f in range(2) for i in range(nr)))

    for o in range(1, nr):
        ct_copy(o).wait_recv()
    change = []
    for f in range(2):
        for i in range(nr):
            x = ctg[i, 1, f]
            if i > 0:
                x = x + ctg[i - 1, 2, f]
            if i < nr - 1:
                x = x + ctg[i + 1, 0, f]
            x = x - old[f * nr + i]
            jall[t, i, f] = x
            change.append(x)
    pl.when(t < nt - 1)(lambda: pl.semaphore_wait(tok_tm, nt - 1 - t))
    for o in range(1, nt):
        pl.when(t + o < nt)(lambda: j_copy(o).start())

    send_row(6)
    for d in range(3, FINE):
        run_diagonal(d)
        if d < 5:
            send_row(d + 4)

    def place(level, side):
        return level if side == 0 else 3 * SUB - 1 - level

    for level in range(1, FINE + 1):
        for side in range(2):
            heat, tracer = advance(ub, (level - 1) % 2, place(level, side), above=side == 1, below=side == 0)
            part[level - 1, side, 0] = heat
            part[level - 1, side, 1] = tracer

    share = FINE // group
    for side in range(2):
        @pl.when(sends[side])
        def _():
            pltpu.make_async_remote_copy(
                kown.at[pl.ds(0, share)], kh.at[side, pl.ds(0, share)], ksend.at[side], krecv.at[side, 0],
                device_id=(t, r + 1 if side == 0 else r - 1), device_id_type=MESH).wait_send()

        if group > 1:
            @pl.when(gets[side])
            def _():
                passed = kh.at[side, pl.ds(0, share * (group - 1))]
                pltpu.make_async_remote_copy(
                    passed, passed, kfwd.at[side], krecv.at[side, 0],
                    device_id=(base + lax.rem(member + 1, group), r), device_id_type=MESH).wait_send()
    if nr > 1:
        for ref, send, recv in ((erg, ersend, errecv), (ctg, ctsend, ctrecv)):
            spread = ref.at[pl.ds(0, nr - 1)]
            pltpu.make_async_remote_copy(
                spread, spread, send, recv.at[0],
                device_id=(t, lax.rem(r + 1, nr)), device_id_type=MESH).wait_send()
    for o in range(1, nt):
        pl.when(t + o < nt)(lambda: j_copy(o).wait_send())

    def link(n, state):
        pltpu.make_async_remote_copy(
            jall.at[n], jall.at[n], jsend.at[0], jrecv.at[n],
            device_id=(n, r), device_id_type=MESH).wait_recv()
        state = coarse_prop(state)
        return tuple(state[f * nr + i] + jall[n, i, f] for f in range(2) for i in range(nr))

    state = tuple(jnp.zeros((SUB, LANES), f32) for _ in range(2 * nr))
    state = lax.fori_loop(0, t, link, state)
    state = coarse_prop(state)

    fix = [None, None]
    for f in range(2):
        for i in range(nr):
            value = state[f * nr + i] - old[f * nr + i]
            fix[f] = value if i == 0 else jnp.where(r == i, value, fix[f])
    natural = exact_dot(jnp.concatenate([state[n] + change[n] for n in range(2 * nr)], axis=0), order[...])
    for f in range(2):
        for i in range(nr):
            n = f * nr + i
            nxt_ref[f, pl.ds(i, SUB, stride=nr), :] = lines_to_lanes(natural[n * SUB:(n + 1) * SUB])

    def write_row(row, f, end):
        end = exchange_lanes([end[m] + fix[f] for m in range(COARSEN)])
        for m in range(SUB):
            out_ref[f, row, m * SUB:(m + 1) * SUB, :] = end[m]

    for row in range(1, SUB - 1):
        for f in range(2):
            write_row(row, f, ub[0, SUB + row, f])

    last = []
    for side in range(2):
        pl.when(gets[side])(lambda: v_copy(side, FINE).wait_recv())
    for side in range(2):
        i = place(0, side)
        last.append([ub[0, i, 0], ub[0, i, 1]])
    for level in range(1, FINE + 1):
        for side in range(2):
            face = (ku, kd)[side][place(level, side)]
            heat, tracer = last[side]
            last[side] = [part[level - 1, side, 0] + face * heat,
                          part[level - 1, side, 1] + (TRACER_DIFF * face) * tracer]
    for side in range(2):
        for f in range(2):
            write_row((0, SUB - 1)[side], f, last[side][f])

    for side in range(2):
        @pl.when(sends[side])
        def _():
            pltpu.make_async_remote_copy(
                own, ub.at[0, pl.ds(0, SUB)], vsend.at[side], vrecv.at[side, 0],
                device_id=(t, r + 1 if side == 0 else r - 1), device_id_type=MESH).wait_send()


def deliver(ends, following, ends_out, following_out, sem):
    fields, rows = ends.shape[:2]
    copies = [pltpu.make_async_copy(ends.at[f, row], ends_out.at[f, :, row, :], sem.at[f * rows + row])
              for row in range(rows) for f in range(fields)]
    copies.append(pltpu.make_async_copy(following, following_out, sem.at[fields * rows]))
    for copy in copies:
        copy.start()
    for copy in copies:
        copy.wait()


def body(nt, nr, starts, conductivity):
    rows, columns = conductivity.shape
    assert rows == SUB == COARSEN == FINE
    assert columns == COARSEN * SUB * LANES
    blocks = columns // LANES
    group = math.gcd(SHARE, nt)
    slab = starts[0].reshape(2, rows, blocks, LANES).transpose(0, 2, 1, 3).reshape(2, blocks * rows, LANES)
    kappa = conductivity.reshape(rows, blocks, LANES).transpose(1, 0, 2).reshape(blocks * rows, LANES)
    slab = pltpu.with_memory_space_constraint(slab, pltpu.HBM)
    kappa = pltpu.with_memory_space_constraint(kappa, pltpu.HBM)
    f32 = jnp.float32
    dma = pltpu.SemaphoreType.DMA
    cell = (SUB, LANES)
    line = (COARSEN,) + cell
    ends, following = pl.pallas_call(
        functools.partial(kernel, nt, nr, group),
        out_shape=(
            jax.ShapeDtypeStruct((2, rows, blocks, LANES), f32),
            jax.ShapeDtypeStruct((2, SUB * nr, LANES), f32),
        ),
        in_specs=[pl.BlockSpec(memory_space=pltpu.HBM)] * 2,
        out_specs=[pl.BlockSpec(memory_space=pltpu.VMEM)] * 2,
        scratch_shapes=[
            pltpu.VMEM((2, blocks * rows, LANES), f32),
            pltpu.VMEM((blocks * rows, LANES), f32),
            dma((2,)),
            pltpu.VMEM((2, 3 * SUB, 2) + line, f32),
            pltpu.VMEM((2, 3 * SUB, 2) + line, f32),
            pltpu.VMEM((SUB, 2) + line, f32),
            pltpu.VMEM((SUB,) + line, f32),
            pltpu.VMEM((2, FINE) + line, f32),
            pltpu.VMEM((3 * SUB,) + line, f32),
            pltpu.VMEM((3 * SUB,) + cell, f32),
            pltpu.VMEM((3 * SUB,) + line, f32),
            pltpu.VMEM((3 * SUB,) + line, f32),
            pltpu.VMEM((3 * SUB,) + line, f32),
            pltpu.VMEM((3 * SUB,) + line, f32),
            pltpu.VMEM((FINE, 2, 2) + line, f32),
            pltpu.VMEM((LANES, LANES), jnp.bfloat16),
            pltpu.VMEM((3,) + cell, f32),
            pltpu.VMEM((nr, 3) + cell, f32),
            pltpu.VMEM((3, 2) + cell, f32),
            pltpu.VMEM((nr, 3, 2) + cell, f32),
            pltpu.VMEM((nt, nr, 2) + cell, f32),
            dma((2,)), dma((2, FINE)),
            dma((2,)), dma((2, FINE)), dma((2,)),
            dma, dma((nr,)),
            dma, dma((nr,)),
            dma((nt,)), dma((nt,)),
            pltpu.SemaphoreType.REGULAR, pltpu.SemaphoreType.REGULAR, pltpu.SemaphoreType.REGULAR,
        ],
        compiler_params=pltpu.CompilerParams(
            collective_id=0, has_side_effects=True, vmem_limit_bytes=48 * 1024 * 1024),
        name="parareal",
    )(slab, kappa)
    ends, following = pl.pallas_call(
        deliver,
        out_shape=(
            jax.ShapeDtypeStruct((2, blocks, rows, LANES), f32),
            jax.ShapeDtypeStruct(following.shape, f32),
        ),
        in_specs=[pl.BlockSpec(memory_space=pltpu.VMEM)] * 2,
        out_specs=[pl.BlockSpec(memory_space=pltpu.HBM)] * 2,
        scratch_shapes=[dma((2 * rows + 1,))],
        compiler_params=pltpu.CompilerParams(vmem_limit_bytes=1024 * 1024),
        name="deliver",
    )(ends, following)
    new_ends = ends.transpose(0, 2, 1, 3).reshape(2, rows, columns)
    coarse_next = following.reshape(2, SUB, nr, LANES).transpose(0, 2, 1, 3).reshape(2, nr, SUB * LANES)
    return new_ends[None], coarse_next[None]


def solution(mesh):
    nt, nr = mesh.shape["tm"], mesh.shape["rows"]
    in_specs = (P("tm", None, "rows", None), P("rows", None))
    out_specs = (P("tm", None, "rows", None), P("tm", None, None, None))
    return jax.shard_map(functools.partial(body, nt, nr), mesh=mesh, in_specs=in_specs, out_specs=out_specs, check_vma=False)
```

```python
import functools
import math

import jax
import jax.numpy as jnp
from jax import lax
from jax.experimental import pallas as pl
from jax.experimental.pallas import tpu as pltpu
from jax.sharding import PartitionSpec as P

FINE = 8
COARSE = 2
COARSEN = 8
EXCHANGE = 0.05
TRACER_DIFF = 0.5

SUB = 8
LANES = 128
MESH = pl.DeviceIdType.MESH
SHARE = 2
SLOTS = 3
LATE = 6
STARTS = (1, 3, 5)
AREA = 1.0 / (COARSEN * COARSEN)


def cell_index(axis):
    return lax.broadcasted_iota(jnp.int32, (SUB, LANES), axis)


def following(v):
    lane = cell_index(1)
    near = pltpu.roll(v, LANES - SUB, 1)
    far = jnp.where(lane < LANES - 1, pltpu.roll(v, LANES - SUB - 1, 1), pltpu.roll(v, LANES - 1, 1))
    edge = pltpu.roll(jnp.where(cell_index(0) == 0, far, near), SUB - 1, 0)
    return jnp.where(lane < LANES - SUB, near, edge)


def preceding(v):
    lane = cell_index(1)
    near = pltpu.roll(v, SUB, 1)
    far = jnp.where(lane >= 1, pltpu.roll(v, SUB + 1, 1), pltpu.roll(v, 1, 1))
    edge = pltpu.roll(jnp.where(cell_index(0) == SUB - 1, far, near), 1, 0)
    return jnp.where(lane >= SUB, near, edge)


def lines_to_lanes(v):
    lane, line = cell_index(1), cell_index(0)
    for step in (1, 2, 4):
        high_lane, high_line = (lane & (step * 16)) != 0, (line & step) != 0
        up = pltpu.roll(pltpu.roll(v, SUB - step, 0), step * 16, 1)
        down = pltpu.roll(pltpu.roll(v, step, 0), LANES - step * 16, 1)
        v = jnp.where(high_lane, jnp.where(high_line, v, up), jnp.where(high_line, down, v))
    return v


def to_right(v):
    return jnp.concatenate([v[1:], following(v[0])[None]], axis=0)


def to_left(v):
    return jnp.concatenate([preceding(v[COARSEN - 1])[None], v[:COARSEN - 1]], axis=0)


def exchange_lanes(rows):
    lane = cell_index(1)
    rows = list(rows)
    for step in (1, 2, 4):
        high = (lane & step) != 0
        for i in range(SUB):
            if not i & step:
                a, b = rows[i], rows[i | step]
                rows[i] = jnp.where(high, pltpu.roll(b, step, 1), a)
                rows[i | step] = jnp.where(high, b, pltpu.roll(a, LANES - step, 1))
    return rows


def exact_dot(x, w):
    rows = x.shape[0]
    hi = x.astype(jnp.bfloat16)
    rest = x - hi.astype(jnp.float32)
    mid = rest.astype(jnp.bfloat16)
    low = (rest - mid.astype(jnp.float32)).astype(jnp.bfloat16)
    y = jnp.dot(jnp.concatenate([hi.astype(jnp.float32), mid.astype(jnp.float32), low.astype(jnp.float32)], axis=0).astype(jnp.bfloat16), w,
                preferred_element_type=jnp.float32)
    return y[:rows] + y[rows:2 * rows] + y[2 * rows:]


def kernel(nt, nr, group, s_hbm, k_hbm, out_ref, nxt_ref,
           s_ref, k_ref, in_sem, wb, ub, own, kown, kh, kr, kl, kd, ku, ch, ct, part, order, ers, erg, cts, ctg, jall,
           vsend, vrecv, ksend, krecv, kfwd, ersend, errecv, ctsend, ctrecv, jsend, jrecv, tok_down, tok_up, tok_tm):
    t = lax.axis_index("tm")
    r = lax.axis_index("rows")
    member = lax.rem(t, group)
    base = t - member
    has_up = r > 0
    has_down = r < nr - 1
    sends = (has_down, has_up)
    gets = (has_up, has_down)
    f32 = jnp.float32

    outer_first = [row for d in range(SUB // 2) for row in (SUB - 1 - d, d)]

    k_in = pltpu.make_async_copy(k_hbm, k_ref, in_sem.at[0])
    s_in = pltpu.make_async_copy(s_hbm, s_ref, in_sem.at[1])
    k_in.start()
    s_in.start()

    barrier = pltpu.get_barrier_semaphore()

    def greet(tm, row):
        pl.semaphore_signal(barrier, inc=1, device_id=(tm, row), device_id_type=MESH)

    pl.when(has_up)(lambda: greet(t, r - 1))
    pl.when(has_down)(lambda: greet(t, r + 1))
    for o in range(1, nt):
        pl.when(t + o < nt)(lambda: greet(t + o, r))
    for o in range(1, group):
        pl.when(member >= o)(lambda: greet(t - o, r))

    source = lax.broadcasted_iota(jnp.int32, order.shape, 0)
    target = lax.broadcasted_iota(jnp.int32, order.shape, 1)
    goes = (source & (SUB - 1)) * (LANES // SUB) + (source >> 3)
    order[...] = jnp.where(goes == target, 1.0, 0.0).astype(jnp.bfloat16)
    for d in range(1, FINE):
        zero = jnp.zeros(wb.shape[2:], f32)
        wb[(d - 1) % 2, SUB - d] = zero
        wb[(d - 1) % 2, 2 * SUB - 1 + d] = zero

    @pl.when(jnp.logical_not(has_up))
    def _():
        ub[0, 0:SUB] = jnp.zeros((SUB,) + ub.shape[2:], f32)
        kh[0] = jnp.zeros(kh.shape[1:], f32)

    @pl.when(jnp.logical_not(has_down))
    def _():
        ub[0, 2 * SUB:] = jnp.zeros((SUB,) + ub.shape[2:], f32)
        kh[1] = jnp.zeros(kh.shape[1:], f32)

    def read_row(ref, row):
        return jnp.stack(exchange_lanes(
            [ref[pl.ds(m * SUB * SUB + row, SUB, stride=SUB), :] for m in range(SUB)]), axis=0)

    k_in.wait()
    total = None
    for row in outer_first:
        x = read_row(k_ref, row)
        kown[row] = x
        total = x if total is None else total + x
    ers[0] = jnp.sum(total, axis=0) * AREA

    pl.semaphore_wait(barrier, t + (group - 1 - member) + has_up.astype(jnp.int32) + has_down.astype(jnp.int32))

    def tell(tok, row):
        pl.semaphore_signal(tok, inc=1, device_id=(t, row), device_id_type=MESH)

    pl.when(jnp.logical_not(has_up) & has_down)(lambda: tell(tok_down, r + 1))
    pl.when(jnp.logical_not(has_down) & has_up)(lambda: tell(tok_up, r - 1))

    for o in range(1, nt):
        @pl.when(t >= o)
        def _():
            pl.semaphore_signal(tok_tm, inc=1, device_id=(t - o, r), device_id_type=MESH)

    def relay(slot):
        @pl.when(has_up & (jnp.minimum(r - 1, SLOTS - 1) == slot))
        def _():
            pl.semaphore_wait(tok_down, 1)
            pl.when(has_down)(lambda: tell(tok_down, r + 1))

        @pl.when(has_down & (jnp.minimum(nr - 2 - r, SLOTS - 1) == slot))
        def _():
            pl.semaphore_wait(tok_up, 1)
            pl.when(has_up)(lambda: tell(tok_up, r - 1))

    def v_copy(side, d):
        if side == 0:
            return pltpu.make_async_remote_copy(
                own.at[SUB - d], ub.at[0, SUB - d], vsend.at[side], vrecv.at[side, d - 1],
                device_id=(t, r + 1), device_id_type=MESH)
        return pltpu.make_async_remote_copy(
            own.at[d - 1], ub.at[0, 2 * SUB - 1 + d], vsend.at[side], vrecv.at[side, d - 1],
            device_id=(t, r - 1), device_id_type=MESH)

    def k_copy(side, d):
        return pltpu.make_async_remote_copy(
            kown.at[SUB - d if side == 0 else d - 1], kh.at[side, d - 1], ksend.at[side], krecv.at[side, d - 1],
            device_id=(t, r + 1 if side == 0 else r - 1), device_id_type=MESH)

    def k_forward(side, d, o):
        return pltpu.make_async_remote_copy(
            kh.at[side, d - 1], kh.at[side, d - 1], kfwd.at[side], krecv.at[side, d - 1],
            device_id=(base + lax.rem(member + o, group), r), device_id_type=MESH)

    def mine(d):
        return member == (d - 1) % group

    def er_copy(o):
        return pltpu.make_async_remote_copy(
            ers, erg.at[r], ersend, errecv.at[o],
            device_id=(t, lax.rem(r + o, nr)), device_id_type=MESH)

    def ct_copy(o):
        return pltpu.make_async_remote_copy(
            cts, ctg.at[r], ctsend, ctrecv.at[o],
            device_id=(t, lax.rem(r + o, nr)), device_id_type=MESH)

    def j_copy(o):
        return pltpu.make_async_remote_copy(
            jall.at[t], jall.at[t], jsend.at[o], jrecv.at[t],
            device_id=(t + o, r), device_id_type=MESH)

    for d in range(1, FINE + 1):
        for side in range(2):
            pl.when(sends[side] & mine(d))(lambda: k_copy(side, d).start())

    s_in.wait()
    sums = [None, None]
    for row in outer_first:
        for f in range(2):
            x = read_row(s_ref.at[f], row)
            own[row, f] = x
            wb[0, SUB + row, f] = x
            ub[0, SUB + row, f] = x
            sums[f] = x if sums[f] is None else sums[f] + x
    for f in range(2):
        ers[1 + f] = jnp.sum(sums[f], axis=0) * AREA
    erg[r] = ers[...]

    def send_row(d):
        for side in range(2):
            pl.when(sends[side])(lambda: v_copy(side, d).start())

    def columns_of(i, k):
        right = 0.5 * (k + to_right(k))
        kr[i] = right
        kl[i] = preceding(right[COARSEN - 1])

    def left_of(i):
        return jnp.concatenate([kl[i][None], kr[i, 0:COARSEN - 1]], axis=0)

    def centre_of(i):
        total = (kr[i] + left_of(i)) + (ku[i] + kd[i])
        ch[i] = (1.0 - EXCHANGE) - total
        ct[i] = (1.0 - EXCHANGE) - TRACER_DIFF * total

    for row in range(SUB):
        k = kown[row]
        columns_of(SUB + row, k)
        if row < SUB - 1:
            face = 0.5 * (k + kown[row + 1])
            kd[SUB + row] = face
            ku[SUB + row + 1] = face
        if 0 < row < SUB - 1:
            centre_of(SUB + row)

    def advance(buf, p, i, above=True, below=True):
        heat, tracer = buf[p, i, 0], buf[p, i, 1]
        right, left = kr[i], left_of(i)
        terms = [right * to_right(heat) + left * to_left(heat), right * to_right(tracer) + left * to_left(tracer)]
        if below:
            face = kd[i]
            terms = [terms[f] + face * buf[p, i + 1, f] for f in range(2)]
        if above:
            face = ku[i]
            terms = [terms[f] + face * buf[p, i - 1, f] for f in range(2)]
        return ((ch[i] * heat + EXCHANGE * tracer) + terms[0],
                (ct[i] * tracer + EXCHANGE * heat) + TRACER_DIFF * terms[1])

    relay(0)
    for level in range(1, SUB // 2):
        p = (level - 1) % 2
        for row in range(level, SUB - level):
            heat, tracer = advance(wb, p, SUB + row)
            for f, x in enumerate((heat, tracer)):
                wb[1 - p, SUB + row, f] = x
                ub[1 - p, SUB + row, f] = x

    def pass_on(d):
        for side in range(2):
            @pl.when(gets[side] & mine(d))
            def _():
                k_copy(side, d).wait_recv()
                for o in range(1, group):
                    k_forward(side, d, o).start()

    outside = (jnp.where(has_up, 1.0, 0.0), jnp.where(has_down, 1.0, 0.0))

    def faces_at(d):
        for side in range(2):
            pl.when(gets[side] & jnp.logical_not(mine(d)))(lambda: k_copy(side, d).wait_recv())
            k = kh[side, d - 1]
            inner = kh[side, d - 2] if d > 1 else kown[0 if side == 0 else SUB - 1]
            face = 0.5 * (k + inner)
            edge = face * outside[side] if d == 1 else face
            i = SUB - d if side == 0 else 2 * SUB - 1 + d
            columns_of(i, k)
            if side == 0:
                ku[i + 1] = face
                kd[i] = edge
                centre_of(i + 1)
            else:
                kd[i - 1] = face
                ku[i] = edge
                centre_of(i - 1)

    for d in range(1, 5):
        pass_on(d)
    for level in range(1, FINE):
        for d in range(2 * level + 3, min(2 * level + 4, FINE) + 1):
            pass_on(d)
        faces_at(level)
        if level in STARTS:
            send_row(STARTS.index(level) + 1)
        if level in (2, 4):
            relay(level // 2)
        if level == 4:
            for o in range(1, nr):
                er_copy(o).start()
        p = (level - 1) % 2
        first, last = SUB + 1 - level, 2 * SUB - 2 + level
        for i in range(first, last + 1):
            if SUB + level <= i < 2 * SUB - level:
                continue
            heat, tracer = advance(wb, p, i)
            wb[1 - p, i, 0] = heat
            wb[1 - p, i, 1] = tracer
        for i, inner, face in ((first - 1, first, kd), (last + 1, last, ku)):
            for f in range(2):
                wb[1 - p, i, f] = (1.0, TRACER_DIFF)[f] * face[i] * wb[p, inner, f]

    p = (FINE - 1) % 2
    fluxes = [[jnp.sum(ku[SUB] * (wb[p, SUB - 1, f] - wb[p, SUB, f]), axis=0) for f in range(2)],
              [jnp.sum(kd[2 * SUB - 1] * (wb[p, 2 * SUB, f] - wb[p, 2 * SUB - 1, f]), axis=0) for f in range(2)]]
    for b in range(3):
        whole, gain = [], []
        for f in range(2):
            total, side_flux = None, None
            for i in range(max(1, SUB * b), min(3 * SUB - 1, SUB * (b + 1))):
                x = wb[p, i, f]
                flux = kr[i, COARSEN - 1] * (following(x[0]) - x[COARSEN - 1])
                total = x if total is None else total + x
                side_flux = flux if side_flux is None else side_flux + flux
            change = side_flux - preceding(side_flux)
            if b == 0:
                change = change - fluxes[0][f]
            elif b == 1:
                change = change + (fluxes[0][f] + fluxes[1][f])
            else:
                change = change - fluxes[1][f]
            whole.append(jnp.sum(total, axis=0))
            gain.append((1.0, TRACER_DIFF)[f] * change)
        moved = EXCHANGE * (whole[1] - whole[0])
        cts[b, 0] = AREA * ((whole[0] + moved) + gain[0])
        cts[b, 1] = AREA * ((whole[1] - moved) + gain[1])
    for o in range(1, nr):
        ct_copy(o).start()
    ctg[r] = cts[...]
    faces_at(FINE)

    def row_pair(level, diagonal):
        p = lax.rem(level + 1, 2)
        new = [(i,) + advance(ub, p, i) for i in (SUB + level - diagonal, 2 * SUB - 1 - level + diagonal)]
        for i, heat, tracer in new:
            ub[1 - p, i, 0] = heat
            ub[1 - p, i, 1] = tracer

    def run_diagonal(diagonal):
        for side in range(2):
            pl.when(gets[side])(lambda: v_copy(side, diagonal).wait_recv())
        def step(level, carry):
            row_pair(level, diagonal)
            return carry
        lax.fori_loop(1, min(FINE, SUB // 2 - 1 + diagonal) + 1, step, 0)

    ratio = (FINE / COARSE) / float(COARSEN * COARSEN)
    rate = EXCHANGE * (FINE / COARSE)

    run_diagonal(1)

    for o in range(1, nr):
        er_copy(o).wait_recv()
    kcv = [erg[i, 0] for i in range(nr)]
    c_right = [ratio * 0.5 * (k + following(k)) for k in kcv]
    c_left = [ratio * 0.5 * (k + preceding(k)) for k in kcv]
    c_face = [ratio * 0.5 * kcv[0]]
    c_face += [ratio * 0.5 * (kcv[i] + kcv[i + 1]) for i in range(nr - 1)]
    c_face += [ratio * 0.5 * kcv[nr - 1]]
    totals = [(c_right[i] + c_left[i]) + (c_face[i] + c_face[i + 1]) for i in range(nr)]
    c_centre = [[(1.0 - rate) - x for x in totals], [(1.0 - rate) - TRACER_DIFF * x for x in totals]]

    def coarse_prop(state):
        for substep in range(COARSE):
            new = []
            for f in range(2):
                rows = state[f * nr:(f + 1) * nr]
                other = state[(1 - f) * nr:(2 - f) * nr]
                for i in range(nr):
                    v = rows[i]
                    around = c_right[i] * following(v) + c_left[i] * preceding(v)
                    if i > 0:
                        around = around + c_face[i] * rows[i - 1]
                    if i < nr - 1:
                        around = around + c_face[i + 1] * rows[i + 1]
                    if f == 1:
                        around = TRACER_DIFF * around
                    new.append((c_centre[f][i] * v + rate * other[i]) + around)
            state = tuple(new)
        return state

    later = jnp.where(t > 0, 1.0, 0.0)
    old = coarse_prop(tuple(later * erg[i, 1 + f] for f in range(2) for i in range(nr)))

    send_row(4)
    run_diagonal(2)
    send_row(5)
    for o in range(1, nr):
        ct_copy(o).wait_recv()
    change = []
    for f in range(2):
        for i in range(nr):
            x = ctg[i, 1, f]
            if i > 0:
                x = x + ctg[i - 1, 2, f]
            if i < nr - 1:
                x = x + ctg[i + 1, 0, f]
            x = x - old[f * nr + i]
            jall[t, i, f] = x
            change.append(x)
    pl.when(t < nt - 1)(lambda: pl.semaphore_wait(tok_tm, nt - 1 - t))
    for o in range(1, nt):
        pl.when(t + o < nt)(lambda: j_copy(o).start())

    send_row(6)
    for d in range(3, LATE):
        run_diagonal(d)
        if d < 5:
            send_row(d + 4)

    def place(level, side, d):
        return SUB + level - d if side == 0 else 2 * SUB - 1 - level + d

    def prepare(d):
        for level in range(1, FINE + 1):
            for side in range(2):
                i = place(level, side, d)
                for f, x in enumerate(advance(ub, (level - 1) % 2, i, above=side == 1, below=side == 0)):
                    part[level - 1, side, f] = x

    def complete(d):
        for side in range(2):
            pl.when(gets[side])(lambda: v_copy(side, d).wait_recv())
        ends = [[ub[0, place(0, side, d), f] for f in range(2)] for side in range(2)]
        for level in range(1, FINE + 1):
            for side in range(2):
                i = place(level, side, d)
                face = (ku, kd)[side][i]
                heat, tracer = ends[side]
                ends[side] = [part[level - 1, side, 0] + face * heat,
                              part[level - 1, side, 1] + (TRACER_DIFF * face) * tracer]
                if d < FINE and level < FINE:
                    for f in range(2):
                        ub[level % 2, i, f] = ends[side][f]
        return ends

    share = FINE // group
    for side in range(2):
        @pl.when(sends[side])
        def _():
            pltpu.make_async_remote_copy(
                kown.at[pl.ds(0, share)], kh.at[side, pl.ds(0, share)], ksend.at[side], krecv.at[side, 0],
                device_id=(t, r + 1 if side == 0 else r - 1), device_id_type=MESH).wait_send()

        if group > 1:
            @pl.when(gets[side])
            def _():
                passed = kh.at[side, pl.ds(0, share * (group - 1))]
                pltpu.make_async_remote_copy(
                    passed, passed, kfwd.at[side], krecv.at[side, 0],
                    device_id=(base + lax.rem(member + 1, group), r), device_id_type=MESH).wait_send()
    if nr > 1:
        for ref, send, recv in ((erg, ersend, errecv), (ctg, ctsend, ctrecv)):
            spread = ref.at[pl.ds(0, nr - 1)]
            pltpu.make_async_remote_copy(
                spread, spread, send, recv.at[0],
                device_id=(t, lax.rem(r + 1, nr)), device_id_type=MESH).wait_send()
    for o in range(1, nt):
        pl.when(t + o < nt)(lambda: j_copy(o).wait_send())

    def link(n, state):
        pltpu.make_async_remote_copy(
            jall.at[n], jall.at[n], jsend.at[0], jrecv.at[n],
            device_id=(n, r), device_id_type=MESH).wait_recv()
        return coarse_prop(tuple(state[f * nr + i] + jall[n, i, f] for f in range(2) for i in range(nr)))

    def write_row(row, ends):
        for f in range(2):
            end = exchange_lanes([ends[f][m] + fix[f] for m in range(COARSEN)])
            for m in range(SUB):
                out_ref[f, row, m * SUB:(m + 1) * SUB, :] = end[m]

    def write_pair(d, ends):
        write_row(FINE - d, ends[0])
        write_row(d - 1, ends[1])

    prepare(LATE)
    early = complete(LATE)
    for side, row in enumerate((FINE - LATE, LATE - 1)):
        for f in range(2):
            ub[FINE % 2, SUB + row, f] = early[side][f]
    prepare(LATE + 1)

    state = tuple(jnp.zeros((SUB, LANES), f32) for _ in range(2 * nr))
    state = lax.fori_loop(0, t, link, state)
    fix = [None, None]
    for f in range(2):
        for i in range(nr):
            value = state[f * nr + i] - old[f * nr + i]
            fix[f] = value if i == 0 else jnp.where(r == i, value, fix[f])
    natural = exact_dot(jnp.concatenate([state[n] + change[n] for n in range(2 * nr)], axis=0), order[...])
    for f in range(2):
        for i in range(nr):
            n = f * nr + i
            nxt_ref[f, pl.ds(i, SUB, stride=nr), :] = lines_to_lanes(natural[n * SUB:(n + 1) * SUB])

    for row in range(FINE - LATE, LATE):
        write_row(row, [ub[FINE % 2, SUB + row, f] for f in range(2)])
    for d in range(LATE + 1, FINE + 1):
        ends = complete(d)
        if d < FINE:
            prepare(d + 1)
        write_pair(d, ends)

    for side in range(2):
        @pl.when(sends[side])
        def _():
            pltpu.make_async_remote_copy(
                own, ub.at[0, pl.ds(0, SUB)], vsend.at[side], vrecv.at[side, 0],
                device_id=(t, r + 1 if side == 0 else r - 1), device_id_type=MESH).wait_send()


def deliver(ends, following, ends_out, following_out, sem):
    fields, rows = ends.shape[:2]
    copies = [pltpu.make_async_copy(ends.at[f, row], ends_out.at[f, :, row, :], sem.at[f * rows + row])
              for row in range(rows) for f in range(fields)]
    copies.append(pltpu.make_async_copy(following, following_out, sem.at[fields * rows]))
    for copy in copies:
        copy.start()
    for copy in copies:
        copy.wait()


def body(nt, nr, starts, conductivity):
    rows, columns = conductivity.shape
    assert rows == SUB == COARSEN == FINE
    assert columns == COARSEN * SUB * LANES
    blocks = columns // LANES
    group = math.gcd(SHARE, nt)
    slab = starts[0].reshape(2, rows, blocks, LANES).transpose(0, 2, 1, 3).reshape(2, blocks * rows, LANES)
    kappa = conductivity.reshape(rows, blocks, LANES).transpose(1, 0, 2).reshape(blocks * rows, LANES)
    slab = pltpu.with_memory_space_constraint(slab, pltpu.HBM)
    kappa = pltpu.with_memory_space_constraint(kappa, pltpu.HBM)
    f32 = jnp.float32
    dma = pltpu.SemaphoreType.DMA
    cell = (SUB, LANES)
    line = (COARSEN,) + cell
    ends, following = pl.pallas_call(
        functools.partial(kernel, nt, nr, group),
        out_shape=(
            jax.ShapeDtypeStruct((2, rows, blocks, LANES), f32),
            jax.ShapeDtypeStruct((2, SUB * nr, LANES), f32),
        ),
        in_specs=[pl.BlockSpec(memory_space=pltpu.HBM)] * 2,
        out_specs=[pl.BlockSpec(memory_space=pltpu.VMEM)] * 2,
        scratch_shapes=[
            pltpu.VMEM((2, blocks * rows, LANES), f32),
            pltpu.VMEM((blocks * rows, LANES), f32),
            dma((2,)),
            pltpu.VMEM((2, 3 * SUB, 2) + line, f32),
            pltpu.VMEM((2, 3 * SUB, 2) + line, f32),
            pltpu.VMEM((SUB, 2) + line, f32),
            pltpu.VMEM((SUB,) + line, f32),
            pltpu.VMEM((2, FINE) + line, f32),
            pltpu.VMEM((3 * SUB,) + line, f32),
            pltpu.VMEM((3 * SUB,) + cell, f32),
            pltpu.VMEM((3 * SUB,) + line, f32),
            pltpu.VMEM((3 * SUB,) + line, f32),
            pltpu.VMEM((3 * SUB,) + line, f32),
            pltpu.VMEM((3 * SUB,) + line, f32),
            pltpu.VMEM((FINE, 2, 2) + line, f32),
            pltpu.VMEM((LANES, LANES), jnp.bfloat16),
            pltpu.VMEM((3,) + cell, f32),
            pltpu.VMEM((nr, 3) + cell, f32),
            pltpu.VMEM((3, 2) + cell, f32),
            pltpu.VMEM((nr, 3, 2) + cell, f32),
            pltpu.VMEM((nt, nr, 2) + cell, f32),
            dma((2,)), dma((2, FINE)),
            dma((2,)), dma((2, FINE)), dma((2,)),
            dma, dma((nr,)),
            dma, dma((nr,)),
            dma((nt,)), dma((nt,)),
            pltpu.SemaphoreType.REGULAR, pltpu.SemaphoreType.REGULAR, pltpu.SemaphoreType.REGULAR,
        ],
        compiler_params=pltpu.CompilerParams(
            collective_id=0, has_side_effects=True, vmem_limit_bytes=48 * 1024 * 1024),
        name="parareal",
    )(slab, kappa)
    ends, following = pl.pallas_call(
        deliver,
        out_shape=(
            jax.ShapeDtypeStruct((2, blocks, rows, LANES), f32),
            jax.ShapeDtypeStruct(following.shape, f32),
        ),
        in_specs=[pl.BlockSpec(memory_space=pltpu.VMEM)] * 2,
        out_specs=[pl.BlockSpec(memory_space=pltpu.HBM)] * 2,
        scratch_shapes=[dma((2 * rows + 1,))],
        compiler_params=pltpu.CompilerParams(vmem_limit_bytes=1024 * 1024),
        name="deliver",
    )(ends, following)
    new_ends = ends.transpose(0, 2, 1, 3).reshape(2, rows, columns)
    coarse_next = following.reshape(2, SUB, nr, LANES).transpose(0, 2, 1, 3).reshape(2, nr, SUB * LANES)
    return new_ends[None], coarse_next[None]


def solution(mesh):
    nt, nr = mesh.shape["tm"], mesh.shape["rows"]
    in_specs = (P("tm", None, "rows", None), P("rows", None))
    out_specs = (P("tm", None, "rows", None), P("tm", None, None, None))
    return jax.shard_map(functools.partial(body, nt, nr), mesh=mesh, in_specs=in_specs, out_specs=out_specs, check_vma=False)
```

```python
import functools
import math

import jax
import jax.numpy as jnp
from jax import lax
from jax.experimental import pallas as pl
from jax.experimental.pallas import tpu as pltpu
from jax.sharding import PartitionSpec as P

FINE = 8
COARSE = 2
COARSEN = 8
EXCHANGE = 0.05
TRACER_DIFF = 0.5

SUB = 8
LANES = 128
MESH = pl.DeviceIdType.MESH
SHARE = 2
SLOTS = 3
LATE = 6
STARTS = (1, 3, 5)
AREA = 1.0 / (COARSEN * COARSEN)


def cell_index(axis):
    return lax.broadcasted_iota(jnp.int32, (SUB, LANES), axis)


def following(v):
    lane = cell_index(1)
    near = pltpu.roll(v, LANES - SUB, 1)
    far = jnp.where(lane < LANES - 1, pltpu.roll(v, LANES - SUB - 1, 1), pltpu.roll(v, LANES - 1, 1))
    edge = pltpu.roll(jnp.where(cell_index(0) == 0, far, near), SUB - 1, 0)
    return jnp.where(lane < LANES - SUB, near, edge)


def preceding(v):
    lane = cell_index(1)
    near = pltpu.roll(v, SUB, 1)
    far = jnp.where(lane >= 1, pltpu.roll(v, SUB + 1, 1), pltpu.roll(v, 1, 1))
    edge = pltpu.roll(jnp.where(cell_index(0) == SUB - 1, far, near), 1, 0)
    return jnp.where(lane >= SUB, near, edge)


def lines_to_lanes(v):
    lane, line = cell_index(1), cell_index(0)
    for step in (1, 2, 4):
        high_lane, high_line = (lane & (step * 16)) != 0, (line & step) != 0
        up = pltpu.roll(pltpu.roll(v, SUB - step, 0), step * 16, 1)
        down = pltpu.roll(pltpu.roll(v, step, 0), LANES - step * 16, 1)
        v = jnp.where(high_lane, jnp.where(high_line, v, up), jnp.where(high_line, down, v))
    return v


def to_right(v):
    return jnp.concatenate([v[1:], following(v[0])[None]], axis=0)


def to_left(v):
    return jnp.concatenate([preceding(v[COARSEN - 1])[None], v[:COARSEN - 1]], axis=0)


def exchange_lanes(rows):
    lane = cell_index(1)
    rows = list(rows)
    for step in (1, 2, 4):
        high = (lane & step) != 0
        for i in range(SUB):
            if not i & step:
                a, b = rows[i], rows[i | step]
                rows[i] = jnp.where(high, pltpu.roll(b, step, 1), a)
                rows[i | step] = jnp.where(high, b, pltpu.roll(a, LANES - step, 1))
    return rows


def exact_dot(x, w):
    rows = x.shape[0]
    hi = x.astype(jnp.bfloat16)
    rest = x - hi.astype(jnp.float32)
    mid = rest.astype(jnp.bfloat16)
    low = (rest - mid.astype(jnp.float32)).astype(jnp.bfloat16)
    y = jnp.dot(jnp.concatenate([hi.astype(jnp.float32), mid.astype(jnp.float32), low.astype(jnp.float32)], axis=0).astype(jnp.bfloat16), w,
                preferred_element_type=jnp.float32)
    return y[:rows] + y[rows:2 * rows] + y[2 * rows:]


def kernel(nt, nr, group, s_hbm, k_hbm, out_ref, nxt_ref,
           s_ref, k_ref, in_sem, wb, ub, own, kown, kh, kr, kl, kd, ku, ch, ct, part, order, ers, erg, cts, ctg, jall,
           vsend, vrecv, ksend, krecv, kfwd, ersend, errecv, ctsend, ctrecv, jsend, jrecv, tok_down, tok_up, tok_tm):
    t = lax.axis_index("tm")
    r = lax.axis_index("rows")
    member = lax.rem(t, group)
    base = t - member
    has_up = r > 0
    has_down = r < nr - 1
    sends = (has_down, has_up)
    gets = (has_up, has_down)
    f32 = jnp.float32

    outer_first = [row for d in range(SUB // 2) for row in (SUB - 1 - d, d)]

    k_in = pltpu.make_async_copy(k_hbm, k_ref, in_sem.at[0])
    s_in = pltpu.make_async_copy(s_hbm, s_ref, in_sem.at[1])
    k_in.start()
    s_in.start()

    barrier = pltpu.get_barrier_semaphore()

    def greet(tm, row):
        pl.semaphore_signal(barrier, inc=1, device_id=(tm, row), device_id_type=MESH)

    pl.when(has_up)(lambda: greet(t, r - 1))
    pl.when(has_down)(lambda: greet(t, r + 1))
    for o in range(1, nt):
        pl.when(t + o < nt)(lambda: greet(t + o, r))
    for o in range(1, group):
        pl.when(member >= o)(lambda: greet(t - o, r))

    source = lax.broadcasted_iota(jnp.int32, order.shape, 0)
    target = lax.broadcasted_iota(jnp.int32, order.shape, 1)
    goes = (source & (SUB - 1)) * (LANES // SUB) + (source >> 3)
    order[...] = jnp.where(goes == target, 1.0, 0.0).astype(jnp.bfloat16)
    for d in range(1, FINE):
        zero = jnp.zeros(wb.shape[2:], f32)
        wb[(d - 1) % 2, SUB - d] = zero
        wb[(d - 1) % 2, 2 * SUB - 1 + d] = zero

    @pl.when(jnp.logical_not(has_up))
    def _():
        ub[0, 0:SUB] = jnp.zeros((SUB,) + ub.shape[2:], f32)
        kh[0] = jnp.zeros(kh.shape[1:], f32)

    @pl.when(jnp.logical_not(has_down))
    def _():
        ub[0, 2 * SUB:] = jnp.zeros((SUB,) + ub.shape[2:], f32)
        kh[1] = jnp.zeros(kh.shape[1:], f32)

    def read_row(ref, row):
        return jnp.stack(exchange_lanes(
            [ref[pl.ds(m * SUB * SUB + row, SUB, stride=SUB), :] for m in range(SUB)]), axis=0)

    def tell(tok, row):
        pl.semaphore_signal(tok, inc=1, device_id=(t, row), device_id_type=MESH)

    def relay(slot):
        @pl.when(has_up & (jnp.minimum(r - 1, SLOTS - 1) == slot))
        def _():
            pl.semaphore_wait(tok_down, 1)
            pl.when(has_down)(lambda: tell(tok_down, r + 1))

        @pl.when(has_down & (jnp.minimum(nr - 2 - r, SLOTS - 1) == slot))
        def _():
            pl.semaphore_wait(tok_up, 1)
            pl.when(has_up)(lambda: tell(tok_up, r - 1))

    def v_copy(side, d):
        if side == 0:
            return pltpu.make_async_remote_copy(
                own.at[SUB - d], ub.at[0, SUB - d], vsend.at[side], vrecv.at[d - 1],
                device_id=(t, r + 1), device_id_type=MESH)
        return pltpu.make_async_remote_copy(
            own.at[d - 1], ub.at[0, 2 * SUB - 1 + d], vsend.at[side], vrecv.at[d - 1],
            device_id=(t, r - 1), device_id_type=MESH)

    def k_copy(side, d):
        return pltpu.make_async_remote_copy(
            kown.at[SUB - d if side == 0 else d - 1], kh.at[side, d - 1], ksend.at[side], krecv.at[d - 1],
            device_id=(t, r + 1 if side == 0 else r - 1), device_id_type=MESH)

    def k_forward(side, d, o):
        return pltpu.make_async_remote_copy(
            kh.at[side, d - 1], kh.at[side, d - 1], kfwd.at[side], krecv.at[d - 1],
            device_id=(base + lax.rem(member + o, group), r), device_id_type=MESH)

    def both_sides(array, sem):
        for count, cond in ((2, has_up & has_down), (1, jnp.logical_xor(has_up, has_down))):
            @pl.when(cond)
            def _():
                rows = array.at[pl.ds(0, count)]
                pltpu.make_async_remote_copy(
                    rows, rows, ksend.at[0], sem, device_id=(t, jnp.where(has_up, r - 1, r + 1)), device_id_type=MESH).wait_recv()

    def mine(d):
        return member == (d - 1) % group

    def er_copy(o):
        return pltpu.make_async_remote_copy(
            ers, erg.at[r], ersend, errecv,
            device_id=(t, lax.rem(r + o, nr)), device_id_type=MESH)

    at_edge = jnp.logical_not(has_up & has_down)
    skipped = jnp.where(has_up, 0, 1)

    def ct_rows(count, o):
        first = skipped if count == 2 else 0
        return pltpu.make_async_remote_copy(
            cts.at[pl.ds(first, count)], ctg.at[pl.ds(3 * r + first, count)], ctsend, ctrecv,
            device_id=(t, lax.rem(r + o, nr)), device_id_type=MESH)

    def ct_total(count):
        rows = ctg.at[pl.ds(0, count)]
        return pltpu.make_async_remote_copy(
            rows, rows, ctsend, ctrecv, device_id=(t, lax.rem(r + 1, nr)), device_id_type=MESH)

    def j_copy(o):
        return pltpu.make_async_remote_copy(
            jall.at[t], jall.at[t], jsend.at[o], jrecv.at[t],
            device_id=(t + o, r), device_id_type=MESH)

    def send_conductivity(d):
        for side in range(2):
            pl.when(sends[side] & mine(d))(lambda: k_copy(side, d).start())

    k_in.wait()
    total = None
    for d in range(1, SUB // 2 + 1):
        for row in (SUB - d, d - 1):
            x = read_row(k_ref, row)
            kown[row] = x
            total = x if total is None else total + x
        if d == 1:
            pl.semaphore_wait(barrier, t + (group - 1 - member) + has_up.astype(jnp.int32) + has_down.astype(jnp.int32))

            pl.when(jnp.logical_not(has_up) & has_down)(lambda: tell(tok_down, r + 1))
            pl.when(jnp.logical_not(has_down) & has_up)(lambda: tell(tok_up, r - 1))

            for o in range(1, nt):
                @pl.when(t >= o)
                def _():
                    pl.semaphore_signal(tok_tm, inc=1, device_id=(t - o, r), device_id_type=MESH)
        send_conductivity(d)
    for d in range(SUB // 2 + 1, FINE + 1):
        send_conductivity(d)
    ers[0] = jnp.sum(total, axis=0) * AREA

    s_in.wait()
    sums = [None, None]
    for row in outer_first:
        for f in range(2):
            x = read_row(s_ref.at[f], row)
            own[row, f] = x
            wb[0, SUB + row, f] = x
            ub[0, SUB + row, f] = x
            sums[f] = x if sums[f] is None else sums[f] + x
    for f in range(2):
        ers[1 + f] = jnp.sum(sums[f], axis=0) * AREA
    erg[r] = ers[...]

    def send_row(d):
        for side in range(2):
            pl.when(sends[side])(lambda: v_copy(side, d).start())

    def columns_of(i, k):
        right = 0.5 * (k + to_right(k))
        kr[i] = right
        kl[i] = preceding(right[COARSEN - 1])

    def left_of(i):
        return jnp.concatenate([kl[i][None], kr[i, 0:COARSEN - 1]], axis=0)

    def centre_of(i):
        total = (kr[i] + left_of(i)) + (ku[i] + kd[i])
        ch[i] = (1.0 - EXCHANGE) - total
        ct[i] = (1.0 - EXCHANGE) - TRACER_DIFF * total

    for row in range(SUB):
        k = kown[row]
        columns_of(SUB + row, k)
        if row < SUB - 1:
            face = 0.5 * (k + kown[row + 1])
            kd[SUB + row] = face
            ku[SUB + row + 1] = face
        if 0 < row < SUB - 1:
            centre_of(SUB + row)

    def advance(buf, p, i, above=True, below=True):
        heat, tracer = buf[p, i, 0], buf[p, i, 1]
        right, left = kr[i], left_of(i)
        terms = [right * to_right(heat) + left * to_left(heat), right * to_right(tracer) + left * to_left(tracer)]
        if below:
            face = kd[i]
            terms = [terms[f] + face * buf[p, i + 1, f] for f in range(2)]
        if above:
            face = ku[i]
            terms = [terms[f] + face * buf[p, i - 1, f] for f in range(2)]
        return ((ch[i] * heat + EXCHANGE * tracer) + terms[0],
                (ct[i] * tracer + EXCHANGE * heat) + TRACER_DIFF * terms[1])

    relay(0)
    for level in range(1, SUB // 2):
        p = (level - 1) % 2
        for row in range(level, SUB - level):
            heat, tracer = advance(wb, p, SUB + row)
            for f, x in enumerate((heat, tracer)):
                wb[1 - p, SUB + row, f] = x
                ub[1 - p, SUB + row, f] = x

    def pass_on(d):
        @pl.when(mine(d))
        def _():
            both_sides(kown, krecv.at[d - 1])
        for side in range(2):
            @pl.when(gets[side] & mine(d))
            def _():
                for o in range(1, group):
                    k_forward(side, d, o).start()

    outside = (jnp.where(has_up, 1.0, 0.0), jnp.where(has_down, 1.0, 0.0))

    def faces_at(d):
        @pl.when(jnp.logical_not(mine(d)))
        def _():
            both_sides(kown, krecv.at[d - 1])
        for side in range(2):
            k = kh[side, d - 1]
            inner = kh[side, d - 2] if d > 1 else kown[0 if side == 0 else SUB - 1]
            face = 0.5 * (k + inner)
            edge = face * outside[side] if d == 1 else face
            i = SUB - d if side == 0 else 2 * SUB - 1 + d
            columns_of(i, k)
            if side == 0:
                ku[i + 1] = face
                kd[i] = edge
                centre_of(i + 1)
            else:
                kd[i - 1] = face
                ku[i] = edge
                centre_of(i - 1)

    send_row(1)
    for d in range(1, 5):
        pass_on(d)
    relay(1)
    for level in range(1, FINE):
        for d in range(2 * level + 3, min(2 * level + 4, FINE) + 1):
            pass_on(d)
        faces_at(level)
        if level in STARTS:
            send_row(STARTS.index(level) + 2)
        if level == 4:
            relay(2)
            for o in range(1, nr):
                er_copy(o).start()
        p = (level - 1) % 2
        first, last = SUB + 1 - level, 2 * SUB - 2 + level
        for i in range(first, last + 1):
            if SUB + level <= i < 2 * SUB - level:
                continue
            heat, tracer = advance(wb, p, i)
            wb[1 - p, i, 0] = heat
            wb[1 - p, i, 1] = tracer
        for i, inner, face in ((first - 1, first, kd), (last + 1, last, ku)):
            for f in range(2):
                wb[1 - p, i, f] = (1.0, TRACER_DIFF)[f] * face[i] * wb[p, inner, f]

    p = (FINE - 1) % 2
    fluxes = [[jnp.sum(ku[SUB] * (wb[p, SUB - 1, f] - wb[p, SUB, f]), axis=0) for f in range(2)],
              [jnp.sum(kd[2 * SUB - 1] * (wb[p, 2 * SUB, f] - wb[p, 2 * SUB - 1, f]), axis=0) for f in range(2)]]
    for b in range(3):
        whole, gain = [], []
        for f in range(2):
            total, side_flux = None, None
            for i in range(max(1, SUB * b), min(3 * SUB - 1, SUB * (b + 1))):
                x = wb[p, i, f]
                flux = kr[i, COARSEN - 1] * (following(x[0]) - x[COARSEN - 1])
                total = x if total is None else total + x
                side_flux = flux if side_flux is None else side_flux + flux
            change = side_flux - preceding(side_flux)
            if b == 0:
                change = change - fluxes[0][f]
            elif b == 1:
                change = change + (fluxes[0][f] + fluxes[1][f])
            else:
                change = change - fluxes[1][f]
            whole.append(jnp.sum(total, axis=0))
            gain.append((1.0, TRACER_DIFF)[f] * change)
        moved = EXCHANGE * (whole[1] - whole[0])
        cts[b, 0] = AREA * ((whole[0] + moved) + gain[0])
        cts[b, 1] = AREA * ((whole[1] - moved) + gain[1])
    for o in range(1, nr):
        pl.when(at_edge)(lambda: ct_rows(2, o).start())
        pl.when(jnp.logical_not(at_edge))(lambda: ct_rows(3, o).start())
    ctg[pl.ds(3 * r, 3)] = cts[...]
    faces_at(FINE)

    def row_pair(level, diagonal):
        p = lax.rem(level + 1, 2)
        new = [(i,) + advance(ub, p, i) for i in (SUB + level - diagonal, 2 * SUB - 1 - level + diagonal)]
        for i, heat, tracer in new:
            ub[1 - p, i, 0] = heat
            ub[1 - p, i, 1] = tracer

    def run_diagonal(diagonal):
        both_sides(own, vrecv.at[diagonal - 1])
        def step(level, carry):
            row_pair(level, diagonal)
            return carry
        lax.fori_loop(1, min(FINE, SUB // 2 - 1 + diagonal) + 1, step, 0)

    ratio = (FINE / COARSE) / float(COARSEN * COARSEN)
    rate = EXCHANGE * (FINE / COARSE)

    run_diagonal(1)

    def er_total():
        rows = erg.at[pl.ds(0, nr - 1)]
        return pltpu.make_async_remote_copy(
            rows, rows, ersend, errecv, device_id=(t, lax.rem(r + 1, nr)), device_id_type=MESH)

    er_total().wait_recv()
    kcv = [erg[i, 0] for i in range(nr)]
    c_right = [ratio * 0.5 * (k + following(k)) for k in kcv]
    c_left = [ratio * 0.5 * (k + preceding(k)) for k in kcv]
    c_face = [ratio * 0.5 * kcv[0]]
    c_face += [ratio * 0.5 * (kcv[i] + kcv[i + 1]) for i in range(nr - 1)]
    c_face += [ratio * 0.5 * kcv[nr - 1]]
    totals = [(c_right[i] + c_left[i]) + (c_face[i] + c_face[i + 1]) for i in range(nr)]
    c_centre = [[(1.0 - rate) - x for x in totals], [(1.0 - rate) - TRACER_DIFF * x for x in totals]]

    def coarse_prop(state):
        for substep in range(COARSE):
            new = []
            for f in range(2):
                rows = state[f * nr:(f + 1) * nr]
                other = state[(1 - f) * nr:(2 - f) * nr]
                for i in range(nr):
                    v = rows[i]
                    around = c_right[i] * following(v) + c_left[i] * preceding(v)
                    if i > 0:
                        around = around + c_face[i] * rows[i - 1]
                    if i < nr - 1:
                        around = around + c_face[i + 1] * rows[i + 1]
                    if f == 1:
                        around = TRACER_DIFF * around
                    new.append((c_centre[f][i] * v + rate * other[i]) + around)
            state = tuple(new)
        return state

    later = jnp.where(t > 0, 1.0, 0.0)
    old = coarse_prop(tuple(later * erg[i, 1 + f] for f in range(2) for i in range(nr)))

    send_row(5)
    run_diagonal(2)
    send_row(6)
    pl.when(at_edge)(lambda: ct_total(3 * nr - 4).wait_recv())
    pl.when(jnp.logical_not(at_edge))(lambda: ct_total(3 * nr - 5).wait_recv())
    change = []
    for f in range(2):
        for i in range(nr):
            x = ctg[3 * i + 1, f]
            if i > 0:
                x = x + ctg[3 * i - 1, f]
            if i < nr - 1:
                x = x + ctg[3 * i + 3, f]
            x = x - old[f * nr + i]
            jall[t, i, f] = x
            change.append(x)
    pl.when(t < nt - 1)(lambda: pl.semaphore_wait(tok_tm, nt - 1 - t))
    for o in range(1, nt):
        pl.when(t + o < nt)(lambda: j_copy(o).start())

    send_row(7)
    for d in range(3, LATE):
        run_diagonal(d)
        if d == 3:
            send_row(8)

    def place(level, side, d):
        return SUB + level - d if side == 0 else 2 * SUB - 1 - level + d

    def prepare(d):
        for level in range(1, FINE + 1):
            for side in range(2):
                i = place(level, side, d)
                for f, x in enumerate(advance(ub, (level - 1) % 2, i, above=side == 1, below=side == 0)):
                    part[level - 1, side, f] = x

    def complete(d):
        both_sides(own, vrecv.at[d - 1])
        ends = [[ub[0, place(0, side, d), f] for f in range(2)] for side in range(2)]
        for level in range(1, FINE + 1):
            for side in range(2):
                i = place(level, side, d)
                face = (ku, kd)[side][i]
                heat, tracer = ends[side]
                ends[side] = [part[level - 1, side, 0] + face * heat,
                              part[level - 1, side, 1] + (TRACER_DIFF * face) * tracer]
                if d < FINE and level < FINE:
                    for f in range(2):
                        ub[level % 2, i, f] = ends[side][f]
        return ends

    share = FINE // group
    for side in range(2):
        @pl.when(sends[side])
        def _():
            pltpu.make_async_remote_copy(
                kown.at[pl.ds(0, share)], kh.at[side, pl.ds(0, share)], ksend.at[side], krecv.at[0],
                device_id=(t, r + 1 if side == 0 else r - 1), device_id_type=MESH).wait_send()

        if group > 1:
            @pl.when(gets[side])
            def _():
                passed = kh.at[side, pl.ds(0, share * (group - 1))]
                pltpu.make_async_remote_copy(
                    passed, passed, kfwd.at[side], krecv.at[0],
                    device_id=(base + lax.rem(member + 1, group), r), device_id_type=MESH).wait_send()
    er_total().wait_send()
    pl.when(at_edge)(lambda: ct_total(2 * nr - 2).wait_send())
    pl.when(jnp.logical_not(at_edge))(lambda: ct_total(3 * nr - 3).wait_send())
    for o in range(1, nt):
        pl.when(t + o < nt)(lambda: j_copy(o).wait_send())

    def link(n, state):
        pltpu.make_async_remote_copy(
            jall.at[n], jall.at[n], jsend.at[0], jrecv.at[n],
            device_id=(n, r), device_id_type=MESH).wait_recv()
        return coarse_prop(tuple(state[f * nr + i] + jall[n, i, f] for f in range(2) for i in range(nr)))

    def write_row(row, ends):
        for f in range(2):
            end = exchange_lanes([ends[f][m] + fix[f] for m in range(COARSEN)])
            for m in range(SUB):
                out_ref[f, row, m * SUB:(m + 1) * SUB, :] = end[m]

    def write_pair(d, ends):
        write_row(FINE - d, ends[0])
        write_row(d - 1, ends[1])

    prepare(LATE)
    early = complete(LATE)
    for side, row in enumerate((FINE - LATE, LATE - 1)):
        for f in range(2):
            ub[FINE % 2, SUB + row, f] = early[side][f]
    prepare(LATE + 1)

    state = tuple(jnp.zeros((SUB, LANES), f32) for _ in range(2 * nr))
    state = lax.fori_loop(0, t, link, state)
    fix = [None, None]
    for f in range(2):
        for i in range(nr):
            value = state[f * nr + i] - old[f * nr + i]
            fix[f] = value if i == 0 else jnp.where(r == i, value, fix[f])
    natural = exact_dot(jnp.concatenate([state[n] + change[n] for n in range(2 * nr)], axis=0), order[...])
    for f in range(2):
        for i in range(nr):
            n = f * nr + i
            nxt_ref[f, pl.ds(i, SUB, stride=nr), :] = lines_to_lanes(natural[n * SUB:(n + 1) * SUB])

    for row in range(FINE - LATE, LATE):
        write_row(row, [ub[FINE % 2, SUB + row, f] for f in range(2)])
    for d in range(LATE + 1, FINE + 1):
        ends = complete(d)
        if d < FINE:
            prepare(d + 1)
        write_pair(d, ends)

    for side in range(2):
        @pl.when(sends[side])
        def _():
            pltpu.make_async_remote_copy(
                own, ub.at[0, pl.ds(0, SUB)], vsend.at[side], vrecv.at[0],
                device_id=(t, r + 1 if side == 0 else r - 1), device_id_type=MESH).wait_send()


def deliver(ends, following, ends_out, following_out, sem):
    fields, rows = ends.shape[:2]
    copies = [pltpu.make_async_copy(ends.at[f, row], ends_out.at[f, :, row, :], sem.at[f * rows + row])
              for row in range(rows) for f in range(fields)]
    copies.append(pltpu.make_async_copy(following, following_out, sem.at[fields * rows]))
    for copy in copies:
        copy.start()
    for copy in copies:
        copy.wait()


def body(nt, nr, starts, conductivity):
    rows, columns = conductivity.shape
    assert rows == SUB == COARSEN == FINE
    assert nr > 1
    assert columns == COARSEN * SUB * LANES
    blocks = columns // LANES
    group = math.gcd(SHARE, nt)
    slab = starts[0].reshape(2, rows, blocks, LANES).transpose(0, 2, 1, 3).reshape(2, blocks * rows, LANES)
    kappa = conductivity.reshape(rows, blocks, LANES).transpose(1, 0, 2).reshape(blocks * rows, LANES)
    slab = pltpu.with_memory_space_constraint(slab, pltpu.HBM)
    kappa = pltpu.with_memory_space_constraint(kappa, pltpu.HBM)
    f32 = jnp.float32
    dma = pltpu.SemaphoreType.DMA
    cell = (SUB, LANES)
    line = (COARSEN,) + cell
    ends, following = pl.pallas_call(
        functools.partial(kernel, nt, nr, group),
        out_shape=(
            jax.ShapeDtypeStruct((2, rows, blocks, LANES), f32),
            jax.ShapeDtypeStruct((2, SUB * nr, LANES), f32),
        ),
        in_specs=[pl.BlockSpec(memory_space=pltpu.HBM)] * 2,
        out_specs=[pl.BlockSpec(memory_space=pltpu.VMEM)] * 2,
        scratch_shapes=[
            pltpu.VMEM((2, blocks * rows, LANES), f32),
            pltpu.VMEM((blocks * rows, LANES), f32),
            dma((2,)),
            pltpu.VMEM((2, 3 * SUB, 2) + line, f32),
            pltpu.VMEM((2, 3 * SUB, 2) + line, f32),
            pltpu.VMEM((SUB, 2) + line, f32),
            pltpu.VMEM((SUB,) + line, f32),
            pltpu.VMEM((2, FINE) + line, f32),
            pltpu.VMEM((3 * SUB,) + line, f32),
            pltpu.VMEM((3 * SUB,) + cell, f32),
            pltpu.VMEM((3 * SUB,) + line, f32),
            pltpu.VMEM((3 * SUB,) + line, f32),
            pltpu.VMEM((3 * SUB,) + line, f32),
            pltpu.VMEM((3 * SUB,) + line, f32),
            pltpu.VMEM((FINE, 2, 2) + line, f32),
            pltpu.VMEM((LANES, LANES), jnp.bfloat16),
            pltpu.VMEM((3,) + cell, f32),
            pltpu.VMEM((nr, 3) + cell, f32),
            pltpu.VMEM((3, 2) + cell, f32),
            pltpu.VMEM((3 * nr, 2) + cell, f32),
            pltpu.VMEM((nt, nr, 2) + cell, f32),
            dma((2,)), dma((FINE,)),
            dma((2,)), dma((FINE,)), dma((2,)),
            dma, dma, dma, dma,
            dma((nt,)), dma((nt,)),
            pltpu.SemaphoreType.REGULAR, pltpu.SemaphoreType.REGULAR, pltpu.SemaphoreType.REGULAR,
        ],
        compiler_params=pltpu.CompilerParams(
            collective_id=0, has_side_effects=True, vmem_limit_bytes=48 * 1024 * 1024),
        name="parareal",
    )(slab, kappa)
    ends, following = pl.pallas_call(
        deliver,
        out_shape=(
            jax.ShapeDtypeStruct((2, blocks, rows, LANES), f32),
            jax.ShapeDtypeStruct(following.shape, f32),
        ),
        in_specs=[pl.BlockSpec(memory_space=pltpu.VMEM)] * 2,
        out_specs=[pl.BlockSpec(memory_space=pltpu.HBM)] * 2,
        scratch_shapes=[dma((2 * rows + 1,))],
        compiler_params=pltpu.CompilerParams(vmem_limit_bytes=1024 * 1024),
        name="deliver",
    )(ends, following)
    new_ends = ends.transpose(0, 2, 1, 3).reshape(2, rows, columns)
    coarse_next = following.reshape(2, SUB, nr, LANES).transpose(0, 2, 1, 3).reshape(2, nr, SUB * LANES)
    return new_ends[None], coarse_next[None]


def solution(mesh):
    nt, nr = mesh.shape["tm"], mesh.shape["rows"]
    in_specs = (P("tm", None, "rows", None), P("rows", None))
    out_specs = (P("tm", None, "rows", None), P("tm", None, None, None))
    return jax.shard_map(functools.partial(body, nt, nr), mesh=mesh, in_specs=in_specs, out_specs=out_specs, check_vma=False)
```

```python
import functools
import math

import jax
import jax.numpy as jnp
from jax import lax
from jax.experimental import pallas as pl
from jax.experimental.pallas import tpu as pltpu
from jax.sharding import PartitionSpec as P

FINE = 8
COARSE = 2
COARSEN = 8
EXCHANGE = 0.05
TRACER_DIFF = 0.5

SUB = 8
LANES = 128
MESH = pl.DeviceIdType.MESH
SHARE = 2
SLOTS = 3
LATE = 6
STARTS = (1, 4)
AREA = 1.0 / (COARSEN * COARSEN)


def cell_index(axis):
    return lax.broadcasted_iota(jnp.int32, (SUB, LANES), axis)


def following(v):
    lane = cell_index(1)
    near = pltpu.roll(v, LANES - SUB, 1)
    far = jnp.where(lane < LANES - 1, pltpu.roll(v, LANES - SUB - 1, 1), pltpu.roll(v, LANES - 1, 1))
    edge = pltpu.roll(jnp.where(cell_index(0) == 0, far, near), SUB - 1, 0)
    return jnp.where(lane < LANES - SUB, near, edge)


def preceding(v):
    lane = cell_index(1)
    near = pltpu.roll(v, SUB, 1)
    far = jnp.where(lane >= 1, pltpu.roll(v, SUB + 1, 1), pltpu.roll(v, 1, 1))
    edge = pltpu.roll(jnp.where(cell_index(0) == SUB - 1, far, near), 1, 0)
    return jnp.where(lane >= SUB, near, edge)


def lines_to_lanes(v):
    lane, line = cell_index(1), cell_index(0)
    for step in (1, 2, 4):
        high_lane, high_line = (lane & (step * 16)) != 0, (line & step) != 0
        up = pltpu.roll(pltpu.roll(v, SUB - step, 0), step * 16, 1)
        down = pltpu.roll(pltpu.roll(v, step, 0), LANES - step * 16, 1)
        v = jnp.where(high_lane, jnp.where(high_line, v, up), jnp.where(high_line, down, v))
    return v


def to_right(v):
    return jnp.concatenate([v[1:], following(v[0])[None]], axis=0)


def to_left(v):
    return jnp.concatenate([preceding(v[COARSEN - 1])[None], v[:COARSEN - 1]], axis=0)


def exchange_lanes(rows):
    lane = cell_index(1)
    rows = list(rows)
    for step in (1, 2, 4):
        high = (lane & step) != 0
        for i in range(SUB):
            if not i & step:
                a, b = rows[i], rows[i | step]
                rows[i] = jnp.where(high, pltpu.roll(b, step, 1), a)
                rows[i | step] = jnp.where(high, b, pltpu.roll(a, LANES - step, 1))
    return rows


def exact_dot(x, w):
    rows = x.shape[0]
    hi = x.astype(jnp.bfloat16)
    rest = x - hi.astype(jnp.float32)
    mid = rest.astype(jnp.bfloat16)
    low = (rest - mid.astype(jnp.float32)).astype(jnp.bfloat16)
    y = jnp.dot(jnp.concatenate([hi.astype(jnp.float32), mid.astype(jnp.float32), low.astype(jnp.float32)], axis=0).astype(jnp.bfloat16), w,
                preferred_element_type=jnp.float32)
    return y[:rows] + y[rows:2 * rows] + y[2 * rows:]


def kernel(nt, nr, group, s_hbm, k_hbm, out_ref, nxt_ref,
           s_ref, k_ref, in_sem, wb, ub, own, kown, kh, kr, kl, kd, ku, ch, ct, part, order, ers, erg, cts, ctg, jall,
           vsend, vrecv, ksend, krecv, kfwd, ersend, errecv, ctsend, ctrecv, jsend, jrecv, tok_down, tok_up, tok_tm):
    t = lax.axis_index("tm")
    r = lax.axis_index("rows")
    member = lax.rem(t, group)
    base = t - member
    has_up = r > 0
    has_down = r < nr - 1
    sends = (has_down, has_up)
    gets = (has_up, has_down)
    f32 = jnp.float32

    outer_first = [row for d in range(SUB // 2) for row in (SUB - 1 - d, d)]

    k_in = pltpu.make_async_copy(k_hbm, k_ref, in_sem.at[0])
    s_in = pltpu.make_async_copy(s_hbm, s_ref, in_sem.at[1])
    k_in.start()
    s_in.start()

    barrier = pltpu.get_barrier_semaphore()

    def greet(tm, row):
        pl.semaphore_signal(barrier, inc=1, device_id=(tm, row), device_id_type=MESH)

    pl.when(has_up)(lambda: greet(t, r - 1))
    pl.when(has_down)(lambda: greet(t, r + 1))
    for o in range(1, nt):
        pl.when(t + o < nt)(lambda: greet(t + o, r))
    for o in range(1, group):
        pl.when(member >= o)(lambda: greet(t - o, r))

    source = lax.broadcasted_iota(jnp.int32, order.shape, 0)
    target = lax.broadcasted_iota(jnp.int32, order.shape, 1)
    goes = (source & (SUB - 1)) * (LANES // SUB) + (source >> 3)
    order[...] = jnp.where(goes == target, 1.0, 0.0).astype(jnp.bfloat16)
    for d in range(1, FINE):
        zero = jnp.zeros(wb.shape[2:], f32)
        wb[(d - 1) % 2, SUB - d] = zero
        wb[(d - 1) % 2, 2 * SUB - 1 + d] = zero

    @pl.when(jnp.logical_not(has_up))
    def _():
        ub[0, 0:SUB] = jnp.zeros((SUB,) + ub.shape[2:], f32)
        kh[0] = jnp.zeros(kh.shape[1:], f32)

    @pl.when(jnp.logical_not(has_down))
    def _():
        ub[0, 2 * SUB:] = jnp.zeros((SUB,) + ub.shape[2:], f32)
        kh[1] = jnp.zeros(kh.shape[1:], f32)

    def read_row(ref, row):
        return jnp.stack(exchange_lanes(
            [ref[pl.ds(m * SUB * SUB + row, SUB, stride=SUB), :] for m in range(SUB)]), axis=0)

    def tell(tok, row):
        pl.semaphore_signal(tok, inc=1, device_id=(t, row), device_id_type=MESH)

    def relay(slot):
        @pl.when(has_up & (jnp.minimum(r - 1, SLOTS - 1) == slot))
        def _():
            pl.semaphore_wait(tok_down, 1)
            pl.when(has_down)(lambda: tell(tok_down, r + 1))

        @pl.when(has_down & (jnp.minimum(nr - 2 - r, SLOTS - 1) == slot))
        def _():
            pl.semaphore_wait(tok_up, 1)
            pl.when(has_up)(lambda: tell(tok_up, r - 1))

    def v_copy(side, d):
        if side == 0:
            return pltpu.make_async_remote_copy(
                own.at[SUB - d], ub.at[0, SUB - d], vsend.at[side], vrecv.at[d - 1],
                device_id=(t, r + 1), device_id_type=MESH)
        return pltpu.make_async_remote_copy(
            own.at[d - 1], ub.at[0, 2 * SUB - 1 + d], vsend.at[side], vrecv.at[d - 1],
            device_id=(t, r - 1), device_id_type=MESH)

    def k_copy(side, d):
        return pltpu.make_async_remote_copy(
            kown.at[SUB - d if side == 0 else d - 1], kh.at[side, d - 1], ksend.at[side], krecv.at[d - 1],
            device_id=(t, r + 1 if side == 0 else r - 1), device_id_type=MESH)

    def k_forward(side, d, o):
        return pltpu.make_async_remote_copy(
            kh.at[side, d - 1], kh.at[side, d - 1], kfwd.at[side], krecv.at[d - 1],
            device_id=(base + lax.rem(member + o, group), r), device_id_type=MESH)

    def both_sides(array, sem):
        for count, cond in ((2, has_up & has_down), (1, jnp.logical_xor(has_up, has_down))):
            @pl.when(cond)
            def _():
                rows = array.at[pl.ds(0, count)]
                pltpu.make_async_remote_copy(
                    rows, rows, ksend.at[0], sem, device_id=(t, jnp.where(has_up, r - 1, r + 1)), device_id_type=MESH).wait_recv()

    def mine(d):
        return member == (d - 1) % group

    def er_copy(o):
        return pltpu.make_async_remote_copy(
            ers, erg.at[r], ersend, errecv,
            device_id=(t, lax.rem(r + o, nr)), device_id_type=MESH)

    at_edge = jnp.logical_not(has_up & has_down)
    skipped = jnp.where(has_up, 0, 1)

    def ct_rows(count, o):
        first = skipped if count == 2 else 0
        return pltpu.make_async_remote_copy(
            cts.at[pl.ds(first, count)], ctg.at[pl.ds(3 * r + first, count)], ctsend, ctrecv,
            device_id=(t, lax.rem(r + o, nr)), device_id_type=MESH)

    def ct_total(count):
        rows = ctg.at[pl.ds(0, count)]
        return pltpu.make_async_remote_copy(
            rows, rows, ctsend, ctrecv, device_id=(t, lax.rem(r + 1, nr)), device_id_type=MESH)

    def j_copy(o):
        return pltpu.make_async_remote_copy(
            jall.at[t], jall.at[t], jsend.at[o], jrecv.at[t],
            device_id=(t + o, r), device_id_type=MESH)

    def send_conductivity(d):
        for side in range(2):
            pl.when(sends[side] & mine(d))(lambda: k_copy(side, d).start())

    k_in.wait()
    total = None
    for d in range(1, SUB // 2 + 1):
        for row in (SUB - d, d - 1):
            x = read_row(k_ref, row)
            kown[row] = x
            total = x if total is None else total + x
        if d == 1:
            pl.semaphore_wait(barrier, t + (group - 1 - member) + has_up.astype(jnp.int32) + has_down.astype(jnp.int32))

            pl.when(jnp.logical_not(has_up) & has_down)(lambda: tell(tok_down, r + 1))
            pl.when(jnp.logical_not(has_down) & has_up)(lambda: tell(tok_up, r - 1))

            for o in range(1, nt):
                @pl.when(t >= o)
                def _():
                    pl.semaphore_signal(tok_tm, inc=1, device_id=(t - o, r), device_id_type=MESH)
        send_conductivity(d)
    for d in range(SUB // 2 + 1, FINE + 1):
        send_conductivity(d)
    ers[0] = jnp.sum(total, axis=0) * AREA

    s_in.wait()
    sums = [None, None]
    for row in outer_first:
        for f in range(2):
            x = read_row(s_ref.at[f], row)
            own[row, f] = x
            wb[0, SUB + row, f] = x
            ub[0, SUB + row, f] = x
            sums[f] = x if sums[f] is None else sums[f] + x
    for f in range(2):
        ers[1 + f] = jnp.sum(sums[f], axis=0) * AREA
    erg[r] = ers[...]

    def send_row(d):
        for side in range(2):
            pl.when(sends[side])(lambda: v_copy(side, d).start())

    def columns_of(i, k):
        right = 0.5 * (k + to_right(k))
        kr[i] = right
        kl[i] = preceding(right[COARSEN - 1])

    def left_of(i):
        return jnp.concatenate([kl[i][None], kr[i, 0:COARSEN - 1]], axis=0)

    def centre_of(i):
        total = (kr[i] + left_of(i)) + (ku[i] + kd[i])
        ch[i] = (1.0 - EXCHANGE) - total
        ct[i] = (1.0 - EXCHANGE) - TRACER_DIFF * total

    for row in range(SUB):
        k = kown[row]
        columns_of(SUB + row, k)
        if row < SUB - 1:
            face = 0.5 * (k + kown[row + 1])
            kd[SUB + row] = face
            ku[SUB + row + 1] = face
        if 0 < row < SUB - 1:
            centre_of(SUB + row)

    def advance(buf, p, i, above=True, below=True):
        heat, tracer = buf[p, i, 0], buf[p, i, 1]
        right, left = kr[i], left_of(i)
        terms = [right * to_right(heat) + left * to_left(heat), right * to_right(tracer) + left * to_left(tracer)]
        if below:
            face = kd[i]
            terms = [terms[f] + face * buf[p, i + 1, f] for f in range(2)]
        if above:
            face = ku[i]
            terms = [terms[f] + face * buf[p, i - 1, f] for f in range(2)]
        return ((ch[i] * heat + EXCHANGE * tracer) + terms[0],
                (ct[i] * tracer + EXCHANGE * heat) + TRACER_DIFF * terms[1])

    relay(0)
    for level in range(1, SUB // 2):
        p = (level - 1) % 2
        for row in range(level, SUB - level):
            heat, tracer = advance(wb, p, SUB + row)
            for f, x in enumerate((heat, tracer)):
                wb[1 - p, SUB + row, f] = x
                ub[1 - p, SUB + row, f] = x

    def pass_on(d):
        @pl.when(mine(d))
        def _():
            both_sides(kown, krecv.at[d - 1])
        for side in range(2):
            @pl.when(gets[side] & mine(d))
            def _():
                for o in range(1, group):
                    k_forward(side, d, o).start()

    outside = (jnp.where(has_up, 1.0, 0.0), jnp.where(has_down, 1.0, 0.0))

    def faces_at(d):
        @pl.when(jnp.logical_not(mine(d)))
        def _():
            both_sides(kown, krecv.at[d - 1])
        for side in range(2):
            k = kh[side, d - 1]
            inner = kh[side, d - 2] if d > 1 else kown[0 if side == 0 else SUB - 1]
            face = 0.5 * (k + inner)
            edge = face * outside[side] if d == 1 else face
            i = SUB - d if side == 0 else 2 * SUB - 1 + d
            columns_of(i, k)
            if side == 0:
                ku[i + 1] = face
                kd[i] = edge
                centre_of(i + 1)
            else:
                kd[i - 1] = face
                ku[i] = edge
                centre_of(i - 1)

    send_row(1)
    for d in range(1, 5):
        pass_on(d)
    relay(1)
    for level in range(1, FINE):
        for d in range(2 * level + 3, min(2 * level + 4, FINE) + 1):
            pass_on(d)
        faces_at(level)
        if level in STARTS:
            send_row(STARTS.index(level) + 2)
        if level == 3:
            relay(2)
            for o in range(1, nr):
                er_copy(o).start()
        p = (level - 1) % 2
        first, last = SUB + 1 - level, 2 * SUB - 2 + level
        for i in range(first, last + 1):
            if SUB + level <= i < 2 * SUB - level:
                continue
            heat, tracer = advance(wb, p, i)
            wb[1 - p, i, 0] = heat
            wb[1 - p, i, 1] = tracer
        for i, inner, face in ((first - 1, first, kd), (last + 1, last, ku)):
            for f in range(2):
                wb[1 - p, i, f] = (1.0, TRACER_DIFF)[f] * face[i] * wb[p, inner, f]

    p = (FINE - 1) % 2
    fluxes = [[jnp.sum(ku[SUB] * (wb[p, SUB - 1, f] - wb[p, SUB, f]), axis=0) for f in range(2)],
              [jnp.sum(kd[2 * SUB - 1] * (wb[p, 2 * SUB, f] - wb[p, 2 * SUB - 1, f]), axis=0) for f in range(2)]]
    for b in range(3):
        whole, gain = [], []
        for f in range(2):
            total, side_flux = None, None
            for i in range(max(1, SUB * b), min(3 * SUB - 1, SUB * (b + 1))):
                x = wb[p, i, f]
                flux = kr[i, COARSEN - 1] * (following(x[0]) - x[COARSEN - 1])
                total = x if total is None else total + x
                side_flux = flux if side_flux is None else side_flux + flux
            change = side_flux - preceding(side_flux)
            if b == 0:
                change = change - fluxes[0][f]
            elif b == 1:
                change = change + (fluxes[0][f] + fluxes[1][f])
            else:
                change = change - fluxes[1][f]
            whole.append(jnp.sum(total, axis=0))
            gain.append((1.0, TRACER_DIFF)[f] * change)
        moved = EXCHANGE * (whole[1] - whole[0])
        cts[b, 0] = AREA * ((whole[0] + moved) + gain[0])
        cts[b, 1] = AREA * ((whole[1] - moved) + gain[1])
    for o in range(1, nr):
        pl.when(at_edge)(lambda: ct_rows(2, o).start())
        pl.when(jnp.logical_not(at_edge))(lambda: ct_rows(3, o).start())
    ctg[pl.ds(3 * r, 3)] = cts[...]
    faces_at(FINE)

    def row_pair(level, diagonal):
        p = lax.rem(level + 1, 2)
        new = [(i,) + advance(ub, p, i) for i in (SUB + level - diagonal, 2 * SUB - 1 - level + diagonal)]
        for i, heat, tracer in new:
            ub[1 - p, i, 0] = heat
            ub[1 - p, i, 1] = tracer

    def run_diagonal(diagonal):
        both_sides(own, vrecv.at[diagonal - 1])
        def step(level, carry):
            row_pair(level, diagonal)
            return carry
        lax.fori_loop(1, min(FINE, SUB // 2 - 1 + diagonal) + 1, step, 0)

    ratio = (FINE / COARSE) / float(COARSEN * COARSEN)
    rate = EXCHANGE * (FINE / COARSE)

    run_diagonal(1)
    send_row(4)
    run_diagonal(2)
    send_row(5)

    def er_total():
        rows = erg.at[pl.ds(0, nr - 1)]
        return pltpu.make_async_remote_copy(
            rows, rows, ersend, errecv, device_id=(t, lax.rem(r + 1, nr)), device_id_type=MESH)

    er_total().wait_recv()
    kcv = [erg[i, 0] for i in range(nr)]
    c_right = [ratio * 0.5 * (k + following(k)) for k in kcv]
    c_left = [ratio * 0.5 * (k + preceding(k)) for k in kcv]
    c_face = [ratio * 0.5 * kcv[0]]
    c_face += [ratio * 0.5 * (kcv[i] + kcv[i + 1]) for i in range(nr - 1)]
    c_face += [ratio * 0.5 * kcv[nr - 1]]
    totals = [(c_right[i] + c_left[i]) + (c_face[i] + c_face[i + 1]) for i in range(nr)]
    c_centre = [[(1.0 - rate) - x for x in totals], [(1.0 - rate) - TRACER_DIFF * x for x in totals]]

    def coarse_prop(state):
        for substep in range(COARSE):
            new = []
            for f in range(2):
                rows = state[f * nr:(f + 1) * nr]
                other = state[(1 - f) * nr:(2 - f) * nr]
                for i in range(nr):
                    v = rows[i]
                    around = c_right[i] * following(v) + c_left[i] * preceding(v)
                    if i > 0:
                        around = around + c_face[i] * rows[i - 1]
                    if i < nr - 1:
                        around = around + c_face[i + 1] * rows[i + 1]
                    if f == 1:
                        around = TRACER_DIFF * around
                    new.append((c_centre[f][i] * v + rate * other[i]) + around)
            state = tuple(new)
        return state

    later = jnp.where(t > 0, 1.0, 0.0)
    old = coarse_prop(tuple(later * erg[i, 1 + f] for f in range(2) for i in range(nr)))

    run_diagonal(3)
    send_row(6)
    pl.when(at_edge)(lambda: ct_total(3 * nr - 4).wait_recv())
    pl.when(jnp.logical_not(at_edge))(lambda: ct_total(3 * nr - 5).wait_recv())
    change = []
    for f in range(2):
        for i in range(nr):
            x = ctg[3 * i + 1, f]
            if i > 0:
                x = x + ctg[3 * i - 1, f]
            if i < nr - 1:
                x = x + ctg[3 * i + 3, f]
            x = x - old[f * nr + i]
            jall[t, i, f] = x
            change.append(x)
    pl.when(t < nt - 1)(lambda: pl.semaphore_wait(tok_tm, nt - 1 - t))
    for o in range(1, nt):
        pl.when(t + o < nt)(lambda: j_copy(o).start())

    send_row(7)
    for d in range(4, LATE):
        run_diagonal(d)
        if d == 4:
            send_row(8)

    def place(level, side, d):
        return SUB + level - d if side == 0 else 2 * SUB - 1 - level + d

    def prepare(d):
        for level in range(1, FINE + 1):
            for side in range(2):
                i = place(level, side, d)
                for f, x in enumerate(advance(ub, (level - 1) % 2, i, above=side == 1, below=side == 0)):
                    part[level - 1, side, f] = x

    def complete(d):
        both_sides(own, vrecv.at[d - 1])
        ends = [[ub[0, place(0, side, d), f] for f in range(2)] for side in range(2)]
        for level in range(1, FINE + 1):
            for side in range(2):
                i = place(level, side, d)
                face = (ku, kd)[side][i]
                heat, tracer = ends[side]
                ends[side] = [part[level - 1, side, 0] + face * heat,
                              part[level - 1, side, 1] + (TRACER_DIFF * face) * tracer]
                if d < FINE and level < FINE:
                    for f in range(2):
                        ub[level % 2, i, f] = ends[side][f]
        return ends

    share = FINE // group
    for side in range(2):
        @pl.when(sends[side])
        def _():
            pltpu.make_async_remote_copy(
                kown.at[pl.ds(0, share)], kh.at[side, pl.ds(0, share)], ksend.at[side], krecv.at[0],
                device_id=(t, r + 1 if side == 0 else r - 1), device_id_type=MESH).wait_send()

        if group > 1:
            @pl.when(gets[side])
            def _():
                passed = kh.at[side, pl.ds(0, share * (group - 1))]
                pltpu.make_async_remote_copy(
                    passed, passed, kfwd.at[side], krecv.at[0],
                    device_id=(base + lax.rem(member + 1, group), r), device_id_type=MESH).wait_send()
    er_total().wait_send()
    pl.when(at_edge)(lambda: ct_total(2 * nr - 2).wait_send())
    pl.when(jnp.logical_not(at_edge))(lambda: ct_total(3 * nr - 3).wait_send())
    for o in range(1, nt):
        pl.when(t + o < nt)(lambda: j_copy(o).wait_send())

    def link(n, state):
        pltpu.make_async_remote_copy(
            jall.at[n], jall.at[n], jsend.at[0], jrecv.at[n],
            device_id=(n, r), device_id_type=MESH).wait_recv()
        return coarse_prop(tuple(state[f * nr + i] + jall[n, i, f] for f in range(2) for i in range(nr)))

    def write_row(row, ends):
        for f in range(2):
            end = exchange_lanes([ends[f][m] + fix[f] for m in range(COARSEN)])
            for m in range(SUB):
                out_ref[f, row, m * SUB:(m + 1) * SUB, :] = end[m]

    def write_pair(d, ends):
        write_row(FINE - d, ends[0])
        write_row(d - 1, ends[1])

    prepare(LATE)
    early = complete(LATE)
    for side, row in enumerate((FINE - LATE, LATE - 1)):
        for f in range(2):
            ub[FINE % 2, SUB + row, f] = early[side][f]
    prepare(LATE + 1)

    state = tuple(jnp.zeros((SUB, LANES), f32) for _ in range(2 * nr))
    state = lax.fori_loop(0, t, link, state)
    fix = [None, None]
    for f in range(2):
        for i in range(nr):
            value = state[f * nr + i] - old[f * nr + i]
            fix[f] = value if i == 0 else jnp.where(r == i, value, fix[f])
    natural = exact_dot(jnp.concatenate([state[n] + change[n] for n in range(2 * nr)], axis=0), order[...])
    for f in range(2):
        for i in range(nr):
            n = f * nr + i
            nxt_ref[f, pl.ds(i, SUB, stride=nr), :] = lines_to_lanes(natural[n * SUB:(n + 1) * SUB])

    for row in range(FINE - LATE, LATE):
        write_row(row, [ub[FINE % 2, SUB + row, f] for f in range(2)])
    for d in range(LATE + 1, FINE + 1):
        ends = complete(d)
        if d < FINE:
            prepare(d + 1)
        write_pair(d, ends)

    for side in range(2):
        @pl.when(sends[side])
        def _():
            pltpu.make_async_remote_copy(
                own, ub.at[0, pl.ds(0, SUB)], vsend.at[side], vrecv.at[0],
                device_id=(t, r + 1 if side == 0 else r - 1), device_id_type=MESH).wait_send()


def deliver(ends, following, ends_out, following_out, sem):
    fields, rows = ends.shape[:2]
    copies = [pltpu.make_async_copy(ends.at[f, row], ends_out.at[f, :, row, :], sem.at[f * rows + row])
              for row in range(rows) for f in range(fields)]
    copies.append(pltpu.make_async_copy(following, following_out, sem.at[fields * rows]))
    for copy in copies:
        copy.start()
    for copy in copies:
        copy.wait()


def body(nt, nr, starts, conductivity):
    rows, columns = conductivity.shape
    assert rows == SUB == COARSEN == FINE
    assert nr > 1
    assert columns == COARSEN * SUB * LANES
    blocks = columns // LANES
    group = math.gcd(SHARE, nt)
    slab = starts[0].reshape(2, rows, blocks, LANES).transpose(0, 2, 1, 3).reshape(2, blocks * rows, LANES)
    kappa = conductivity.reshape(rows, blocks, LANES).transpose(1, 0, 2).reshape(blocks * rows, LANES)
    slab = pltpu.with_memory_space_constraint(slab, pltpu.HBM)
    kappa = pltpu.with_memory_space_constraint(kappa, pltpu.HBM)
    f32 = jnp.float32
    dma = pltpu.SemaphoreType.DMA
    cell = (SUB, LANES)
    line = (COARSEN,) + cell
    ends, following = pl.pallas_call(
        functools.partial(kernel, nt, nr, group),
        out_shape=(
            jax.ShapeDtypeStruct((2, rows, blocks, LANES), f32),
            jax.ShapeDtypeStruct((2, SUB * nr, LANES), f32),
        ),
        in_specs=[pl.BlockSpec(memory_space=pltpu.HBM)] * 2,
        out_specs=[pl.BlockSpec(memory_space=pltpu.VMEM)] * 2,
        scratch_shapes=[
            pltpu.VMEM((2, blocks * rows, LANES), f32),
            pltpu.VMEM((blocks * rows, LANES), f32),
            dma((2,)),
            pltpu.VMEM((2, 3 * SUB, 2) + line, f32),
            pltpu.VMEM((2, 3 * SUB, 2) + line, f32),
            pltpu.VMEM((SUB, 2) + line, f32),
            pltpu.VMEM((SUB,) + line, f32),
            pltpu.VMEM((2, FINE) + line, f32),
            pltpu.VMEM((3 * SUB,) + line, f32),
            pltpu.VMEM((3 * SUB,) + cell, f32),
            pltpu.VMEM((3 * SUB,) + line, f32),
            pltpu.VMEM((3 * SUB,) + line, f32),
            pltpu.VMEM((3 * SUB,) + line, f32),
            pltpu.VMEM((3 * SUB,) + line, f32),
            pltpu.VMEM((FINE, 2, 2) + line, f32),
            pltpu.VMEM((LANES, LANES), jnp.bfloat16),
            pltpu.VMEM((3,) + cell, f32),
            pltpu.VMEM((nr, 3) + cell, f32),
            pltpu.VMEM((3, 2) + cell, f32),
            pltpu.VMEM((3 * nr, 2) + cell, f32),
            pltpu.VMEM((nt, nr, 2) + cell, f32),
            dma((2,)), dma((FINE,)),
            dma((2,)), dma((FINE,)), dma((2,)),
            dma, dma, dma, dma,
            dma((nt,)), dma((nt,)),
            pltpu.SemaphoreType.REGULAR, pltpu.SemaphoreType.REGULAR, pltpu.SemaphoreType.REGULAR,
        ],
        compiler_params=pltpu.CompilerParams(
            collective_id=0, has_side_effects=True, vmem_limit_bytes=48 * 1024 * 1024),
        name="parareal",
    )(slab, kappa)
    ends, following = pl.pallas_call(
        deliver,
        out_shape=(
            jax.ShapeDtypeStruct((2, blocks, rows, LANES), f32),
            jax.ShapeDtypeStruct(following.shape, f32),
        ),
        in_specs=[pl.BlockSpec(memory_space=pltpu.VMEM)] * 2,
        out_specs=[pl.BlockSpec(memory_space=pltpu.HBM)] * 2,
        scratch_shapes=[dma((2 * rows + 1,))],
        compiler_params=pltpu.CompilerParams(vmem_limit_bytes=1024 * 1024),
        name="deliver",
    )(ends, following)
    new_ends = ends.transpose(0, 2, 1, 3).reshape(2, rows, columns)
    coarse_next = following.reshape(2, SUB, nr, LANES).transpose(0, 2, 1, 3).reshape(2, nr, SUB * LANES)
    return new_ends[None], coarse_next[None]


def solution(mesh):
    nt, nr = mesh.shape["tm"], mesh.shape["rows"]
    in_specs = (P("tm", None, "rows", None), P("rows", None))
    out_specs = (P("tm", None, "rows", None), P("tm", None, None, None))
    return jax.shard_map(functools.partial(body, nt, nr), mesh=mesh, in_specs=in_specs, out_specs=out_specs, check_vma=False)
```
